128 devices in a mesh: row: 4 (over x), col: 32 (over z, y, core).
Axes of the slice: x: 4, y: 4, z: 4, core: 2. Of those that a mesh axis runs over, the one named last changes fastest.
Arguments:
- flexibility: float32 [4, 32, 5, 1024, 1024], P('row', 'col'), as said below
- coupling: float32 [4, 32, 5, 24, 1024], P('row', 'col'), may hold values from -0.75 to 0.75
- coarse_inverse: float32 [6144, 6144], P(('row', 'col')), as said below
- precon_weight: float32 [4, 32, 5, 4, 128], P('row', 'col'), may hold values from 0.25 to 2
- right_side: float32 [4, 32, 5, 16, 4, 128], P('row', 'col'), may hold values from -6 to 6
- counts: int32 [4, 32], P('row', 'col'), may hold values from 2 to 5, as said below
- partner: int32 [4, 32, 4, 5], P('row', 'col'), may hold values from 0 to 4, each once within a row
- dof_index: int32 [4, 32, 5, 4, 128], P('row', 'col'), may hold values from 0 to 127, each once within a row
- corner_map: int32 [4, 32, 5, 24], P('row', 'col'), may hold values from 0 to 6143
Outputs:
- solution: float32 [4, 32, 5, 16, 4, 128], P('row', 'col')
- residual: float32 [4, 32, 5, 16, 4, 128], P('row', 'col')
The draws below stay inside these ranges and needn't reach their ends.
Inputs may be any that keep to these rules, and one draw needn't show every extreme that they name: A device's live subdomains are its first counts slots; some device has 5 and some device has 2 in every draw. `partner`: for each device and each link block separately, the 5 entries are a permutation of the slots; the same values recur on other devices, link blocks and device rows. `dof_index`: for each device, slot and link block separately, the 128 entries are a permutation of the block's unknowns; the same values recur on other slots, link blocks, devices and device rows. `flexibility`: symmetric positive definite. `coarse_inverse`: symmetric positive definite.
All inputs are finite; a program needn't handle non-finite values.
Results may differ from the reference program's by a relative error of at most 0.00029.
Values sent between devices are 32-bit elements; how exact they have to be, the bound alone decides.
A program may use at most 128 MiB of HBM per device.

```python
import math
import jax
import jax.numpy as jnp
from jax import lax

IFACE = 1024
LINKS = 4
PAIR = 128
NCOR = 24
SLOTS = 5
NC = 6144
LOADS = 16
ITERS = 3
N_ROW = 4
N_COL = 32


def dominant_matrix(key, shape, order, low, high, spread):
    key_off, key_diag = jax.random.split(key, 2)
    offdiag = jax.random.uniform(key_off, shape, jnp.float32, -1.0, 1.0) * (spread * order ** (-0.5))
    offdiag = (offdiag + jnp.swapaxes(offdiag, -1, -2)) * 0.5
    diag_vals = jax.random.uniform(key_diag, shape[:-1], jnp.float32, low, high)
    ident = (jnp.arange(order)[:, None] == jnp.arange(order)[None, :]).astype(jnp.float32)
    matrix = offdiag * (1.0 - ident) + ident * diag_vals[..., None, :]
    return matrix


def draw_flexibility(key, part):
    return dominant_matrix(jax.random.fold_in(key, 11), (N_ROW, N_COL, SLOTS, IFACE, IFACE), IFACE, 1.5, 3.0, 1.2)


def draw_coarse_inverse(key, part):
    return dominant_matrix(jax.random.fold_in(key, 12), (NC, NC), NC, 1.0, 2.0, 0.9)


def draw_counts(key, part):
    key_main, key_high, key_low = jax.random.split(jax.random.fold_in(key, 13), 3)
    total = N_ROW * N_COL
    flat = jax.random.randint(key_main, (total,), 2, SLOTS + 1)
    high_at = jax.random.randint(key_high, (), 0, total)
    low_at = (high_at + 1 + jax.random.randint(key_low, (), 0, total - 1)) % total
    flat = flat.at[high_at].set(SLOTS).at[low_at].set(2)
    return flat.reshape(N_ROW, N_COL).astype(jnp.int32)


def set_ends(drawn, key, smallest, top_value):
    place = [jax.random.randint(jax.random.fold_in(key, axis), (), 0, length) for axis, length in enumerate(drawn.shape)]
    longest = drawn.shape.index(max(drawn.shape))
    next_to = place[:longest] + [(place[longest] + 1) % drawn.shape[longest]] + place[longest + 1:]
    return drawn.at[tuple(place)].set(smallest).at[tuple(next_to)].set(top_value)


def level_of(stream_key, shape, shards, smallest, largest):
    def one(position, parts):
        heights = jax.random.uniform(jax.random.fold_in(jax.random.fold_in(stream_key, 6), position), (parts,), jnp.float32, smallest / len(shards), largest / len(shards))
        return jnp.repeat(jnp.exp(heights), shape[position] // parts).reshape((-1,) + (1,) * (len(shape) - position - 1))

    loudness = one(*shards[0])
    for cut in shards[1:]:
        loudness = loudness * one(*cut)
    return loudness


def gaussian(key, dims, width, reach, pieces=(), kind=jnp.bfloat16):
    factor_of = level_of(key, dims, pieces, -0.22, 0.18) if pieces else 1.0
    values = jax.random.normal(key, dims, jnp.float32) * width * factor_of
    return jnp.minimum(jnp.maximum(values, -reach), reach).astype(kind)


def setup_inputs(seed: int = 0) -> dict:
    seeds = jax.random.split(jax.random.key(seed), 10)
    return {
        "flexibility": draw_flexibility(jax.random.fold_in(seeds[9], 71), 0),
        "coupling": gaussian(seeds[1], (N_ROW, N_COL, SLOTS, NCOR, IFACE), (IFACE // 16) ** -0.5, 0.75, ((0, 4), (1, 32)), jnp.float32),
        "coarse_inverse": draw_coarse_inverse(jax.random.fold_in(seeds[9], 71), 0),
        "precon_weight": jnp.clip(jnp.exp(math.log(2.0) - 2.0794415 * jax.random.uniform(seeds[3], (N_ROW, N_COL, SLOTS, LINKS, PAIR), jnp.float32) ** level_of(seeds[3], (N_ROW, N_COL, SLOTS, LINKS, PAIR), ((0, 4), (1, 32)), -0.2, 0.2)), 0.25, 2.0),
        "right_side": gaussian(seeds[4], (N_ROW, N_COL, SLOTS, LOADS, LINKS, PAIR), 1.0, 6.0, ((0, 4), (1, 32)), jnp.float32),
        "counts": draw_counts(jax.random.fold_in(seeds[9], 71), 0),
        "partner": jax.vmap(lambda own: jax.random.permutation(own, SLOTS))(jax.random.split(seeds[6], N_ROW * N_COL * LINKS)).reshape((N_ROW, N_COL, LINKS, SLOTS)).astype(jnp.int32),
        "dof_index": jax.vmap(lambda own: jax.random.permutation(own, PAIR))(jax.random.split(seeds[7], N_ROW * N_COL * SLOTS * LINKS)).reshape((N_ROW, N_COL, SLOTS, LINKS, PAIR)).astype(jnp.int32),
        "corner_map": set_ends(jax.random.randint(seeds[8], (N_ROW, N_COL, SLOTS, NCOR), 0, NC), jax.random.fold_in(seeds[8], 1), 0, NC - 1).astype(jnp.int32),
    }


HIGH = lax.Precision.HIGHEST


def link_mask(counts, partner):
    slot_ids = jnp.arange(SLOTS, dtype=jnp.int32)
    live = (slot_ids[None, None, :] < counts[:, :, None]).astype(jnp.float32)
    live_prev = jnp.roll(live, 1, axis=1)
    chosen = (partner[..., None] == slot_ids).astype(jnp.float32)
    link_live = jnp.einsum('rckjp,rcp->rcjk', chosen, live_prev, precision=HIGH)
    return live[..., None] * link_live


def apply_operator(values, flexibility, coupling, coarse_inverse, partner, dof_index, corner_map, mask):
    slot_ids = jnp.arange(SLOTS, dtype=jnp.int32)
    inverse_index = jnp.argsort(dof_index, axis=-1).astype(jnp.int32)
    gather_back = jnp.broadcast_to(inverse_index[:, :, :, None], values.shape)
    forces = jnp.take_along_axis(values, gather_back, axis=5)
    forces_next = jnp.roll(forces, -1, axis=1)
    partner_next = jnp.roll(partner, -1, axis=1)
    chosen_next = (partner_next[..., None] == slot_ids).astype(jnp.float32)
    facing = -jnp.einsum('rckjp,rcjqkw->rcpqkw', chosen_next, forces_next, precision=HIGH)
    shape = values.shape
    force_full = jnp.concatenate([values, facing], axis=4).reshape(shape[0], shape[1], shape[2], shape[3], IFACE)
    answer = jnp.einsum('rcsab,rcsqb->rcsqa', flexibility, force_full, precision=HIGH)
    corner_terms = jnp.einsum('rcsnb,rcsqb->qrcsn', coupling, force_full, precision=HIGH)
    flat_map = corner_map.reshape(-1)
    corner_load = jnp.zeros((LOADS, NC), jnp.float32).at[:, flat_map].add(corner_terms.reshape(LOADS, -1))
    corner_answer = jnp.dot(corner_load, coarse_inverse, precision=HIGH, preferred_element_type=jnp.float32)
    picked = corner_answer[:, flat_map].reshape(LOADS, shape[0], shape[1], shape[2], NCOR)
    answer = answer + jnp.einsum('rcsnb,qrcsn->rcsqb', coupling, picked, precision=HIGH)
    split = answer.reshape(shape[0], shape[1], shape[2], shape[3], 2 * LINKS, PAIR)
    link_part = split[:, :, :, :, :LINKS, :]
    facing_part = jnp.roll(split[:, :, :, :, LINKS:, :], 1, axis=1)
    chosen_own = (partner[..., None] == slot_ids).astype(jnp.float32)
    selected = jnp.einsum('rckjp,rcpqkw->rcjqkw', chosen_own, facing_part, precision=HIGH)
    forward = jnp.broadcast_to(dof_index[:, :, :, None], values.shape)
    selected = jnp.take_along_axis(selected, forward, axis=5)
    return (link_part - selected) * mask


def inner(first, second):
    return jnp.sum(first * second, axis=(0, 1, 2, 4, 5))


def reference(flexibility, coupling, coarse_inverse, precon_weight, right_side, counts, partner, dof_index, corner_map):
    mask = link_mask(counts, partner)[:, :, :, None, :, None]
    weight = precon_weight[:, :, :, None]
    residual = right_side * mask
    solution = jnp.zeros_like(residual)
    precond = weight * residual
    direction = precond
    norm_now = inner(residual, precond)
    for iteration in range(ITERS):
        image = apply_operator(direction, flexibility, coupling, coarse_inverse, partner, dof_index, corner_map, mask)
        alpha = (norm_now / inner(direction, image))[None, None, None, :, None, None]
        solution = solution + alpha * direction
        residual = residual - alpha * image
        precond = weight * residual
        norm_next = inner(residual, precond)
        direction = precond + (norm_next / norm_now)[None, None, None, :, None, None] * direction
        norm_now = norm_next
    return solution, residual
```

```python
import functools

import jax
import jax.numpy as jnp
from jax import lax
from jax.experimental import pallas as pl
from jax.experimental.pallas import tpu as pltpu
from jax.sharding import PartitionSpec as P

ITERS = 3
NX, NZ, NY, NK = 4, 4, 4, 2
NYZ = NZ * NY
STAGES = 3
SCAL = 120

MESH = pl.DeviceIdType.MESH
F32 = jnp.float32
BF16 = jnp.bfloat16
NT = (((1,), (1,)), ((), ()))
NN = (((1,), (0,)), ((), ()))


def split2(value):
    high = value.astype(BF16)
    low = (value - high.astype(F32)).astype(BF16)
    return high, low


def split3(value):
    high = value.astype(BF16)
    rest = value - high.astype(F32)
    middle = rest.astype(BF16)
    low = (rest - middle.astype(F32)).astype(BF16)
    return high, middle, low


def stack3(value):
    return jnp.concatenate(split3(value), axis=0)


def dot(left, right, dims):
    return lax.dot_general(left, right, dims, preferred_element_type=F32)


def sum3(value):
    rows = value.shape[0] // 3
    return value[2 * rows :] + value[rows : 2 * rows] + value[:rows]


def rcopy(src, dst, send, recv, device):
    return pltpu.make_async_remote_copy(
        src_ref=src,
        dst_ref=dst,
        send_sem=send,
        recv_sem=recv,
        device_id=device,
        device_id_type=MESH,
    )


def group_start(src, buf, mine, send, recv, peers):
    for i, (device, _) in enumerate(peers):
        rcopy(src, buf.at[mine], send.at[i], recv.at[mine], device).start()


def group_wait(src, buf, send, recv, peers):
    for i, (device, theirs) in enumerate(peers):
        rcopy(src, buf.at[theirs], send.at[i], recv.at[theirs], device).wait_recv()
    for i, (device, theirs) in enumerate(peers):
        rcopy(src, buf.at[theirs], send.at[i], recv.at[theirs], device).wait_send()


def kernel(
    flex, cinv, cpl, weight, rhs, info, partner, partner_inv, dof, dof_inv,
    x_out, r_out,
    stage, flex_hi, flex_lo, m32, m_hi, m_lo, cplp, infop, maps, w32, wo_hi, wo_lo, wp_hi, wp_lo,
    scatter, pick, t8, ybuf, zbuf, cbuf, xbuf, abuf, gsend, frecv, usend, urecv,
    vblk, vsp, gsp, fsp, yv, tv, dv, sv, zv, rv, mask, ulink, clink, cface, sc, ans3,
    pxbuf, pcbuf, pybuf,
    flex_sem, mloc_sem, info_s, info_r, cpl_s, cpl_r, map_s, map_r, m_s, m_r,
    tx_s, tx_r, tc_s, tc_r, y_s, y_r, z_s, z_r, c_s, c_r, x_s, x_r, a_s, a_r,
    f_s, f_r, u_s, u_r, px_s, px_r, pc_s, pc_r, py_s, py_r,
):
    slots, iface = flex.shape[:2]
    half = iface // 2
    links, width = partner.shape[0], dof.shape[-1]
    loads = rhs.shape[1]
    corners = cpl.shape[1]
    own_rows, coarse = cinv.shape
    crange = coarse // NYZ
    cset = own_rows * NYZ
    blocks = slots * links
    tiles = 2 * width

    row, col = lax.axis_index("row"), lax.axis_index("col")
    cz = lax.div(col, NY * NK)
    cy = lax.rem(lax.div(col, NK), NY)
    ck = lax.rem(col, NK)
    cols = NZ * NY * NK
    me_yz = cz * NY + cy
    prev = (row, lax.rem(col + cols - 1, cols))
    nxt = (row, lax.rem(col + 1, cols))

    def device(x, z, y, k):
        return (x, (z * NY + y) * NK + k)

    def turn(value, by, size):
        return lax.rem(value + by, size)

    xs = [(turn(row, i, NX),) * 2 for i in (2, 1, 3)]
    xs = [(device(p, cz, cy, ck), p) for p, _ in xs]
    ys = [(device(row, cz, turn(cy, i, NY), ck), turn(cy, i, NY)) for i in (2, 1, 3)]
    zs = [(device(row, turn(cz, i, NZ), cy, ck), turn(cz, i, NZ)) for i in (2, 1, 3)]
    cs = [(device(row, cz, cy, 1 - ck), 1 - ck)]
    order = sorted(
        [(i, j) for i in range(NZ) for j in range(NY) if (i, j) != (0, 0)],
        key=lambda ij: -(min(ij[0], NZ - ij[0]) + min(ij[1], NY - ij[1])),
    )
    yzs = [
        (device(row, turn(cz, i, NZ), turn(cy, j, NY), ck), turn(cz, i, NZ) * NY + turn(cy, j, NY))
        for i, j in order
    ]
    xcs = [
        (device(turn(row, i, NX), cz, cy, turn(ck, j, NK)), turn(ck, j, NK) * NX + turn(row, i, NX))
        for i in range(NX)
        for j in range(NK)
        if (i, j) != (0, 0)
    ]
    me_xc = ck * NX + row

    def flex_copy(s):
        return pltpu.make_async_copy(flex.at[s], stage.at[s % STAGES], flex_sem.at[s])

    for s in range(STAGES):
        flex_copy(s).start()

    def m_part(other):
        return cinv.at[:, pl.ds(pl.multiple_of(other * crange, 128), crange)]

    m_local = pltpu.make_async_copy(m_part(me_yz), m32.at[me_yz], mloc_sem)
    m_local.start()

    barrier = pltpu.get_barrier_semaphore()
    everyone = [d for d, _ in yzs] + [d for d, _ in xcs] + [prev, nxt]
    for d in everyone:
        pl.semaphore_signal(barrier, inc=1, device_id=d, device_id_type=MESH)
    pl.semaphore_wait(barrier, len(everyone))

    info_copy = rcopy(info, infop, info_s, info_r, nxt)
    info_copy.start()
    for i, (d, _) in enumerate(xcs):
        rcopy(info.at[slots], maps.at[me_xc, 0], map_s.at[0, i], map_r.at[0, me_xc], d).start()
    cpl_copy = rcopy(cpl.at[:, :, half:], cplp, cpl_s, cpl_r, nxt)
    cpl_copy.start()
    for i, (d, other) in enumerate(yzs):
        rcopy(m_part(other), m32.at[me_yz], m_s.at[i], m_r.at[me_yz], d).start()

    def build_coupling(source, offset, out_hi, out_lo):
        w32[...] = jnp.zeros_like(w32)
        for s in range(slots):
            w32[s, s * corners : (s + 1) * corners, :] = source[s, :, offset : offset + half]
        for s in range(slots):
            high, low = split2(w32[s])
            out_hi[s] = high
            out_lo[s] = low

    build_coupling(cpl, 0, wo_hi, wo_lo)
    tv[...] = jnp.zeros_like(tv)
    dv[...] = jnp.zeros_like(dv)
    sv[...] = jnp.zeros_like(sv)
    x_out[...] = jnp.zeros_like(x_out)
    sc[0] = jnp.ones_like(sc[0])
    sc[1] = jnp.zeros_like(sc[1])
    sc[2] = jnp.zeros_like(sc[2])
    sc[3] = jnp.zeros_like(sc[3])

    info_copy.wait_recv()
    for i, (d, _) in enumerate(xcs):
        rcopy(infop.at[slots], maps.at[me_xc, 1], map_s.at[1, i], map_r.at[1, me_xc], d).start()
    maps[me_xc, 0] = info[slots]
    maps[me_xc, 1] = infop[slots]

    for b in range(blocks):
        s, k = b // links, b % links
        live = info[s] * infop[partner[k, s]]
        live = jnp.concatenate([live] * (loads // 8), axis=0)
        mask[b] = live
        resid = live * rhs[b]
        rv[b] = resid
        yv[b] = resid
        zv[b] = weight[b] * resid

    cpl_copy.wait_recv()
    build_coupling(cplp, 0, wp_hi, wp_lo)

    lane = lax.broadcasted_iota(jnp.int32, (loads, width), 1)

    def total(first, second):
        return jnp.sum(jnp.sum(first * second, axis=0), axis=1, keepdims=True)

    def scalar_terms():
        z, y = zv[...], yv[...]
        found = [total(rv[...], z), total(z, y), total(z, sv[...]), total(dv[...], y)]
        tile = jnp.zeros((loads, width), F32)
        for i, value in enumerate(found):
            tile = jnp.where(lane == SCAL + i, value, tile)
        return tile

    def update(tile, first):
        rz, zy, zs_, dy = [
            jnp.broadcast_to(
                jnp.sum(jnp.where(lane == SCAL + i, tile, 0.0), axis=1, keepdims=True), tile.shape
            )
            for i in range(4)
        ]
        beta = rz / sc[0]
        if first is not None:
            beta = jnp.where(first, 0.0, beta)
        curv = zy + beta * (zs_ + dy) + beta * beta * sc[1]
        alpha = rz / curv
        sc[0], sc[1], sc[2], sc[3] = rz, curv, alpha, beta
        direction = zv[...] + beta[None] * dv[...]
        image = yv[...] + beta[None] * sv[...]
        dv[...] = direction
        sv[...] = image
        x_out[...] = x_out[...] + alpha[None] * direction
        resid = rv[...] - alpha[None] * image
        rv[...] = resid
        return resid

    def put3(ref, s, k, value):
        for i, part in enumerate(split3(value)):
            ref[s, i * loads : (i + 1) * loads, k * width : (k + 1) * width] = part

    def take(value, index):
        index = jnp.broadcast_to(index, value.shape)
        return jnp.take_along_axis(value, index, axis=1, mode="promise_in_bounds")

    def convert(s):
        flex_copy(s).wait()
        here = s % STAGES

        def chunk(i, _):
            at = pl.ds(pl.multiple_of(i * 64, 64), 64)
            high, low = split2(stage[here, at, :])
            flex_hi[s, at, :] = high
            flex_lo[s, at, :] = low
            return 0

        lax.fori_loop(0, iface // 64, chunk, 0)
        if s + STAGES < slots:
            flex_copy(s + STAGES).start()

    def local_answers(it, first, last):
        @pl.when(it == 0)
        def _():
            for s in range(first, last):
                convert(s)

        def one(s, _):
            left = jnp.concatenate([vsp[s], fsp[s]], axis=1)
            for n in range(iface // 256):
                at = slice(n * 256, (n + 1) * 256)
                out = dot(left, flex_hi[s, :, at], NN) + dot(left, flex_lo[s, :, at], NN)
                out = sum3(out)
                for h in range(2):
                    piece = out[:, h * width : (h + 1) * width]
                    k = 2 * n + h
                    if k < links:
                        ulink[s * links + k] = piece
                    else:
                        usend[it, s * links + k - links] = piece
            return 0

        lax.fori_loop(first, last, one, 0)

    def body(it, _):
        tile = scalar_terms()
        for b in range(blocks):
            value = weight[b] * yv[b]
            vblk[b] = value
            put3(vsp, b // links, b % links, value)
        for b in range(blocks):
            p, k = b // links, b % links
            from_block = partner_inv[k, p] * links + k
            value = -take(vblk[from_block], dof_inv[from_block])
            gsend[it, b] = value
            put3(gsp, p, k, value)
        force_copy = rcopy(gsend.at[it], frecv.at[it], f_s.at[it], f_r.at[it], prev)
        force_copy.start()

        def terms(blocks3, high, low):
            found = None
            for s in range(slots):
                left = blocks3[s]
                part = dot(left, high[s], NT) + dot(left, low[s], NT)
                found = part if found is None else found + part
            return sum3(found)

        own = jnp.where(lane < SCAL, terms(vsp, wo_hi, wo_lo), tile)
        t8[it, ck, row, :, 0:width] = own
        t8[it, ck, row, :, width:tiles] = terms(gsp, wp_hi, wp_lo)
        group_start(t8.at[it, ck, row], t8.at[it, ck], row, tx_s.at[it], tx_r.at[it], xs)

        @pl.when(it == 0)
        def _():
            for source in range(2):
                for i, (d, other) in enumerate(xcs):
                    src = (info, infop)[source].at[slots]
                    cp = rcopy(
                        src, maps.at[other, source], map_s.at[source, i], map_r.at[source, other], d
                    )
                    cp.wait_recv()
                    cp.wait_send()

            def rows(b, _):
                base = (row * cols + b * NK + ck) * own_rows
                index = lax.broadcasted_iota(jnp.int32, (own_rows, width), 0) + base
                index = index.astype(F32)
                at = pl.ds(pl.multiple_of(b * own_rows, own_rows), own_rows)
                for q in range(NX * NK):
                    for h in range(2):
                        hit = jnp.where(index == maps[q, h, 0:1, :], 1.0, 0.0)
                        lo = (2 * q + h) * width
                        scatter[at, lo : lo + width] = hit.astype(BF16)
                return 0

            lax.fori_loop(0, NYZ, rows, 0)

        group_wait(t8.at[it, ck, row], t8.at[it, ck], tx_s.at[it], tx_r.at[it], xs)
        group_start(t8.at[it, ck], t8.at[it], ck, tc_s.at[it], tc_r.at[it], cs)
        group_wait(t8.at[it, ck], t8.at[it], tc_s.at[it], tc_r.at[it], cs)

        gathered = [t8[it, q // NX, q % NX] for q in range(NX * NK)]
        carried = gathered[0][:, :width]
        for value in gathered[1:]:
            carried = carried + value[:, :width]
        dense = sum3(dot(stack3(jnp.concatenate(gathered, axis=1)), scatter[...], NT))
        ybuf[it, cy, :, 0:cset] = dense
        ybuf[it, cy, :, cset : cset + width] = carried
        group_start(ybuf.at[it, cy], ybuf.at[it], cy, y_s.at[it], y_r.at[it], ys)

        force_copy.wait_recv()
        for b in range(blocks):
            put3(fsp, b // links, b % links, frecv[it, b])
        local_answers(it, 0, 2)

        group_wait(ybuf.at[it, cy], ybuf.at[it], y_s.at[it], y_r.at[it], ys)
        zbuf[it, cz] = ybuf[it, 0] + ybuf[it, 1] + ybuf[it, 2] + ybuf[it, 3]
        group_start(zbuf.at[it, cz], zbuf.at[it], cz, z_s.at[it], z_r.at[it], zs)

        local_answers(it, 2, 4)

        @pl.when(it == 0)
        def _():
            m_local.wait()
            for i, (d, other) in enumerate(yzs):
                cp = rcopy(m_part(other), m32.at[other], m_s.at[i], m_r.at[other], d)
                cp.wait_recv()
                cp.wait_send()
            for b in range(NYZ):
                high, low = split2(m32[b])
                m_hi[b * own_rows : (b + 1) * own_rows, :] = high
                m_lo[b * own_rows : (b + 1) * own_rows, :] = low

        group_wait(zbuf.at[it, cz], zbuf.at[it], z_s.at[it], z_r.at[it], zs)
        load = zbuf[it, 0] + zbuf[it, 1] + zbuf[it, 2] + zbuf[it, 3]
        scalars = load[:, cset:]
        left = stack3(load[:, :cset])
        cbuf[it, ck] = sum3(dot(left, m_hi[...], NN) + dot(left, m_lo[...], NN))
        group_start(cbuf.at[it, ck], cbuf.at[it], ck, c_s.at[it], c_r.at[it], cs)

        local_answers(it, 4, slots)
        answer_copy = rcopy(usend.at[it], urecv.at[it], u_s.at[it], u_r.at[it], nxt)
        answer_copy.start()

        group_wait(cbuf.at[it, ck], cbuf.at[it], c_s.at[it], c_r.at[it], cs)
        xbuf[it, row] = cbuf[it, 0] + cbuf[it, 1]
        group_start(xbuf.at[it, row], xbuf.at[it], row, x_s.at[it], x_r.at[it], xs)

        @pl.when(it > 0)
        def _():
            resid = update(scalars, it == 1)
            for b in range(blocks):
                zv[b] = weight[b] * resid[b]

        @pl.when(it == 0)
        def _():
            mine = [info[slots, 0:1, :], infop[slots, 0:1, :]]

            def rows(b, _):
                index = lax.broadcasted_iota(jnp.int32, (crange // 2, width), 0)
                index = (index + b * (crange // 2)).astype(F32)
                at = pl.ds(pl.multiple_of(b * (crange // 2), crange // 2), crange // 2)
                for h in range(2):
                    hit = jnp.where(index == mine[h], 1.0, 0.0)
                    pick[at, h * width : (h + 1) * width] = hit.astype(BF16)
                return 0

            lax.fori_loop(0, 2 * NYZ, rows, 0)

        group_wait(xbuf.at[it, row], xbuf.at[it], x_s.at[it], x_r.at[it], xs)
        abuf[it, me_yz] = xbuf[it, 0] + xbuf[it, 1] + xbuf[it, 2] + xbuf[it, 3]
        group_start(abuf.at[it, me_yz], abuf.at[it], me_yz, a_s.at[it], a_r.at[it], yzs)
        group_wait(abuf.at[it, me_yz], abuf.at[it], a_s.at[it], a_r.at[it], yzs)

        for b in range(NYZ):
            ans3[:, b * crange : (b + 1) * crange] = stack3(abuf[it, b])
        picked = stack3(sum3(dot(ans3[...], pick[...], NN)))
        for s in range(slots):
            found = dot(picked[:, :width], wo_hi[s], NN) + dot(picked[:, :width], wo_lo[s], NN)
            found = sum3(found)
            other = dot(picked[:, width:], wp_hi[s], NN) + dot(picked[:, width:], wp_lo[s], NN)
            other = sum3(other)
            for k in range(links):
                clink[s * links + k] = found[:, k * width : (k + 1) * width]
                cface[s * links + k] = other[:, k * width : (k + 1) * width]

        answer_copy.wait_recv()
        answer_copy.wait_send()
        force_copy.wait_send()
        alpha, beta = sc[2], sc[3]
        for b in range(blocks):
            s, k = b // links, b % links
            facing = partner[k, s] * links + k
            far = take(urecv[it, facing] + cface[facing], dof[b])
            image = (ulink[b] + clink[b] - far) * mask[b]
            image = image + beta * tv[b]
            tv[b] = jnp.where(it == 0, 0.0, image)
            yv[b] = jnp.where(it == 0, image, yv[b] - alpha * image)
        return 0

    lax.fori_loop(0, ITERS, body, 0)

    info_copy.wait_send()
    cpl_copy.wait_send()
    pxbuf[row] = scalar_terms()
    group_start(pxbuf.at[row], pxbuf, row, px_s, px_r, xs)
    group_wait(pxbuf.at[row], pxbuf, px_s, px_r, xs)
    pcbuf[ck] = pxbuf[0] + pxbuf[1] + pxbuf[2] + pxbuf[3]
    group_start(pcbuf.at[ck], pcbuf, ck, pc_s, pc_r, cs)
    group_wait(pcbuf.at[ck], pcbuf, pc_s, pc_r, cs)
    pybuf[me_yz] = pcbuf[0] + pcbuf[1]
    group_start(pybuf.at[me_yz], pybuf, me_yz, py_s, py_r, yzs)
    group_wait(pybuf.at[me_yz], pybuf, py_s, py_r, yzs)
    tile = pybuf[0]
    for b in range(1, NYZ):
        tile = tile + pybuf[b]
    r_out[...] = update(tile, None)


def local(
    flexibility,
    coupling,
    coarse_inverse,
    precon_weight,
    right_side,
    counts,
    partner,
    dof_index,
    corner_map,
):
    flex = flexibility[0, 0]
    cpl = coupling[0, 0]
    slots, iface = flex.shape[:2]
    half = iface // 2
    links, width = dof_index.shape[3:]
    loads = right_side.shape[3]
    own_rows, coarse = coarse_inverse.shape
    corners = corner_map.shape[-1]
    blocks = slots * links
    crange, cset = coarse // NYZ, own_rows * NYZ
    rows3 = 3 * loads

    weight = precon_weight[0, 0].reshape(blocks, 1, width)
    rhs = right_side[0, 0].transpose(0, 2, 1, 3).reshape(blocks, loads, width)
    slot_ids = jnp.arange(slots, dtype=jnp.int32)
    live = (slot_ids < counts[0, 0]).astype(F32)
    live = jnp.broadcast_to(live[:, None, None], (slots, 8, width))
    row_map = jnp.pad(
        corner_map[0, 0].reshape(-1).astype(F32), (0, width - slots * corners), constant_values=-1.0
    )
    info = jnp.concatenate([live, jnp.broadcast_to(row_map, (1, 8, width))], axis=0)
    own_partner = partner[0, 0]
    partner_inv = jnp.sum(
        jnp.where(own_partner[:, :, None] == slot_ids, slot_ids[None, :, None], 0), axis=1
    ).astype(jnp.int32)
    dof = dof_index[0, 0].reshape(blocks, 1, width)
    unknowns = jnp.arange(width, dtype=jnp.int32)
    dof_inv = jnp.sum(
        jnp.where(dof[:, 0, :, None] == unknowns, unknowns[None, :, None], 0), axis=1
    ).astype(jnp.int32)
    dof_inv = dof_inv[:, None, :]

    vec = (blocks, loads, width)
    vm = pltpu.VMEM
    dma = pltpu.SemaphoreType.DMA
    scratch = [
        vm((STAGES, iface, iface), F32),
        vm((slots, iface, iface), BF16),
        vm((slots, iface, iface), BF16),
        vm((NYZ, own_rows, crange), F32),
        vm((cset, crange), BF16),
        vm((cset, crange), BF16),
        vm((slots, corners, half), F32),
        vm((slots + 1, 8, width), F32),
        vm((NX * NK, 2, 8, width), F32),
        vm((slots, width, half), F32),
        vm((slots, width, half), BF16),
        vm((slots, width, half), BF16),
        vm((slots, width, half), BF16),
        vm((slots, width, half), BF16),
        vm((cset, NX * NK * 2 * width), BF16),
        vm((coarse, 2 * width), BF16),
        vm((ITERS, NK, NX, loads, 2 * width), F32),
        vm((ITERS, NY, loads, cset + width), F32),
        vm((ITERS, NZ, loads, cset + width), F32),
        vm((ITERS, NK, loads, crange), F32),
        vm((ITERS, NX, loads, crange), F32),
        vm((ITERS, NYZ, loads, crange), F32),
        vm((ITERS,) + vec, F32),
        vm((ITERS,) + vec, F32),
        vm((ITERS,) + vec, F32),
        vm((ITERS,) + vec, F32),
        vm(vec, F32),
        vm((slots, rows3, half), BF16),
        vm((slots, rows3, half), BF16),
        vm((slots, rows3, half), BF16),
        vm(vec, F32),
        vm(vec, F32),
        vm(vec, F32),
        vm(vec, F32),
        vm(vec, F32),
        vm(vec, F32),
        vm(vec, F32),
        vm(vec, F32),
        vm(vec, F32),
        vm(vec, F32),
        vm((4, loads, width), F32),
        vm((rows3, coarse), BF16),
        vm((NX, loads, width), F32),
        vm((NK, loads, width), F32),
        vm((NYZ, loads, width), F32),
        dma((slots,)),
        dma,
        dma,
        dma,
        dma,
        dma,
        dma((2, NX * NK - 1)),
        dma((2, NX * NK)),
        dma((NYZ - 1,)),
        dma((NYZ,)),
        dma((ITERS, NX - 1)),
        dma((ITERS, NX)),
        dma((ITERS, NK - 1)),
        dma((ITERS, NK)),
        dma((ITERS, NY - 1)),
        dma((ITERS, NY)),
        dma((ITERS, NZ - 1)),
        dma((ITERS, NZ)),
        dma((ITERS, NK - 1)),
        dma((ITERS, NK)),
        dma((ITERS, NX - 1)),
        dma((ITERS, NX)),
        dma((ITERS, NYZ - 1)),
        dma((ITERS, NYZ)),
        dma((ITERS,)),
        dma((ITERS,)),
        dma((ITERS,)),
        dma((ITERS,)),
        dma((NX - 1,)),
        dma((NX,)),
        dma((NK - 1,)),
        dma((NK,)),
        dma((NYZ - 1,)),
        dma((NYZ,)),
    ]
    in_vmem = pl.BlockSpec(memory_space=pltpu.VMEM)
    in_smem = pl.BlockSpec(memory_space=pltpu.SMEM)
    in_place = pl.BlockSpec(memory_space=pl.ANY)
    solved, resid = pl.pallas_call(
        kernel,
        name="feti",
        out_shape=[jax.ShapeDtypeStruct(vec, F32)] * 2,
        in_specs=[in_place, in_place] + [in_vmem] * 4 + [in_smem] * 2 + [in_vmem] * 2,
        out_specs=[in_vmem] * 2,
        scratch_shapes=scratch,
        compiler_params=pltpu.CompilerParams(
            collective_id=0, has_side_effects=True, vmem_limit_bytes=67043328
        ),
    )(flex, coarse_inverse, cpl, weight, rhs, info, own_partner, partner_inv, dof, dof_inv)

    def outer(value):
        value = value.reshape(slots, links, loads, width).transpose(0, 2, 1, 3)
        return value[None, None]

    return outer(solved), outer(resid)


def solution(mesh):
    in_specs = (
        P("row", "col", None, None, None),
        P("row", "col", None, None, None),
        P(("row", "col"), None),
        P("row", "col", None, None, None),
        P("row", "col", None, None, None, None),
        P("row", "col"),
        P("row", "col", None, None),
        P("row", "col", None, None, None),
        P("row", "col", None, None),
    )
    out_specs = (P("row", "col", None, None, None, None), P("row", "col", None, None, None, None))
    return jax.shard_map(local, mesh=mesh, in_specs=in_specs, out_specs=out_specs, check_vma=False)
```

```python
import functools

import jax
import jax.numpy as jnp
from jax import lax
from jax.experimental import pallas as pl
from jax.experimental.pallas import tpu as pltpu
from jax.sharding import PartitionSpec as P

ITERS = 3
NX, NZ, NY, NK = 4, 4, 4, 2
NYZ = NZ * NY
STAGES = 3

MESH = pl.DeviceIdType.MESH
F32 = jnp.float32
BF16 = jnp.bfloat16
NT = (((1,), (1,)), ((), ()))
NN = (((1,), (0,)), ((), ()))


def split2(value):
    high = value.astype(BF16)
    low = (value - high.astype(F32)).astype(BF16)
    return high, low


def split3(value):
    high = value.astype(BF16)
    rest = value - high.astype(F32)
    middle = rest.astype(BF16)
    low = (rest - middle.astype(F32)).astype(BF16)
    return high, middle, low


def stack3(value):
    return jnp.concatenate(split3(value), axis=0)


def dot(left, right, dims):
    return lax.dot_general(left, right, dims, preferred_element_type=F32)


def sum3(value):
    rows = value.shape[0] // 3
    return value[2 * rows :] + value[rows : 2 * rows] + value[:rows]


def rcopy(src, dst, send, recv, device):
    return pltpu.make_async_remote_copy(
        src_ref=src,
        dst_ref=dst,
        send_sem=send,
        recv_sem=recv,
        device_id=device,
        device_id_type=MESH,
    )


def group_start(src, buf, mine, send, recv, peers):
    for i, (device, _) in enumerate(peers):
        rcopy(src, buf.at[mine], send.at[i], recv.at[mine], device).start()


def group_wait(src, buf, send, recv, peers):
    for i, (device, theirs) in enumerate(peers):
        rcopy(src, buf.at[theirs], send.at[i], recv.at[theirs], device).wait_recv()
    for i, (device, theirs) in enumerate(peers):
        rcopy(src, buf.at[theirs], send.at[i], recv.at[theirs], device).wait_send()


def kernel(
    flex, cinv, cpl_in, weight_in, rhs_in, dof_in, map_in, partner, counts,
    x_out, r_out,
    stage, flex_hi, flex_lo, m32, m2, cpl, weight, rhs, dof, rowmap, dof_inv, cplp, info, infop,
    maps_yz, maps_xc, w32, wo, wp, scatter, pick, tbuf, cbuf, xbuf, y1buf, z1buf, y2buf, z2buf,
    psend, precv, qsend, qrecv, gsend, frecv, usend, urecv,
    vblk, vsp, gsp, fsp, yv, tv, dv, sv, zv, rv, mask, ulink, clink, cface, sc,
    pxbuf, pcbuf, pybuf,
    flex_sem, load_sem, mloc_sem, info_s, info_r, cpl_s, cpl_r, mapa_s, mapa_r, mapb_s, mapb_r,
    m_s, m_r, t_s, t_r, c_s, c_r, x_s, x_r, y1_s, y1_r, z1_s, z1_r, y2_s, y2_r, z2_s, z2_r,
    p_s, p_r, q_s, q_r, f_s, f_r, u_s, u_r, px_s, px_r, pc_s, pc_r, py_s, py_r,
):
    slots, iface = flex.shape[:2]
    half = iface // 2
    links, width = dof.shape[1:]
    loads = rhs.shape[1]
    corners = cpl.shape[1]
    own_rows, coarse = cinv.shape
    nxc = NX * NK
    kset = coarse // nxc
    rset = own_rows * nxc
    khalf = kset // 2
    blocks = slots * links
    tiles = 2 * width

    row, col = lax.axis_index("row"), lax.axis_index("col")
    cz = lax.div(col, NY * NK)
    cy = lax.rem(lax.div(col, NK), NY)
    ck = lax.rem(col, NK)
    cols = NZ * NY * NK
    me_yz = cz * NY + cy
    me_xc = ck * NX + row
    prev = (row, lax.rem(col + cols - 1, cols))
    nxt = (row, lax.rem(col + 1, cols))

    def device(x, z, y, k):
        return (x, (z * NY + y) * NK + k)

    def turn(value, by, size):
        return lax.rem(value + by, size)

    xs = [(device(turn(row, i, NX), cz, cy, ck), turn(row, i, NX)) for i in (2, 1, 3)]
    ys = [(device(row, cz, turn(cy, i, NY), ck), turn(cy, i, NY)) for i in (2, 1, 3)]
    zs = [(device(row, turn(cz, i, NZ), cy, ck), turn(cz, i, NZ)) for i in (2, 1, 3)]
    cs = [(device(row, cz, cy, 1 - ck), 1 - ck)]
    order = sorted(
        [(i, j) for i in range(NZ) for j in range(NY) if (i, j) != (0, 0)],
        key=lambda ij: -(min(ij[0], NZ - ij[0]) + min(ij[1], NY - ij[1])),
    )
    yzs = [
        (device(row, turn(cz, i, NZ), turn(cy, j, NY), ck), turn(cz, i, NZ) * NY + turn(cy, j, NY))
        for i, j in order
    ]
    xcs = [
        (device(turn(row, i, NX), cz, cy, turn(ck, j, NK)), turn(ck, j, NK) * NX + turn(row, i, NX))
        for i in (2, 1, 3, 0)
        for j in range(NK)
        if (i, j) != (0, 0)
    ]

    barrier = pltpu.get_barrier_semaphore()
    everyone = [d for d, _ in yzs] + [d for d, _ in xcs] + [prev, nxt]
    for d in everyone:
        pl.semaphore_signal(barrier, inc=1, device_id=d, device_id_type=MESH)

    def flex_copy(s):
        return pltpu.make_async_copy(flex.at[s], stage.at[s % STAGES], flex_sem.at[s])

    def m_part(other):
        return cinv.at[:, pl.ds(pl.multiple_of(other * kset, 128), kset)]

    loaded = [
        pltpu.make_async_copy(src, dst, load_sem.at[i])
        for i, (src, dst) in enumerate(
            [(map_in, rowmap), (dof_in, dof), (rhs_in, rhs), (weight_in, weight), (cpl_in, cpl)]
        )
    ]
    for copy in loaded:
        copy.start()
    m_local = pltpu.make_async_copy(m_part(me_xc), m32.at[me_xc], mloc_sem)
    m_local.start()
    for s in range(STAGES):
        flex_copy(s).start()

    for s in range(slots):
        live = jnp.where(s < counts[0, 0], 1.0, 0.0).astype(F32)
        info[s] = jnp.broadcast_to(live, (8, width))
    loaded[0].wait()
    lane8 = lax.broadcasted_iota(jnp.int32, (8, width), 1)
    found = jnp.full((8, width), -1, jnp.int32)
    for s in range(slots):
        ids = jnp.broadcast_to(rowmap[s : s + 1, :], (8, corners))
        ids = jnp.concatenate([ids, jnp.zeros((8, width - corners), jnp.int32)], axis=1)
        if s:
            ids = pltpu.roll(ids, s * corners, 1)
        inside = jnp.logical_and(lane8 >= s * corners, lane8 < (s + 1) * corners)
        found = jnp.where(inside, ids, found)
    info[slots] = found.astype(F32)

    pl.semaphore_wait(barrier, len(everyone))

    info_copy = rcopy(info, infop, info_s, info_r, nxt)
    info_copy.start()
    loaded[4].wait()
    cpl_copy = rcopy(cpl.at[:, :, half:], cplp, cpl_s, cpl_r, nxt)
    cpl_copy.start()
    for i, (d, other) in enumerate(xcs):
        rcopy(m_part(other), m32.at[me_xc], m_s.at[i], m_r.at[me_xc], d).start()
    map_groups = [(maps_yz, me_yz, mapa_s, mapa_r, yzs), (maps_xc, me_xc, mapb_s, mapb_r, xcs)]

    def send_maps(src, h):
        for buf, mine, send, recv, peers in map_groups:
            for i, (d, _) in enumerate(peers):
                rcopy(src, buf.at[mine, h], send.at[h, i], recv.at[h, mine], d).start()
            buf[mine, h] = src[...]

    def wait_maps(h, group):
        buf, _, send, recv, peers = map_groups[group]
        src = (info, infop)[h].at[slots]
        for i, (d, other) in enumerate(peers):
            cp = rcopy(src, buf.at[other, h], send.at[h, i], recv.at[h, other], d)
            cp.wait_recv()
            cp.wait_send()

    send_maps(info.at[slots], 0)

    w32[...] = jnp.zeros_like(w32)

    def build_coupling(source, out):
        for s in range(slots):
            w32[s, s * corners : (s + 1) * corners, :] = source[s, :, 0:half]
        for s in range(slots):
            high, low = split2(w32[s])
            out[s, 0:width] = high
            out[s, width:tiles] = low

    build_coupling(cpl, wo)
    tv[...] = jnp.zeros_like(tv)
    dv[...] = jnp.zeros_like(dv)
    sv[...] = jnp.zeros_like(sv)
    x_out[...] = jnp.zeros_like(x_out)
    sc[0] = jnp.ones_like(sc[0])
    sc[1] = jnp.zeros_like(sc[1])
    sc[2] = jnp.zeros_like(sc[2])
    sc[3] = jnp.zeros_like(sc[3])

    loaded[1].wait()
    sub = lax.broadcasted_iota(jnp.int32, (width, width), 0)
    numbers = lane8.astype(F32).astype(BF16)
    for b in range(blocks):
        ids = dof[b // links, b % links : b % links + 1, :]
        hit = jnp.where(sub == ids, 1.0, 0.0).astype(BF16)
        dof_inv[b] = dot(numbers, hit, NT).astype(jnp.int32)

    inverse = {}
    for k in range(links):
        for p in range(slots):
            at = jnp.int32(0)
            for j in range(1, slots):
                at = jnp.where(partner[k, j] == p, j, at)
            inverse[k, p] = at

    loaded[2].wait()
    loaded[3].wait()
    info_copy.wait_recv()
    send_maps(infop.at[slots], 1)

    def weight_of(b):
        return weight[b // links, b % links : b % links + 1, :]

    for b in range(blocks):
        s, k = b // links, b % links
        live = info[s] * infop[partner[k, s]]
        live = jnp.concatenate([live] * (loads // 8), axis=0)
        mask[b] = live
        resid = live * rhs[s, :, k, :]
        rv[b] = resid
        yv[b] = resid
        zv[b] = weight_of(b) * resid

    cpl_copy.wait_recv()
    build_coupling(cplp, wp)

    lane = lax.broadcasted_iota(jnp.int32, (loads, width), 1)
    load_id = lax.broadcasted_iota(jnp.int32, (loads, width), 0)

    def total(first, second):
        return jnp.sum(jnp.sum(first * second, axis=0), axis=1, keepdims=True)

    def scalar_terms(packed):
        z, y = zv[...], yv[...]
        found = [total(rv[...], z), total(z, y), total(z, sv[...]), total(dv[...], y)]
        tile = jnp.zeros((loads, width), F32)
        for i, value in enumerate(found):
            at = lane == (4 * load_id + i if packed else i)
            tile = jnp.where(at, value, tile)
        return tile

    def update(tile, packed, first):
        rz, zy, zs_, dy = [
            jnp.broadcast_to(
                jnp.sum(
                    jnp.where(lane == (4 * load_id + i if packed else i), tile, 0.0),
                    axis=1,
                    keepdims=True,
                ),
                tile.shape,
            )
            for i in range(4)
        ]
        beta = rz / sc[0]
        if first is not None:
            beta = jnp.where(first, 0.0, beta)
        curv = zy + beta * (zs_ + dy) + beta * beta * sc[1]
        alpha = rz / curv
        sc[0], sc[1], sc[2], sc[3] = rz, curv, alpha, beta
        direction = zv[...] + beta[None] * dv[...]
        image = yv[...] + beta[None] * sv[...]
        dv[...] = direction
        sv[...] = image
        x_out[...] = x_out[...] + alpha[None] * direction
        resid = rv[...] - alpha[None] * image
        rv[...] = resid
        return resid

    def put3(ref, s, k, value):
        for i, part in enumerate(split3(value)):
            ref[s, i * loads : (i + 1) * loads, k * width : (k + 1) * width] = part

    def take(value, index):
        return jnp.take_along_axis(value, index, axis=1, mode="promise_in_bounds")

    def convert(s):
        flex_copy(s).wait()
        here = s % STAGES

        def chunk(i, _):
            at = pl.ds(pl.multiple_of(i * 64, 64), 64)
            high, low = split2(stage[here, at, :])
            flex_hi[s, at, :] = high
            flex_lo[s, at, :] = low
            return 0

        lax.fori_loop(0, iface // 64, chunk, 0)
        if s + STAGES < slots:
            flex_copy(s + STAGES).start()

    def local_answers(it, first, last):
        def one(s, _):
            left = jnp.concatenate([vsp[s], fsp[s]], axis=1)
            for n in range(iface // 256):
                at = slice(n * 256, (n + 1) * 256)
                out = dot(left, flex_hi[s, :, at], NN) + dot(left, flex_lo[s, :, at], NN)
                out = sum3(out)
                for h in range(2):
                    piece = out[:, h * width : (h + 1) * width]
                    k = 2 * n + h
                    if k < links:
                        ulink[s * links + k] = piece
                    else:
                        usend[it, s * links + k - links] = piece
            return 0

        lax.fori_loop(first, last, one, 0)

    def both(value):
        return value[:, :width] + value[:, width:]

    def body(it, _):
        for b in range(blocks):
            value = weight_of(b) * yv[b]
            vblk[b] = value
            put3(vsp, b // links, b % links, value)
        for b in range(blocks):
            p, k = b // links, b % links
            from_block = inverse[k, p] * links + k
            index = jnp.concatenate([dof_inv[from_block]] * (loads // 8), axis=0)
            value = -take(vblk[from_block], index)
            gsend[it, b] = value
            put3(gsp, p, k, value)

        def terms(blocks3, factors):
            found = None
            for s in range(slots):
                part = dot(blocks3[s], factors[s], NT)
                found = part if found is None else found + part
            return both(sum3(found))

        tbuf[it, me_yz, :, 0:width] = terms(vsp, wo)
        tbuf[it, me_yz, :, width:tiles] = terms(gsp, wp)
        group_start(tbuf.at[it, me_yz], tbuf.at[it], me_yz, t_s.at[it], t_r.at[it], yzs)
        force_copy = rcopy(gsend.at[it], frecv.at[it], f_s.at[it], f_r.at[it], prev)
        force_copy.start()
        tile = scalar_terms(False)

        @pl.when(it == 0)
        def _():
            wait_maps(0, 0)
            wait_maps(1, 0)

            def rows(p, _):
                base = (lax.rem(p, NX) * cols + me_yz * NK + lax.div(p, NX)) * own_rows
                index = lax.broadcasted_iota(jnp.int32, (own_rows, width), 0) + base
                index = index.astype(F32)
                at = pl.ds(pl.multiple_of(p * own_rows, own_rows), own_rows)
                for q in range(NYZ):
                    for h in range(2):
                        hit = jnp.where(index == maps_yz[q, h, 0:1, :], 1.0, 0.0)
                        lo = (2 * q + h) * width
                        scatter[at, lo : lo + width] = hit.astype(BF16)
                return 0

            lax.fori_loop(0, nxc, rows, 0)
            for s in range(STAGES):
                convert(s)

        group_wait(tbuf.at[it, me_yz], tbuf.at[it], t_s.at[it], t_r.at[it], yzs)
        gathered = jnp.concatenate([stack3(tbuf[it, q]) for q in range(NYZ)], axis=1)
        cbuf[it, ck, :, 0:rset] = sum3(dot(gathered, scatter[...], NT))
        cbuf[it, ck, :, rset : rset + width] = tile
        group_start(cbuf.at[it, ck], cbuf.at[it], ck, c_s.at[it], c_r.at[it], cs)
        group_wait(cbuf.at[it, ck], cbuf.at[it], c_s.at[it], c_r.at[it], cs)
        xbuf[it, row] = cbuf[it, 0] + cbuf[it, 1]
        group_start(xbuf.at[it, row], xbuf.at[it], row, x_s.at[it], x_r.at[it], xs)

        force_copy.wait_recv()
        for b in range(blocks):
            put3(fsp, b // links, b % links, frecv[it, b])
        local_answers(it, 0, 3)

        @pl.when(it == 0)
        def _():
            m_local.wait()
            for i, (d, other) in enumerate(xcs):
                cp = rcopy(m_part(other), m32.at[other], m_s.at[i], m_r.at[other], d)
                cp.wait_recv()
                cp.wait_send()
            for b in range(nxc):
                high, low = split2(m32[b])
                m2[b * own_rows : (b + 1) * own_rows, :] = high
                m2[rset + b * own_rows : rset + (b + 1) * own_rows, :] = low

        group_wait(xbuf.at[it, row], xbuf.at[it], x_s.at[it], x_r.at[it], xs)
        load = xbuf[it, 0] + xbuf[it, 1] + xbuf[it, 2] + xbuf[it, 3]
        left = stack3(load[:, :rset])
        answer = sum3(dot(jnp.concatenate([left, left], axis=1), m2[...], NN))
        y1buf[it, cy, :, 0:khalf] = answer[:, :khalf]
        y1buf[it, cy, :, khalf : khalf + width] = load[:, rset:]
        z1buf[it, cz] = answer[:, khalf:]
        group_start(y1buf.at[it, cy], y1buf.at[it], cy, y1_s.at[it], y1_r.at[it], ys)
        group_start(z1buf.at[it, cz], z1buf.at[it], cz, z1_s.at[it], z1_r.at[it], zs)

        @pl.when(it == 0)
        def _():
            for s in range(STAGES, slots):
                convert(s)

        local_answers(it, 3, slots)

        group_wait(y1buf.at[it, cy], y1buf.at[it], y1_s.at[it], y1_r.at[it], ys)
        group_wait(z1buf.at[it, cz], z1buf.at[it], z1_s.at[it], z1_r.at[it], zs)
        z2buf[it, cz] = y1buf[it, 0] + y1buf[it, 1] + y1buf[it, 2] + y1buf[it, 3]
        y2buf[it, cy] = z1buf[it, 0] + z1buf[it, 1] + z1buf[it, 2] + z1buf[it, 3]
        group_start(z2buf.at[it, cz], z2buf.at[it], cz, z2_s.at[it], z2_r.at[it], zs)
        group_start(y2buf.at[it, cy], y2buf.at[it], cy, y2_s.at[it], y2_r.at[it], ys)
        answer_copy = rcopy(usend.at[it], urecv.at[it], u_s.at[it], u_r.at[it], nxt)
        answer_copy.start()

        @pl.when(it == 0)
        def _():
            wait_maps(0, 1)
            wait_maps(1, 1)
            step = own_rows

            def rows(b, _):
                index = lax.broadcasted_iota(jnp.int32, (step, width), 0) + (me_xc * kset + b * step)
                index = index.astype(F32)
                at = pl.ds(pl.multiple_of(b * step, step), step)
                for q in range(nxc):
                    for h in range(2):
                        hit = jnp.where(index == maps_xc[q, h, 0:1, :], 1.0, 0.0)
                        lo = (2 * q + h) * width
                        pick[at, lo : lo + width] = hit.astype(BF16)
                return 0

            lax.fori_loop(0, kset // step, rows, 0)

        group_wait(z2buf.at[it, cz], z2buf.at[it], z2_s.at[it], z2_r.at[it], zs)
        group_wait(y2buf.at[it, cy], y2buf.at[it], y2_s.at[it], y2_r.at[it], ys)
        first = z2buf[it, 0] + z2buf[it, 1] + z2buf[it, 2] + z2buf[it, 3]
        second = y2buf[it, 0] + y2buf[it, 1] + y2buf[it, 2] + y2buf[it, 3]
        scalars = first[:, khalf:]
        left = stack3(jnp.concatenate([first[:, :khalf], second], axis=1))
        found = sum3(dot(left, pick[...], NN))
        for q in range(nxc):
            psend[it, q // NX, q % NX] = found[:, q * tiles : (q + 1) * tiles]
        core_copy = rcopy(
            psend.at[it, 1 - ck], precv.at[it], p_s.at[it], p_r.at[it], cs[0][0]
        )
        core_copy.start()
        core_copy.wait()
        for q in range(NX):
            qsend[it, q] = psend[it, ck, q] + precv[it, q]
        for i, (d, other) in enumerate(xs):
            rcopy(
                qsend.at[it, other], qrecv.at[it, row], q_s.at[it, i], q_r.at[it, row], d
            ).start()
        qrecv[it, row] = qsend[it, row]

        @pl.when(it > 0)
        def _():
            resid = update(scalars, False, it == 1)
            for b in range(blocks):
                zv[b] = weight_of(b) * resid[b]

        for i, (d, other) in enumerate(xs):
            cp = rcopy(
                qsend.at[it, other], qrecv.at[it, other], q_s.at[it, i], q_r.at[it, other], d
            )
            cp.wait_recv()
            cp.wait_send()
        picked = stack3(qrecv[it, 0] + qrecv[it, 1] + qrecv[it, 2] + qrecv[it, 3])
        to_link = jnp.concatenate([picked[:, :width]] * 2, axis=1)
        to_face = jnp.concatenate([picked[:, width:]] * 2, axis=1)
        for s in range(slots):
            found = sum3(dot(to_link, wo[s], NN))
            other = sum3(dot(to_face, wp[s], NN))
            for k in range(links):
                clink[s * links + k] = found[:, k * width : (k + 1) * width]
                cface[s * links + k] = other[:, k * width : (k + 1) * width]

        answer_copy.wait_recv()
        answer_copy.wait_send()
        force_copy.wait_send()
        alpha, beta = sc[2], sc[3]
        for b in range(blocks):
            s, k = b // links, b % links
            facing = partner[k, s] * links + k
            index = jnp.broadcast_to(dof[s, k : k + 1, :], (loads, width))
            far = take(urecv[it, facing] + cface[facing], index)
            image = (ulink[b] + clink[b] - far) * mask[b]
            image = image + beta * tv[b]
            tv[b] = jnp.where(it == 0, 0.0, image)
            yv[b] = jnp.where(it == 0, image, yv[b] - alpha * image)
        return 0

    lax.fori_loop(0, ITERS, body, 0)

    info_copy.wait_send()
    cpl_copy.wait_send()
    pxbuf[row] = jnp.sum(scalar_terms(True), axis=0, keepdims=True)
    group_start(pxbuf.at[row], pxbuf, row, px_s, px_r, xs)
    group_wait(pxbuf.at[row], pxbuf, px_s, px_r, xs)
    pcbuf[ck] = pxbuf[0] + pxbuf[1] + pxbuf[2] + pxbuf[3]
    group_start(pcbuf.at[ck], pcbuf, ck, pc_s, pc_r, cs)
    group_wait(pcbuf.at[ck], pcbuf, pc_s, pc_r, cs)
    pybuf[me_yz] = pcbuf[0] + pcbuf[1]
    group_start(pybuf.at[me_yz], pybuf, me_yz, py_s, py_r, yzs)
    group_wait(pybuf.at[me_yz], pybuf, py_s, py_r, yzs)
    line = pybuf[0]
    for b in range(1, NYZ):
        line = line + pybuf[b]
    r_out[...] = update(jnp.broadcast_to(line, (loads, width)), True, None)


def local(
    flexibility,
    coupling,
    coarse_inverse,
    precon_weight,
    right_side,
    counts,
    partner,
    dof_index,
    corner_map,
):
    flex = flexibility[0, 0]
    cpl = coupling[0, 0]
    slots, iface = flex.shape[:2]
    half = iface // 2
    links, width = dof_index.shape[3:]
    loads = right_side.shape[3]
    own_rows, coarse = coarse_inverse.shape
    corners = corner_map.shape[-1]
    blocks = slots * links
    nxc = NX * NK
    kset, rset = coarse // nxc, own_rows * nxc
    rows3 = 3 * loads
    pair = 2 * width

    vec = (blocks, loads, width)
    per = (ITERS,)
    vm = pltpu.VMEM
    dma = pltpu.SemaphoreType.DMA
    scratch = [
        vm((STAGES, iface, iface), F32),
        vm((slots, iface, iface), BF16),
        vm((slots, iface, iface), BF16),
        vm((nxc, own_rows, kset), F32),
        vm((2 * rset, kset), BF16),
        vm(cpl.shape, F32),
        vm((slots, links, width), F32),
        vm((slots, loads, links, width), F32),
        vm((slots, links, width), jnp.int32),
        vm((slots, corners), jnp.int32),
        vm((blocks, 8, width), jnp.int32),
        vm((slots, corners, half), F32),
        vm((slots + 1, 8, width), F32),
        vm((slots + 1, 8, width), F32),
        vm((NYZ, 2, 8, width), F32),
        vm((nxc, 2, 8, width), F32),
        vm((slots, width, half), F32),
        vm((slots, pair, half), BF16),
        vm((slots, pair, half), BF16),
        vm((rset, NYZ * pair), BF16),
        vm((kset, nxc * pair), BF16),
        vm(per + (NYZ, loads, pair), F32),
        vm(per + (NK, loads, rset + width), F32),
        vm(per + (NX, loads, rset + width), F32),
        vm(per + (NY, loads, kset // 2 + width), F32),
        vm(per + (NZ, loads, kset // 2), F32),
        vm(per + (NY, loads, kset // 2), F32),
        vm(per + (NZ, loads, kset // 2 + width), F32),
        vm(per + (NK, NX, loads, pair), F32),
        vm(per + (NX, loads, pair), F32),
        vm(per + (NX, loads, pair), F32),
        vm(per + (NX, loads, pair), F32),
        vm(per + vec, F32),
        vm(per + vec, F32),
        vm(per + vec, F32),
        vm(per + vec, F32),
        vm(vec, F32),
        vm((slots, rows3, half), BF16),
        vm((slots, rows3, half), BF16),
        vm((slots, rows3, half), BF16),
    ]
    scratch += [vm(vec, F32)] * 10
    scratch += [
        vm((4, loads, width), F32),
        vm((NX, 1, width), F32),
        vm((NK, 1, width), F32),
        vm((NYZ, 1, width), F32),
        dma((slots,)),
        dma((5,)),
        dma,
        dma,
        dma,
        dma,
        dma,
        dma((2, NYZ - 1)),
        dma((2, NYZ)),
        dma((2, nxc - 1)),
        dma((2, nxc)),
        dma((nxc - 1,)),
        dma((nxc,)),
    ]
    for size in (NYZ, NK, NX, NY, NZ, NY, NZ):
        scratch += [dma(per + (size - 1,)), dma(per + (size,))]
    scratch += [dma(per)] * 2 + [dma(per + (NX - 1,)), dma(per + (NX,))] + [dma(per)] * 4
    for size in (NX, NK, NYZ):
        scratch += [dma((size - 1,)), dma((size,))]
    in_vmem = pl.BlockSpec(memory_space=pltpu.VMEM)
    in_smem = pl.BlockSpec(memory_space=pltpu.SMEM)
    in_place = pl.BlockSpec(memory_space=pl.ANY)
    solved, resid = pl.pallas_call(
        kernel,
        name="feti",
        out_shape=[jax.ShapeDtypeStruct(vec, F32)] * 2,
        in_specs=[in_place] * 7 + [in_smem] * 2,
        out_specs=[in_vmem] * 2,
        scratch_shapes=scratch,
        compiler_params=pltpu.CompilerParams(
            collective_id=0, has_side_effects=True, vmem_limit_bytes=67043328
        ),
    )(
        flex,
        coarse_inverse,
        cpl,
        precon_weight[0, 0],
        right_side[0, 0],
        dof_index[0, 0],
        corner_map[0, 0],
        partner[0, 0],
        counts,
    )

    def outer(value):
        value = value.reshape(slots, links, loads, width).transpose(0, 2, 1, 3)
        return value[None, None]

    return outer(solved), outer(resid)


def solution(mesh):
    in_specs = (
        P("row", "col", None, None, None),
        P("row", "col", None, None, None),
        P(("row", "col"), None),
        P("row", "col", None, None, None),
        P("row", "col", None, None, None, None),
        P("row", "col"),
        P("row", "col", None, None),
        P("row", "col", None, None, None),
        P("row", "col", None, None),
    )
    out_specs = (P("row", "col", None, None, None, None), P("row", "col", None, None, None, None))
    return jax.shard_map(local, mesh=mesh, in_specs=in_specs, out_specs=out_specs, check_vma=False)
```

```python
import functools

import jax
import jax.numpy as jnp
from jax import lax
from jax.experimental import pallas as pl
from jax.experimental.pallas import tpu as pltpu
from jax.sharding import PartitionSpec as P

ITERS = 3
NX, NZ, NY, NK = 4, 4, 4, 2
NYZ = NZ * NY
STAGES = 3

MESH = pl.DeviceIdType.MESH
F32 = jnp.float32
BF16 = jnp.bfloat16
NT = (((1,), (1,)), ((), ()))
NN = (((1,), (0,)), ((), ()))


def split2(value):
    high = value.astype(BF16)
    low = (value - high.astype(F32)).astype(BF16)
    return high, low


def split3(value):
    high = value.astype(BF16)
    rest = value - high.astype(F32)
    middle = rest.astype(BF16)
    low = (rest - middle.astype(F32)).astype(BF16)
    return high, middle, low


def stack3(value):
    return jnp.concatenate(split3(value), axis=0)


def dot(left, right, dims):
    return lax.dot_general(left, right, dims, preferred_element_type=F32)


def sum3(value):
    rows = value.shape[0] // 3
    return value[2 * rows :] + value[rows : 2 * rows] + value[:rows]


def rcopy(src, dst, send, recv, device):
    return pltpu.make_async_remote_copy(
        src_ref=src,
        dst_ref=dst,
        send_sem=send,
        recv_sem=recv,
        device_id=device,
        device_id_type=MESH,
    )


def group_start(src, buf, mine, send, recv, peers):
    for i, (device, _) in enumerate(peers):
        rcopy(src, buf.at[mine], send.at[i], recv.at[mine], device).start()


def group_wait(src, buf, send, recv, peers):
    for i, (device, theirs) in enumerate(peers):
        rcopy(src, buf.at[theirs], send.at[i], recv.at[theirs], device).wait_recv()
    for i, (device, theirs) in enumerate(peers):
        rcopy(src, buf.at[theirs], send.at[i], recv.at[theirs], device).wait_send()


def kernel(
    flex, cinv, cpl_in, weight_in, rhs_in, dof_in, map_in, partner, counts,
    x_out, r_out,
    stage, flex_hi, flex_lo, m32, m2, cpl, weight, rhs, dof, rowmap, dof_inv, cplp, info, infop,
    maps_yz, maps_xc, w32, wo, wp, scatter, pick, tbuf, cbuf, xbuf, y1buf, z1buf, y2buf, z2buf,
    psend, precv, qsend, qrecv, gsend, frecv, usend, urecv,
    vblk, vsp, gsp, fsp, yv, tv, dv, sv, zv, rv, mask, ulink, clink, cface, sc,
    pxbuf, pcbuf, pybuf,
    flex_sem, load_sem, mloc_sem, info_s, info_r, cpl_s, cpl_r, mapa_s, mapa_r, mapb_s, mapb_r,
    m_s, m_r, t_s, t_r, c_s, c_r, x_s, x_r, y1_s, y1_r, z1_s, z1_r, y2_s, y2_r, z2_s, z2_r,
    p_s, p_r, q_s, q_r, f_s, f_r, u_s, u_r, px_s, px_r, pc_s, pc_r, py_s, py_r,
):
    slots, iface = flex.shape[:2]
    half = iface // 2
    links, width = dof.shape[1:]
    loads = rhs.shape[1]
    corners = cpl.shape[1]
    own_rows, coarse = cinv.shape
    nxc = NX * NK
    kset = coarse // nxc
    rset = own_rows * nxc
    khalf = kset // 2
    blocks = slots * links
    tiles = 2 * width

    row, col = lax.axis_index("row"), lax.axis_index("col")
    cz = lax.div(col, NY * NK)
    cy = lax.rem(lax.div(col, NK), NY)
    ck = lax.rem(col, NK)
    cols = NZ * NY * NK
    me_yz = cz * NY + cy
    me_xc = ck * NX + row
    prev = (row, lax.rem(col + cols - 1, cols))
    nxt = (row, lax.rem(col + 1, cols))

    def device(x, z, y, k):
        return (x, (z * NY + y) * NK + k)

    def turn(value, by, size):
        return lax.rem(value + by, size)

    xs = [(device(turn(row, i, NX), cz, cy, ck), turn(row, i, NX)) for i in (2, 1, 3)]
    ys = [(device(row, cz, turn(cy, i, NY), ck), turn(cy, i, NY)) for i in (2, 1, 3)]
    zs = [(device(row, turn(cz, i, NZ), cy, ck), turn(cz, i, NZ)) for i in (2, 1, 3)]
    cs = [(device(row, cz, cy, 1 - ck), 1 - ck)]
    order = sorted(
        [(i, j) for i in range(NZ) for j in range(NY) if (i, j) != (0, 0)],
        key=lambda ij: -(min(ij[0], NZ - ij[0]) + min(ij[1], NY - ij[1])),
    )
    yzs = [
        (device(row, turn(cz, i, NZ), turn(cy, j, NY), ck), turn(cz, i, NZ) * NY + turn(cy, j, NY))
        for i, j in order
    ]
    xcs = [
        (device(turn(row, i, NX), cz, cy, turn(ck, j, NK)), turn(ck, j, NK) * NX + turn(row, i, NX))
        for i in (2, 1, 3, 0)
        for j in range(NK)
        if (i, j) != (0, 0)
    ]

    barrier = pltpu.get_barrier_semaphore()
    everyone = [d for d, _ in yzs] + [d for d, _ in xcs] + [prev, nxt]
    for d in everyone:
        pl.semaphore_signal(barrier, inc=1, device_id=d, device_id_type=MESH)

    def flex_copy(s):
        return pltpu.make_async_copy(flex.at[s], stage.at[s % STAGES], flex_sem.at[s])

    def m_part(other):
        return cinv.at[:, pl.ds(pl.multiple_of(other * kset, 128), kset)]

    loaded = [
        pltpu.make_async_copy(src, dst, load_sem.at[i])
        for i, (src, dst) in enumerate(
            [(map_in, rowmap), (dof_in, dof), (rhs_in, rhs), (weight_in, weight), (cpl_in, cpl)]
        )
    ]
    for copy in loaded:
        copy.start()
    m_local = pltpu.make_async_copy(m_part(me_xc), m32.at[me_xc], mloc_sem)
    m_local.start()
    for s in range(STAGES):
        flex_copy(s).start()

    for s in range(slots):
        live = jnp.where(s < counts[0, 0], 1.0, 0.0).astype(F32)
        info[s] = jnp.broadcast_to(live, (1, width))
    loaded[0].wait()
    lane8 = lax.broadcasted_iota(jnp.int32, (8, width), 1)
    found = jnp.full((8, width), -1, jnp.int32)
    for s in range(slots):
        ids = jnp.broadcast_to(rowmap[s], (8, corners))
        ids = jnp.concatenate([ids, jnp.zeros((8, width - corners), jnp.int32)], axis=1)
        if s:
            ids = pltpu.roll(ids, s * corners, 1)
        inside = jnp.logical_and(lane8 >= s * corners, lane8 < (s + 1) * corners)
        found = jnp.where(inside, ids, found)
    info[slots] = found[0:1].astype(F32)

    pl.semaphore_wait(barrier, len(everyone))

    info_copy = rcopy(info, infop, info_s, info_r, nxt)
    info_copy.start()
    loaded[4].wait()
    cpl_copy = rcopy(cpl.at[:, :, half:], cplp, cpl_s, cpl_r, nxt)
    cpl_copy.start()
    for i, (d, other) in enumerate(xcs):
        rcopy(m_part(other), m32.at[me_xc], m_s.at[i], m_r.at[me_xc], d).start()
    map_groups = [(maps_yz, me_yz, mapa_s, mapa_r, yzs), (maps_xc, me_xc, mapb_s, mapb_r, xcs)]

    def send_maps(src, h):
        for buf, mine, send, recv, peers in map_groups:
            for i, (d, _) in enumerate(peers):
                rcopy(src, buf.at[mine, h], send.at[h, i], recv.at[h, mine], d).start()
            buf[mine, h] = src[...]

    def wait_maps(h, group):
        buf, _, send, recv, peers = map_groups[group]
        src = (info, infop)[h].at[slots]
        for i, (d, other) in enumerate(peers):
            cp = rcopy(src, buf.at[other, h], send.at[h, i], recv.at[h, other], d)
            cp.wait_recv()
            cp.wait_send()

    send_maps(info.at[slots], 0)

    w32[...] = jnp.zeros_like(w32)

    def build_coupling(source, out):
        for s in range(slots):
            w32[s, s * corners : (s + 1) * corners, :] = source[s, :, 0:half]
        for s in range(slots):
            high, low = split2(w32[s])
            out[s, 0:width] = high
            out[s, width:tiles] = low

    build_coupling(cpl, wo)
    tv[...] = jnp.zeros_like(tv)
    dv[...] = jnp.zeros_like(dv)
    sv[...] = jnp.zeros_like(sv)
    x_out[...] = jnp.zeros_like(x_out)
    sc[0] = jnp.ones_like(sc[0])
    sc[1] = jnp.zeros_like(sc[1])
    sc[2] = jnp.zeros_like(sc[2])
    sc[3] = jnp.zeros_like(sc[3])

    loaded[1].wait()
    sub = lax.broadcasted_iota(jnp.int32, (width, width), 0)
    numbers = lane8.astype(F32).astype(BF16)
    for b in range(blocks):
        ids = dof[b // links, b % links : b % links + 1, :]
        hit = jnp.where(sub == ids, 1.0, 0.0).astype(BF16)
        dof_inv[b] = dot(numbers, hit, NT).astype(jnp.int32)

    inverse = {}
    for k in range(links):
        for p in range(slots):
            at = jnp.int32(0)
            for j in range(1, slots):
                at = jnp.where(partner[k, j] == p, j, at)
            inverse[k, p] = at

    loaded[2].wait()
    loaded[3].wait()
    info_copy.wait_recv()
    send_maps(infop.at[slots], 1)

    def weight_of(b):
        return weight[b // links, b % links : b % links + 1, :]

    for b in range(blocks):
        s, k = b // links, b % links
        live = info[s] * infop[partner[k, s]]
        live = jnp.broadcast_to(live, (loads, width))
        mask[b] = live
        resid = live * rhs[s, :, k, :]
        rv[b] = resid
        yv[b] = resid
        zv[b] = weight_of(b) * resid

    lane = lax.broadcasted_iota(jnp.int32, (loads, width), 1)
    load_id = lax.broadcasted_iota(jnp.int32, (loads, width), 0)

    def total(first, second):
        return jnp.sum(jnp.sum(first * second, axis=0), axis=1, keepdims=True)

    def scalar_terms(packed):
        z, y = zv[...], yv[...]
        found = [total(rv[...], z), total(z, y), total(z, sv[...]), total(dv[...], y)]
        tile = jnp.zeros((loads, width), F32)
        for i, value in enumerate(found):
            at = lane == (4 * load_id + i if packed else i)
            tile = jnp.where(at, value, tile)
        return tile

    def update(tile, packed, first):
        rz, zy, zs_, dy = [
            jnp.broadcast_to(
                jnp.sum(
                    jnp.where(lane == (4 * load_id + i if packed else i), tile, 0.0),
                    axis=1,
                    keepdims=True,
                ),
                tile.shape,
            )
            for i in range(4)
        ]
        beta = rz / sc[0]
        if first is not None:
            beta = jnp.where(first, 0.0, beta)
        curv = zy + beta * (zs_ + dy) + beta * beta * sc[1]
        alpha = rz / curv
        sc[0], sc[1], sc[2], sc[3] = rz, curv, alpha, beta
        direction = zv[...] + beta[None] * dv[...]
        image = yv[...] + beta[None] * sv[...]
        dv[...] = direction
        sv[...] = image
        x_out[...] = x_out[...] + alpha[None] * direction
        resid = rv[...] - alpha[None] * image
        rv[...] = resid
        return resid

    def put3(ref, s, k, value):
        for i, part in enumerate(split3(value)):
            ref[s, i * loads : (i + 1) * loads, k * width : (k + 1) * width] = part

    def take(value, index):
        return jnp.take_along_axis(value, index, axis=1, mode="promise_in_bounds")

    def convert(s):
        flex_copy(s).wait()
        here = s % STAGES

        def chunk(i, _):
            at = pl.ds(pl.multiple_of(i * 64, 64), 64)
            high, low = split2(stage[here, at, :])
            flex_hi[s, at, :] = high
            flex_lo[s, at, :] = low
            return 0

        lax.fori_loop(0, iface // 64, chunk, 0)
        if s + STAGES < slots:
            flex_copy(s + STAGES).start()

    def local_answers(it, first, last):
        def one(s, _):
            left = jnp.concatenate([vsp[s], fsp[s]], axis=1)
            for n in range(iface // 256):
                at = slice(n * 256, (n + 1) * 256)
                out = dot(left, flex_hi[s, :, at], NN) + dot(left, flex_lo[s, :, at], NN)
                out = sum3(out)
                for h in range(2):
                    piece = out[:, h * width : (h + 1) * width]
                    k = 2 * n + h
                    if k < links:
                        ulink[s * links + k] = piece
                    else:
                        usend[it, s * links + k - links] = piece
            return 0

        lax.fori_loop(first, last, one, 0)

    def both(value):
        return value[:, :width] + value[:, width:]

    def body(it, _):
        for b in range(blocks):
            value = weight_of(b) * yv[b]
            vblk[b] = value
            put3(vsp, b // links, b % links, value)
        for b in range(blocks):
            p, k = b // links, b % links
            from_block = inverse[k, p] * links + k
            index = jnp.concatenate([dof_inv[from_block]] * (loads // 8), axis=0)
            value = -take(vblk[from_block], index)
            gsend[it, b] = value
            put3(gsp, p, k, value)

        def terms(blocks3, factors):
            found = None
            for s in range(slots):
                part = dot(blocks3[s], factors[s], NT)
                found = part if found is None else found + part
            return both(sum3(found))

        tbuf[it, me_yz, :, 0:width] = terms(vsp, wo)

        @pl.when(it == 0)
        def _():
            cpl_copy.wait_recv()
            build_coupling(cplp, wp)

        tbuf[it, me_yz, :, width:tiles] = terms(gsp, wp)
        group_start(tbuf.at[it, me_yz], tbuf.at[it], me_yz, t_s.at[it], t_r.at[it], yzs)
        tile = scalar_terms(False)

        @pl.when(it == 0)
        def _():
            wait_maps(0, 0)
            wait_maps(1, 0)

            def rows(p, _):
                base = (lax.rem(p, NX) * cols + me_yz * NK + lax.div(p, NX)) * own_rows
                index = lax.broadcasted_iota(jnp.int32, (own_rows, width), 0) + base
                index = index.astype(F32)
                at = pl.ds(pl.multiple_of(p * own_rows, own_rows), own_rows)
                for q in range(NYZ):
                    for h in range(2):
                        hit = jnp.where(index == maps_yz[q, h], 1.0, 0.0)
                        scatter[q, at, h * width : (h + 1) * width] = hit.astype(BF16)
                return 0

            lax.fori_loop(0, nxc, rows, 0)
            for s in range(STAGES):
                convert(s)

        def spread(q):
            return dot(stack3(tbuf[it, q]), scatter[q], NT)

        found = spread(me_yz)
        arrivals = [
            rcopy(tbuf.at[it, me_yz], tbuf.at[it, q], t_s.at[it, i], t_r.at[it, q], d)
            for i, (d, q) in enumerate(yzs)
        ]
        for copy, (_, q) in reversed(list(zip(arrivals, yzs))):
            copy.wait_recv()
            found = found + spread(q)
        for copy in arrivals:
            copy.wait_send()
        cbuf[it, ck, :, 0:rset] = sum3(found)
        cbuf[it, ck, :, rset : rset + width] = tile
        group_start(cbuf.at[it, ck], cbuf.at[it], ck, c_s.at[it], c_r.at[it], cs)
        force_copy = rcopy(gsend.at[it], frecv.at[it], f_s.at[it], f_r.at[it], prev)
        force_copy.start()
        group_wait(cbuf.at[it, ck], cbuf.at[it], c_s.at[it], c_r.at[it], cs)
        xbuf[it, row] = cbuf[it, 0] + cbuf[it, 1]
        group_start(xbuf.at[it, row], xbuf.at[it], row, x_s.at[it], x_r.at[it], xs)

        @pl.when(it == 0)
        def _():
            for s in range(STAGES, slots):
                convert(s)
            m_local.wait()
            for i, (d, other) in enumerate(xcs):
                cp = rcopy(m_part(other), m32.at[other], m_s.at[i], m_r.at[other], d)
                cp.wait_recv()
                cp.wait_send()
            for b in range(nxc):
                high, low = split2(m32[b])
                m2[b * own_rows : (b + 1) * own_rows, :] = high
                m2[rset + b * own_rows : rset + (b + 1) * own_rows, :] = low

        group_wait(xbuf.at[it, row], xbuf.at[it], x_s.at[it], x_r.at[it], xs)
        load = xbuf[it, 0] + xbuf[it, 1] + xbuf[it, 2] + xbuf[it, 3]
        left = stack3(load[:, :rset])
        answer = sum3(dot(jnp.concatenate([left, left], axis=1), m2[...], NN))
        y1buf[it, cy, :, 0:khalf] = answer[:, :khalf]
        y1buf[it, cy, :, khalf : khalf + width] = load[:, rset:]
        z1buf[it, cz] = answer[:, khalf:]
        group_start(y1buf.at[it, cy], y1buf.at[it], cy, y1_s.at[it], y1_r.at[it], ys)
        group_start(z1buf.at[it, cz], z1buf.at[it], cz, z1_s.at[it], z1_r.at[it], zs)

        force_copy.wait_recv()
        for b in range(blocks):
            put3(fsp, b // links, b % links, frecv[it, b])
        local_answers(it, 0, 3)

        group_wait(y1buf.at[it, cy], y1buf.at[it], y1_s.at[it], y1_r.at[it], ys)
        group_wait(z1buf.at[it, cz], z1buf.at[it], z1_s.at[it], z1_r.at[it], zs)
        z2buf[it, cz] = y1buf[it, 0] + y1buf[it, 1] + y1buf[it, 2] + y1buf[it, 3]
        y2buf[it, cy] = z1buf[it, 0] + z1buf[it, 1] + z1buf[it, 2] + z1buf[it, 3]
        group_start(z2buf.at[it, cz], z2buf.at[it], cz, z2_s.at[it], z2_r.at[it], zs)
        group_start(y2buf.at[it, cy], y2buf.at[it], cy, y2_s.at[it], y2_r.at[it], ys)
        local_answers(it, 3, slots)

        @pl.when(it == 0)
        def _():
            wait_maps(0, 1)
            wait_maps(1, 1)
            step = own_rows

            def rows(b, _):
                index = lax.broadcasted_iota(jnp.int32, (step, width), 0) + (me_xc * kset + b * step)
                index = index.astype(F32)
                at = pl.ds(pl.multiple_of(b * step, step), step)
                for q in range(nxc):
                    for h in range(2):
                        hit = jnp.where(index == maps_xc[q, h], 1.0, 0.0)
                        lo = (2 * (q % NX) + h) * width
                        pick[q // NX, at, lo : lo + width] = hit.astype(BF16)
                return 0

            lax.fori_loop(0, kset // step, rows, 0)

        group_wait(z2buf.at[it, cz], z2buf.at[it], z2_s.at[it], z2_r.at[it], zs)
        group_wait(y2buf.at[it, cy], y2buf.at[it], y2_s.at[it], y2_r.at[it], ys)
        answer_copy = rcopy(usend.at[it], urecv.at[it], u_s.at[it], u_r.at[it], nxt)
        answer_copy.start()
        first = z2buf[it, 0] + z2buf[it, 1] + z2buf[it, 2] + z2buf[it, 3]
        second = y2buf[it, 0] + y2buf[it, 1] + y2buf[it, 2] + y2buf[it, 3]
        scalars = first[:, khalf:]
        left = stack3(jnp.concatenate([first[:, :khalf], second], axis=1))
        found = sum3(dot(left, pick[1 - ck], NN))
        for q in range(NX):
            psend[it, q] = found[:, q * tiles : (q + 1) * tiles]
        core_copy = rcopy(psend.at[it], precv.at[it], p_s.at[it], p_r.at[it], cs[0][0])
        core_copy.start()
        found = sum3(dot(left, pick[ck], NN))
        core_copy.wait()
        for q in range(NX):
            qsend[it, q] = found[:, q * tiles : (q + 1) * tiles] + precv[it, q]
        for i, (d, other) in enumerate(xs):
            rcopy(
                qsend.at[it, other], qrecv.at[it, row], q_s.at[it, i], q_r.at[it, row], d
            ).start()
        qrecv[it, row] = qsend[it, row]

        @pl.when(it > 0)
        def _():
            resid = update(scalars, False, it == 1)
            for b in range(blocks):
                zv[b] = weight_of(b) * resid[b]

        for i, (d, other) in enumerate(xs):
            cp = rcopy(
                qsend.at[it, other], qrecv.at[it, other], q_s.at[it, i], q_r.at[it, other], d
            )
            cp.wait_recv()
            cp.wait_send()
        picked = stack3(qrecv[it, 0] + qrecv[it, 1] + qrecv[it, 2] + qrecv[it, 3])
        to_link = jnp.concatenate([picked[:, :width]] * 2, axis=1)
        to_face = jnp.concatenate([picked[:, width:]] * 2, axis=1)
        for s in range(slots):
            found = sum3(dot(to_link, wo[s], NN))
            other = sum3(dot(to_face, wp[s], NN))
            for k in range(links):
                clink[s * links + k] = found[:, k * width : (k + 1) * width]
                cface[s * links + k] = other[:, k * width : (k + 1) * width]

        answer_copy.wait_recv()
        answer_copy.wait_send()
        force_copy.wait_send()
        alpha, beta = sc[2], sc[3]
        for b in range(blocks):
            s, k = b // links, b % links
            facing = partner[k, s] * links + k
            index = jnp.broadcast_to(dof[s, k : k + 1, :], (loads, width))
            far = take(urecv[it, facing] + cface[facing], index)
            image = (ulink[b] + clink[b] - far) * mask[b]
            image = image + beta * tv[b]
            tv[b] = jnp.where(it == 0, 0.0, image)
            yv[b] = jnp.where(it == 0, image, yv[b] - alpha * image)
        return 0

    lax.fori_loop(0, ITERS, body, 0)

    info_copy.wait_send()
    cpl_copy.wait_send()
    pxbuf[row] = jnp.sum(scalar_terms(True), axis=0, keepdims=True)
    group_start(pxbuf.at[row], pxbuf, row, px_s, px_r, xs)
    group_wait(pxbuf.at[row], pxbuf, px_s, px_r, xs)
    pcbuf[ck] = pxbuf[0] + pxbuf[1] + pxbuf[2] + pxbuf[3]
    group_start(pcbuf.at[ck], pcbuf, ck, pc_s, pc_r, cs)
    group_wait(pcbuf.at[ck], pcbuf, pc_s, pc_r, cs)
    pybuf[me_yz] = pcbuf[0] + pcbuf[1]
    group_start(pybuf.at[me_yz], pybuf, me_yz, py_s, py_r, yzs)
    group_wait(pybuf.at[me_yz], pybuf, py_s, py_r, yzs)
    line = pybuf[0]
    for b in range(1, NYZ):
        line = line + pybuf[b]
    r_out[...] = update(jnp.broadcast_to(line, (loads, width)), True, None)


def local(
    flexibility,
    coupling,
    coarse_inverse,
    precon_weight,
    right_side,
    counts,
    partner,
    dof_index,
    corner_map,
):
    flex = flexibility[0, 0]
    cpl = coupling[0, 0]
    slots, iface = flex.shape[:2]
    half = iface // 2
    links, width = dof_index.shape[3:]
    loads = right_side.shape[3]
    own_rows, coarse = coarse_inverse.shape
    corners = corner_map.shape[-1]
    blocks = slots * links
    nxc = NX * NK
    kset, rset = coarse // nxc, own_rows * nxc
    rows3 = 3 * loads
    pair = 2 * width

    vec = (blocks, loads, width)
    per = (ITERS,)
    vm = pltpu.VMEM
    dma = pltpu.SemaphoreType.DMA
    scratch = [
        vm((STAGES, iface, iface), F32),
        vm((slots, iface, iface), BF16),
        vm((slots, iface, iface), BF16),
        vm((nxc, own_rows, kset), F32),
        vm((2 * rset, kset), BF16),
        vm(cpl.shape, F32),
        vm((slots, links, width), F32),
        vm((slots, loads, links, width), F32),
        vm((slots, links, width), jnp.int32),
        vm((slots, 1, corners), jnp.int32),
        vm((blocks, 8, width), jnp.int32),
        vm((slots, corners, half), F32),
        vm((slots + 1, 1, width), F32),
        vm((slots + 1, 1, width), F32),
        vm((NYZ, 2, 1, width), F32),
        vm((nxc, 2, 1, width), F32),
        vm((slots, width, half), F32),
        vm((slots, pair, half), BF16),
        vm((slots, pair, half), BF16),
        vm((NYZ, rset, pair), BF16),
        vm((NK, kset, NX * pair), BF16),
        vm(per + (NYZ, loads, pair), F32),
        vm(per + (NK, loads, rset + width), F32),
        vm(per + (NX, loads, rset + width), F32),
        vm(per + (NY, loads, kset // 2 + width), F32),
        vm(per + (NZ, loads, kset // 2), F32),
        vm(per + (NY, loads, kset // 2), F32),
        vm(per + (NZ, loads, kset // 2 + width), F32),
        vm(per + (NX, loads, pair), F32),
        vm(per + (NX, loads, pair), F32),
        vm(per + (NX, loads, pair), F32),
        vm(per + (NX, loads, pair), F32),
        vm(per + vec, F32),
        vm(per + vec, F32),
        vm(per + vec, F32),
        vm(per + vec, F32),
        vm(vec, F32),
        vm((slots, rows3, half), BF16),
        vm((slots, rows3, half), BF16),
        vm((slots, rows3, half), BF16),
    ]
    scratch += [vm(vec, F32)] * 10
    scratch += [
        vm((4, loads, width), F32),
        vm((NX, 1, width), F32),
        vm((NK, 1, width), F32),
        vm((NYZ, 1, width), F32),
        dma((slots,)),
        dma((5,)),
        dma,
        dma,
        dma,
        dma,
        dma,
        dma((2, NYZ - 1)),
        dma((2, NYZ)),
        dma((2, nxc - 1)),
        dma((2, nxc)),
        dma((nxc - 1,)),
        dma((nxc,)),
    ]
    for size in (NYZ, NK, NX, NY, NZ, NY, NZ):
        scratch += [dma(per + (size - 1,)), dma(per + (size,))]
    scratch += [dma(per)] * 2 + [dma(per + (NX - 1,)), dma(per + (NX,))] + [dma(per)] * 4
    for size in (NX, NK, NYZ):
        scratch += [dma((size - 1,)), dma((size,))]
    in_vmem = pl.BlockSpec(memory_space=pltpu.VMEM)
    in_smem = pl.BlockSpec(memory_space=pltpu.SMEM)
    in_place = pl.BlockSpec(memory_space=pl.ANY)
    solved, resid = pl.pallas_call(
        kernel,
        name="feti",
        out_shape=[jax.ShapeDtypeStruct(vec, F32)] * 2,
        in_specs=[in_place] * 7 + [in_smem] * 2,
        out_specs=[in_vmem] * 2,
        scratch_shapes=scratch,
        compiler_params=pltpu.CompilerParams(
            collective_id=0, has_side_effects=True, vmem_limit_bytes=67043328
        ),
    )(
        flex,
        coarse_inverse,
        cpl,
        precon_weight[0, 0],
        right_side[0, 0],
        dof_index[0, 0],
        corner_map.reshape(slots, 1, corners),
        partner[0, 0],
        counts,
    )

    def outer(value):
        value = value.reshape(slots, links, loads, width).transpose(0, 2, 1, 3)
        return value[None, None]

    return outer(solved), outer(resid)


def solution(mesh):
    in_specs = (
        P("row", "col", None, None, None),
        P("row", "col", None, None, None),
        P(("row", "col"), None),
        P("row", "col", None, None, None),
        P("row", "col", None, None, None, None),
        P("row", "col"),
        P("row", "col", None, None),
        P("row", "col", None, None, None),
        P("row", "col", None, None),
    )
    out_specs = (P("row", "col", None, None, None, None), P("row", "col", None, None, None, None))
    return jax.shard_map(local, mesh=mesh, in_specs=in_specs, out_specs=out_specs, check_vma=False)
```

```python
import functools

import jax
import jax.numpy as jnp
from jax import lax
from jax.experimental import pallas as pl
from jax.experimental.pallas import tpu as pltpu
from jax.sharding import PartitionSpec as P

ITERS = 3
NX, NZ, NY, NK = 4, 4, 4, 2
NYZ = NZ * NY
STAGES = 3

MESH = pl.DeviceIdType.MESH
F32 = jnp.float32
BF16 = jnp.bfloat16
NT = (((1,), (1,)), ((), ()))
NN = (((1,), (0,)), ((), ()))


def split2(value):
    high = value.astype(BF16)
    low = (value - high.astype(F32)).astype(BF16)
    return high, low


def split3(value):
    high = value.astype(BF16)
    rest = value - high.astype(F32)
    middle = rest.astype(BF16)
    low = (rest - middle.astype(F32)).astype(BF16)
    return high, middle, low


def stack3(value):
    return jnp.concatenate(split3(value), axis=0)


def dot(left, right, dims):
    return lax.dot_general(left, right, dims, preferred_element_type=F32)


def sum3(value):
    rows = value.shape[0] // 3
    return value[2 * rows :] + value[rows : 2 * rows] + value[:rows]


def rcopy(src, dst, send, recv, device):
    return pltpu.make_async_remote_copy(
        src_ref=src,
        dst_ref=dst,
        send_sem=send,
        recv_sem=recv,
        device_id=device,
        device_id_type=MESH,
    )


def group_start(src, buf, mine, send, recv, peers):
    for i, (device, _) in enumerate(peers):
        rcopy(src, buf.at[mine], send.at[i], recv.at[mine], device).start()


def group_wait(src, buf, send, recv, peers):
    for i, (device, theirs) in enumerate(peers):
        rcopy(src, buf.at[theirs], send.at[i], recv.at[theirs], device).wait_recv()


def group_sent(src, buf, send, recv, peers):
    for i, (device, theirs) in enumerate(peers):
        rcopy(src, buf.at[theirs], send.at[i], recv.at[theirs], device).wait_send()


def kernel(
    flex, cinv, cpl_in, weight_in, rhs_in, dof_in, map_in, partner, counts,
    x_out, r_out,
    stage, flex_hi, flex_lo, m32, m2, cpl, weight, rhs, dof, rowmap, dof_inv, cplp, info, infop,
    maps_yz, maps_xc, wo, wp, scatter, pick, tbuf, cbuf, xbuf, y1buf, z1buf, y2buf, z2buf,
    psend, precv, qsend, qrecv, gsend, frecv, usend, urecv,
    vblk, vsp, gsp, fsp, yv, tv, dv, sv, zv, rv, mask, ulink, clink, cface, sc,
    pxbuf, pcbuf, pybuf,
    flex_sem, load_sem, mloc_sem, info_s, info_r, cpl_s, cpl_r, mapa_s, mapa_r, mapb_s, mapb_r,
    m_s, m_r, t_s, t_r, c_s, c_r, x_s, x_r, y1_s, y1_r, z1_s, z1_r, y2_s, y2_r, z2_s, z2_r,
    p_s, p_r, q_s, q_r, f_s, f_r, u_s, u_r, px_s, px_r, pc_s, pc_r, py_s, py_r,
):
    slots, iface = flex.shape[:2]
    half = iface // 2
    links, width = dof.shape[1:]
    loads = rhs.shape[1]
    corners = cpl.shape[1]
    own_rows, coarse = cinv.shape
    nxc = NX * NK
    kset = coarse // nxc
    rset = own_rows * nxc
    khalf = kset // 2
    blocks = slots * links
    tiles = 2 * width

    row, col = lax.axis_index("row"), lax.axis_index("col")
    cz = lax.div(col, NY * NK)
    cy = lax.rem(lax.div(col, NK), NY)
    ck = lax.rem(col, NK)
    cols = NZ * NY * NK
    me_yz = cz * NY + cy
    me_xc = ck * NX + row
    prev = (row, lax.rem(col + cols - 1, cols))
    nxt = (row, lax.rem(col + 1, cols))

    def device(x, z, y, k):
        return (x, (z * NY + y) * NK + k)

    def turn(value, by, size):
        return lax.rem(value + by, size)

    xs = [(device(turn(row, i, NX), cz, cy, ck), turn(row, i, NX)) for i in (2, 1, 3)]
    ys = [(device(row, cz, turn(cy, i, NY), ck), turn(cy, i, NY)) for i in (2, 1, 3)]
    zs = [(device(row, turn(cz, i, NZ), cy, ck), turn(cz, i, NZ)) for i in (2, 1, 3)]
    cs = [(device(row, cz, cy, 1 - ck), 1 - ck)]
    order = sorted(
        [(i, j) for i in range(NZ) for j in range(NY) if (i, j) != (0, 0)],
        key=lambda ij: -(min(ij[0], NZ - ij[0]) + min(ij[1], NY - ij[1])),
    )
    yzs = [
        (device(row, turn(cz, i, NZ), turn(cy, j, NY), ck), turn(cz, i, NZ) * NY + turn(cy, j, NY))
        for i, j in order
    ]
    xcs = [
        (device(turn(row, i, NX), cz, cy, turn(ck, j, NK)), turn(ck, j, NK) * NX + turn(row, i, NX))
        for i in (2, 1, 3, 0)
        for j in range(NK)
        if (i, j) != (0, 0)
    ]

    barrier = pltpu.get_barrier_semaphore()
    everyone = [d for d, _ in yzs] + [d for d, _ in xcs] + [prev, nxt]
    for d in everyone:
        pl.semaphore_signal(barrier, inc=1, device_id=d, device_id_type=MESH)

    def flex_copy(s):
        return pltpu.make_async_copy(flex.at[s], stage.at[s % STAGES], flex_sem.at[s])

    def m_part(other):
        return cinv.at[:, pl.ds(pl.multiple_of(other * kset, 128), kset)]

    loaded = [
        pltpu.make_async_copy(src, dst, load_sem.at[i])
        for i, (src, dst) in enumerate(
            [(map_in, rowmap), (dof_in, dof), (rhs_in, rhs), (weight_in, weight), (cpl_in, cpl)]
        )
    ]
    for copy in loaded:
        copy.start()
    m_local = pltpu.make_async_copy(m_part(me_xc), m32.at[me_xc], mloc_sem)
    m_local.start()
    for s in range(STAGES):
        flex_copy(s).start()

    for s in range(slots):
        live = jnp.where(s < counts[0, 0], 1.0, 0.0).astype(F32)
        info[s] = jnp.broadcast_to(live, (1, width))
    loaded[0].wait()
    lane8 = lax.broadcasted_iota(jnp.int32, (8, width), 1)
    found = jnp.full((8, width), -1, jnp.int32)
    for s in range(slots):
        ids = jnp.broadcast_to(rowmap[s], (8, corners))
        ids = jnp.concatenate([ids, jnp.zeros((8, width - corners), jnp.int32)], axis=1)
        if s:
            ids = pltpu.roll(ids, s * corners, 1)
        inside = jnp.logical_and(lane8 >= s * corners, lane8 < (s + 1) * corners)
        found = jnp.where(inside, ids, found)
    info[slots] = found[0:1].astype(F32)

    pl.semaphore_wait(barrier, len(everyone))

    info_copy = rcopy(info, infop, info_s, info_r, nxt)
    info_copy.start()
    loaded[4].wait()
    cpl_copy = rcopy(cpl.at[:, :, half:], cplp, cpl_s, cpl_r, nxt)
    cpl_copy.start()
    for i, (d, other) in enumerate(xcs):
        rcopy(m_part(other), m32.at[me_xc], m_s.at[i], m_r.at[me_xc], d).start()
    map_groups = [(maps_yz, me_yz, mapa_s, mapa_r, yzs), (maps_xc, me_xc, mapb_s, mapb_r, xcs)]

    def send_maps(src, h):
        for buf, mine, send, recv, peers in map_groups:
            for i, (d, _) in enumerate(peers):
                rcopy(src, buf.at[mine, h], send.at[h, i], recv.at[h, mine], d).start()
            buf[mine, h] = src[...]

    def wait_maps(h, group):
        buf, _, send, recv, peers = map_groups[group]
        src = (info, infop)[h].at[slots]
        for i, (d, other) in enumerate(peers):
            cp = rcopy(src, buf.at[other, h], send.at[h, i], recv.at[h, other], d)
            cp.wait_recv()
            cp.wait_send()

    send_maps(info.at[slots], 0)

    def build_coupling(source, out):
        for s in range(slots):
            value = source[s, :, 0:half]
            high = value.astype(BF16).astype(F32)
            out[s] = jnp.concatenate([high, value - high], axis=0).astype(BF16)

    build_coupling(cpl, wo)
    tv[...] = jnp.zeros_like(tv)
    dv[...] = jnp.zeros_like(dv)
    sv[...] = jnp.zeros_like(sv)
    x_out[...] = jnp.zeros_like(x_out)
    sc[0] = jnp.ones_like(sc[0])
    sc[1] = jnp.zeros_like(sc[1])
    sc[2] = jnp.zeros_like(sc[2])
    sc[3] = jnp.zeros_like(sc[3])

    loaded[1].wait()
    sub = lax.broadcasted_iota(jnp.int32, (width, width), 0)
    numbers = lane8.astype(F32).astype(BF16)
    for b in range(blocks):
        ids = dof[b // links, b % links : b % links + 1, :]
        hit = jnp.where(sub == ids, 1.0, 0.0).astype(BF16)
        dof_inv[b] = dot(numbers, hit, NT).astype(jnp.int32)

    inverse = {}
    for k in range(links):
        for p in range(slots):
            at = jnp.int32(0)
            for j in range(1, slots):
                at = jnp.where(partner[k, j] == p, j, at)
            inverse[k, p] = at

    loaded[2].wait()
    loaded[3].wait()
    info_copy.wait_recv()
    send_maps(infop.at[slots], 1)

    def weight_of(b):
        return weight[b // links, b % links : b % links + 1, :]

    for b in range(blocks):
        s, k = b // links, b % links
        live = info[s] * infop[partner[k, s]]
        live = jnp.broadcast_to(live, (loads, width))
        mask[b] = live
        resid = live * rhs[s, :, k, :]
        rv[b] = resid
        yv[b] = resid
        zv[b] = weight_of(b) * resid

    lane = lax.broadcasted_iota(jnp.int32, (loads, width), 1)
    load_id = lax.broadcasted_iota(jnp.int32, (loads, width), 0)

    def total(first, second):
        return jnp.sum(jnp.sum(first * second, axis=0), axis=1, keepdims=True)

    def scalar_terms(packed):
        z, y = zv[...], yv[...]
        found = [total(rv[...], z), total(z, y), total(z, sv[...]), total(dv[...], y)]
        tile = jnp.zeros((loads, width), F32)
        for i, value in enumerate(found):
            at = lane == (4 * load_id + i if packed else i)
            tile = jnp.where(at, value, tile)
        return tile

    def update(tile, packed, first):
        rz, zy, zs_, dy = [
            jnp.broadcast_to(
                jnp.sum(
                    jnp.where(lane == (4 * load_id + i if packed else i), tile, 0.0),
                    axis=1,
                    keepdims=True,
                ),
                tile.shape,
            )
            for i in range(4)
        ]
        beta = rz / sc[0]
        if first is not None:
            beta = jnp.where(first, 0.0, beta)
        curv = zy + beta * (zs_ + dy) + beta * beta * sc[1]
        alpha = rz / curv
        sc[0], sc[1], sc[2], sc[3] = rz, curv, alpha, beta
        direction = zv[...] + beta[None] * dv[...]
        image = yv[...] + beta[None] * sv[...]
        dv[...] = direction
        sv[...] = image
        x_out[...] = x_out[...] + alpha[None] * direction
        resid = rv[...] - alpha[None] * image
        rv[...] = resid
        return resid

    def put3(ref, s, k, value):
        for i, part in enumerate(split3(value)):
            ref[s, i * loads : (i + 1) * loads, k * width : (k + 1) * width] = part

    def take(value, index):
        return jnp.take_along_axis(value, index, axis=1, mode="promise_in_bounds")

    def convert(s):
        flex_copy(s).wait()
        here = s % STAGES

        def chunk(i, _):
            at = pl.ds(pl.multiple_of(i * 64, 64), 64)
            high, low = split2(stage[here, at, :])
            flex_hi[s, at, :] = high
            flex_lo[s, at, :] = low
            return 0

        lax.fori_loop(0, iface // 64, chunk, 0)
        if s + STAGES < slots:
            flex_copy(s + STAGES).start()

    def local_answers(it, first, last):
        def one(s, _):
            left = jnp.concatenate([vsp[s], fsp[s]], axis=1)
            for n in range(iface // 256):
                at = slice(n * 256, (n + 1) * 256)
                out = dot(left, flex_hi[s, :, at], NN) + dot(left, flex_lo[s, :, at], NN)
                out = sum3(out)
                for h in range(2):
                    piece = out[:, h * width : (h + 1) * width]
                    k = 2 * n + h
                    if k < links:
                        ulink[s * links + k] = piece
                    else:
                        usend[it, s * links + k - links] = piece
            return 0

        lax.fori_loop(first, last, one, 0)

    def within(s):
        return jnp.logical_and(lane >= s * corners, lane < (s + 1) * corners)

    def shift(value, by):
        by = by % width
        return pltpu.roll(value, by, 1) if by else value

    def sent(it):
        group_sent(tbuf.at[it, me_yz], tbuf.at[it], t_s.at[it], t_r.at[it], yzs)
        group_sent(cbuf.at[it, ck], cbuf.at[it], c_s.at[it], c_r.at[it], cs)
        group_sent(xbuf.at[it, row], xbuf.at[it], x_s.at[it], x_r.at[it], xs)
        group_sent(y1buf.at[it, cy], y1buf.at[it], y1_s.at[it], y1_r.at[it], ys)
        group_sent(z1buf.at[it, cz], z1buf.at[it], z1_s.at[it], z1_r.at[it], zs)
        group_sent(z2buf.at[it, cz], z2buf.at[it], z2_s.at[it], z2_r.at[it], zs)
        group_sent(y2buf.at[it, cy], y2buf.at[it], y2_s.at[it], y2_r.at[it], ys)
        rcopy(psend.at[it], precv.at[it], p_s.at[it], p_r.at[it], cs[0][0]).wait_send()
        group_sent(qsend.at[it, row], qrecv.at[it], q_s.at[it], q_r.at[it], xs)
        rcopy(gsend.at[it], frecv.at[it], f_s.at[it], f_r.at[it], prev).wait_send()
        rcopy(usend.at[it], urecv.at[it], u_s.at[it], u_r.at[it], nxt).wait_send()

    def body(it, _):
        for b in range(blocks):
            value = weight_of(b) * yv[b]
            vblk[b] = value
            put3(vsp, b // links, b % links, value)
        for b in range(blocks):
            p, k = b // links, b % links
            from_block = inverse[k, p] * links + k
            index = jnp.concatenate([dof_inv[from_block]] * (loads // 8), axis=0)
            value = -take(vblk[from_block], index)
            gsend[it, b] = value
            put3(gsp, p, k, value)

        def terms(blocks3, factors):
            found = jnp.zeros((loads, width), F32)
            for s in range(slots):
                part = sum3(dot(blocks3[s], factors[s], NT))
                rest = jnp.zeros((loads, width - 2 * corners), F32)
                part = jnp.concatenate([part, rest], axis=1)
                part = shift(part, s * corners) + shift(part, (s - 1) * corners)
                found = jnp.where(within(s), part, found)
            return found

        tbuf[it, me_yz, :, 0:width] = terms(vsp, wo)

        @pl.when(it == 0)
        def _():
            cpl_copy.wait_recv()
            build_coupling(cplp, wp)

        tbuf[it, me_yz, :, width:tiles] = terms(gsp, wp)
        group_start(tbuf.at[it, me_yz], tbuf.at[it], me_yz, t_s.at[it], t_r.at[it], yzs)
        tile = scalar_terms(False)

        @pl.when(it > 0)
        def _():
            sent(it - 1)

        @pl.when(it == 0)
        def _():
            wait_maps(0, 0)
            wait_maps(1, 0)

            def rows(p, _):
                base = (lax.rem(p, NX) * cols + me_yz * NK + lax.div(p, NX)) * own_rows
                index = lax.broadcasted_iota(jnp.int32, (own_rows, width), 0) + base
                index = index.astype(F32)
                at = pl.ds(pl.multiple_of(p * own_rows, own_rows), own_rows)
                for q in range(NYZ):
                    for h in range(2):
                        hit = jnp.where(index == maps_yz[q, h], 1.0, 0.0)
                        scatter[q, at, h * width : (h + 1) * width] = hit.astype(BF16)
                return 0

            lax.fori_loop(0, nxc, rows, 0)
            for s in range(STAGES):
                convert(s)

        def spread(q):
            return dot(stack3(tbuf[it, q]), scatter[q], NT)

        found = spread(me_yz)
        arrivals = [
            rcopy(tbuf.at[it, me_yz], tbuf.at[it, q], t_s.at[it, i], t_r.at[it, q], d)
            for i, (d, q) in enumerate(yzs)
        ]
        for copy, (_, q) in reversed(list(zip(arrivals, yzs))):
            copy.wait_recv()
            found = found + spread(q)
        cbuf[it, ck, :, 0:rset] = sum3(found)
        cbuf[it, ck, :, rset : rset + width] = tile
        group_start(cbuf.at[it, ck], cbuf.at[it], ck, c_s.at[it], c_r.at[it], cs)
        force_copy = rcopy(gsend.at[it], frecv.at[it], f_s.at[it], f_r.at[it], prev)
        force_copy.start()
        group_wait(cbuf.at[it, ck], cbuf.at[it], c_s.at[it], c_r.at[it], cs)
        xbuf[it, row] = cbuf[it, 0] + cbuf[it, 1]
        group_start(xbuf.at[it, row], xbuf.at[it], row, x_s.at[it], x_r.at[it], xs)

        @pl.when(it == 0)
        def _():
            for s in range(STAGES, slots):
                convert(s)
            m_local.wait()
            for i, (d, other) in enumerate(xcs):
                cp = rcopy(m_part(other), m32.at[other], m_s.at[i], m_r.at[other], d)
                cp.wait_recv()
                cp.wait_send()
            for b in range(nxc):
                high, low = split2(m32[b])
                m2[b * own_rows : (b + 1) * own_rows, :] = high
                m2[rset + b * own_rows : rset + (b + 1) * own_rows, :] = low

        group_wait(xbuf.at[it, row], xbuf.at[it], x_s.at[it], x_r.at[it], xs)
        load = xbuf[it, 0] + xbuf[it, 1] + xbuf[it, 2] + xbuf[it, 3]
        left = stack3(load[:, :rset])
        answer = sum3(dot(jnp.concatenate([left, left], axis=1), m2[...], NN))
        y1buf[it, cy, :, 0:khalf] = answer[:, :khalf]
        y1buf[it, cy, :, khalf : khalf + width] = load[:, rset:]
        z1buf[it, cz] = answer[:, khalf:]
        group_start(y1buf.at[it, cy], y1buf.at[it], cy, y1_s.at[it], y1_r.at[it], ys)
        group_start(z1buf.at[it, cz], z1buf.at[it], cz, z1_s.at[it], z1_r.at[it], zs)

        force_copy.wait_recv()
        for b in range(blocks):
            put3(fsp, b // links, b % links, frecv[it, b])
        local_answers(it, 0, 3)

        group_wait(y1buf.at[it, cy], y1buf.at[it], y1_s.at[it], y1_r.at[it], ys)
        group_wait(z1buf.at[it, cz], z1buf.at[it], z1_s.at[it], z1_r.at[it], zs)
        z2buf[it, cz] = y1buf[it, 0] + y1buf[it, 1] + y1buf[it, 2] + y1buf[it, 3]
        y2buf[it, cy] = z1buf[it, 0] + z1buf[it, 1] + z1buf[it, 2] + z1buf[it, 3]
        group_start(z2buf.at[it, cz], z2buf.at[it], cz, z2_s.at[it], z2_r.at[it], zs)
        group_start(y2buf.at[it, cy], y2buf.at[it], cy, y2_s.at[it], y2_r.at[it], ys)
        local_answers(it, 3, slots)

        @pl.when(it == 0)
        def _():
            wait_maps(0, 1)
            wait_maps(1, 1)
            step = own_rows

            def rows(b, _):
                index = lax.broadcasted_iota(jnp.int32, (step, width), 0) + (me_xc * kset + b * step)
                index = index.astype(F32)
                at = pl.ds(pl.multiple_of(b * step, step), step)
                for q in range(nxc):
                    for h in range(2):
                        hit = jnp.where(index == maps_xc[q, h], 1.0, 0.0)
                        lo = (2 * (q % NX) + h) * width
                        pick[q // NX, at, lo : lo + width] = hit.astype(BF16)
                return 0

            lax.fori_loop(0, kset // step, rows, 0)

        group_wait(z2buf.at[it, cz], z2buf.at[it], z2_s.at[it], z2_r.at[it], zs)
        group_wait(y2buf.at[it, cy], y2buf.at[it], y2_s.at[it], y2_r.at[it], ys)
        answer_copy = rcopy(usend.at[it], urecv.at[it], u_s.at[it], u_r.at[it], nxt)
        answer_copy.start()
        first = z2buf[it, 0] + z2buf[it, 1] + z2buf[it, 2] + z2buf[it, 3]
        second = y2buf[it, 0] + y2buf[it, 1] + y2buf[it, 2] + y2buf[it, 3]
        scalars = first[:, khalf:]
        left = stack3(jnp.concatenate([first[:, :khalf], second], axis=1))
        found = sum3(dot(left, pick[1 - ck], NN))
        for q in range(NX):
            psend[it, q] = found[:, q * tiles : (q + 1) * tiles]
        core_copy = rcopy(psend.at[it], precv.at[it], p_s.at[it], p_r.at[it], cs[0][0])
        core_copy.start()
        found = sum3(dot(left, pick[ck], NN))
        core_copy.wait_recv()
        for q in range(NX):
            qsend[it, q] = found[:, q * tiles : (q + 1) * tiles] + precv[it, q]
        for i, (d, other) in enumerate(xs):
            rcopy(
                qsend.at[it, other], qrecv.at[it, row], q_s.at[it, i], q_r.at[it, row], d
            ).start()
        qrecv[it, row] = qsend[it, row]

        @pl.when(it > 0)
        def _():
            resid = update(scalars, False, it == 1)
            for b in range(blocks):
                zv[b] = weight_of(b) * resid[b]

        for i, (d, other) in enumerate(xs):
            cp = rcopy(
                qsend.at[it, other], qrecv.at[it, other], q_s.at[it, i], q_r.at[it, other], d
            )
            cp.wait_recv()
        picked = qrecv[it, 0] + qrecv[it, 1] + qrecv[it, 2] + qrecv[it, 3]

        def spread_back(part, s, factors):
            left = shift(part, -s * corners)
            left = jnp.where(lane < corners, left, shift(part, (1 - s) * corners))
            return sum3(dot(stack3(left[:, : 2 * corners]), factors[s], NN))

        for s in range(slots):
            found = spread_back(picked[:, :width], s, wo)
            other = spread_back(picked[:, width:], s, wp)
            for k in range(links):
                clink[s * links + k] = found[:, k * width : (k + 1) * width]
                cface[s * links + k] = other[:, k * width : (k + 1) * width]

        answer_copy.wait_recv()
        alpha, beta = sc[2], sc[3]
        for b in range(blocks):
            s, k = b // links, b % links
            facing = partner[k, s] * links + k
            index = jnp.broadcast_to(dof[s, k : k + 1, :], (loads, width))
            far = take(urecv[it, facing] + cface[facing], index)
            image = (ulink[b] + clink[b] - far) * mask[b]
            image = image + beta * tv[b]
            tv[b] = jnp.where(it == 0, 0.0, image)
            yv[b] = jnp.where(it == 0, image, yv[b] - alpha * image)
        return 0

    lax.fori_loop(0, ITERS, body, 0)

    pxbuf[row] = jnp.sum(scalar_terms(True), axis=0, keepdims=True)
    group_start(pxbuf.at[row], pxbuf, row, px_s, px_r, xs)
    sent(ITERS - 1)
    info_copy.wait_send()
    cpl_copy.wait_send()
    group_wait(pxbuf.at[row], pxbuf, px_s, px_r, xs)
    pcbuf[ck] = pxbuf[0] + pxbuf[1] + pxbuf[2] + pxbuf[3]
    group_start(pcbuf.at[ck], pcbuf, ck, pc_s, pc_r, cs)
    group_wait(pcbuf.at[ck], pcbuf, pc_s, pc_r, cs)
    pybuf[me_yz] = pcbuf[0] + pcbuf[1]
    group_start(pybuf.at[me_yz], pybuf, me_yz, py_s, py_r, yzs)
    group_wait(pybuf.at[me_yz], pybuf, py_s, py_r, yzs)
    group_sent(pxbuf.at[row], pxbuf, px_s, px_r, xs)
    group_sent(pcbuf.at[ck], pcbuf, pc_s, pc_r, cs)
    group_sent(pybuf.at[me_yz], pybuf, py_s, py_r, yzs)
    line = pybuf[0]
    for b in range(1, NYZ):
        line = line + pybuf[b]
    r_out[...] = update(jnp.broadcast_to(line, (loads, width)), True, None)


def local(
    flexibility,
    coupling,
    coarse_inverse,
    precon_weight,
    right_side,
    counts,
    partner,
    dof_index,
    corner_map,
):
    flex = flexibility[0, 0]
    cpl = coupling[0, 0]
    slots, iface = flex.shape[:2]
    half = iface // 2
    links, width = dof_index.shape[3:]
    loads = right_side.shape[3]
    own_rows, coarse = coarse_inverse.shape
    corners = corner_map.shape[-1]
    blocks = slots * links
    nxc = NX * NK
    kset, rset = coarse // nxc, own_rows * nxc
    rows3 = 3 * loads
    pair = 2 * width

    vec = (blocks, loads, width)
    per = (ITERS,)
    vm = pltpu.VMEM
    dma = pltpu.SemaphoreType.DMA
    scratch = [
        vm((STAGES, iface, iface), F32),
        vm((slots, iface, iface), BF16),
        vm((slots, iface, iface), BF16),
        vm((nxc, own_rows, kset), F32),
        vm((2 * rset, kset), BF16),
        vm(cpl.shape, F32),
        vm((slots, links, width), F32),
        vm((slots, loads, links, width), F32),
        vm((slots, links, width), jnp.int32),
        vm((slots, 1, corners), jnp.int32),
        vm((blocks, 8, width), jnp.int32),
        vm((slots, corners, half), F32),
        vm((slots + 1, 1, width), F32),
        vm((slots + 1, 1, width), F32),
        vm((NYZ, 2, 1, width), F32),
        vm((nxc, 2, 1, width), F32),
        vm((slots, 2 * corners, half), BF16),
        vm((slots, 2 * corners, half), BF16),
        vm((NYZ, rset, pair), BF16),
        vm((NK, kset, NX * pair), BF16),
        vm(per + (NYZ, loads, pair), F32),
        vm(per + (NK, loads, rset + width), F32),
        vm(per + (NX, loads, rset + width), F32),
        vm(per + (NY, loads, kset // 2 + width), F32),
        vm(per + (NZ, loads, kset // 2), F32),
        vm(per + (NY, loads, kset // 2), F32),
        vm(per + (NZ, loads, kset // 2 + width), F32),
        vm(per + (NX, loads, pair), F32),
        vm(per + (NX, loads, pair), F32),
        vm(per + (NX, loads, pair), F32),
        vm(per + (NX, loads, pair), F32),
        vm(per + vec, F32),
        vm(per + vec, F32),
        vm(per + vec, F32),
        vm(per + vec, F32),
        vm(vec, F32),
        vm((slots, rows3, half), BF16),
        vm((slots, rows3, half), BF16),
        vm((slots, rows3, half), BF16),
    ]
    scratch += [vm(vec, F32)] * 10
    scratch += [
        vm((4, loads, width), F32),
        vm((NX, 1, width), F32),
        vm((NK, 1, width), F32),
        vm((NYZ, 1, width), F32),
        dma((slots,)),
        dma((5,)),
        dma,
        dma,
        dma,
        dma,
        dma,
        dma((2, NYZ - 1)),
        dma((2, NYZ)),
        dma((2, nxc - 1)),
        dma((2, nxc)),
        dma((nxc - 1,)),
        dma((nxc,)),
    ]
    for size in (NYZ, NK, NX, NY, NZ, NY, NZ):
        scratch += [dma(per + (size - 1,)), dma(per + (size,))]
    scratch += [dma(per)] * 2 + [dma(per + (NX - 1,)), dma(per + (NX,))] + [dma(per)] * 4
    for size in (NX, NK, NYZ):
        scratch += [dma((size - 1,)), dma((size,))]
    in_vmem = pl.BlockSpec(memory_space=pltpu.VMEM)
    in_smem = pl.BlockSpec(memory_space=pltpu.SMEM)
    in_place = pl.BlockSpec(memory_space=pl.ANY)
    solved, resid = pl.pallas_call(
        kernel,
        name="feti",
        out_shape=[jax.ShapeDtypeStruct(vec, F32)] * 2,
        in_specs=[in_place] * 7 + [in_smem] * 2,
        out_specs=[in_vmem] * 2,
        scratch_shapes=scratch,
        compiler_params=pltpu.CompilerParams(
            collective_id=0, has_side_effects=True, vmem_limit_bytes=67043328
        ),
    )(
        flex,
        coarse_inverse,
        cpl,
        precon_weight[0, 0],
        right_side[0, 0],
        dof_index[0, 0],
        corner_map.reshape(slots, 1, corners),
        partner[0, 0],
        counts,
    )

    def outer(value):
        value = value.reshape(slots, links, loads, width).transpose(0, 2, 1, 3)
        return value[None, None]

    return outer(solved), outer(resid)


def solution(mesh):
    in_specs = (
        P("row", "col", None, None, None),
        P("row", "col", None, None, None),
        P(("row", "col"), None),
        P("row", "col", None, None, None),
        P("row", "col", None, None, None, None),
        P("row", "col"),
        P("row", "col", None, None),
        P("row", "col", None, None, None),
        P("row", "col", None, None),
    )
    out_specs = (P("row", "col", None, None, None, None), P("row", "col", None, None, None, None))
    return jax.shard_map(local, mesh=mesh, in_specs=in_specs, out_specs=out_specs, check_vma=False)
```

```python
import functools

import jax
import jax.numpy as jnp
from jax import lax
from jax.experimental import pallas as pl
from jax.experimental.pallas import tpu as pltpu
from jax.sharding import PartitionSpec as P

ITERS = 3
NX, NZ, NY, NK = 4, 4, 4, 2
NYZ = NZ * NY
STAGES = 3

MESH = pl.DeviceIdType.MESH
F32 = jnp.float32
BF16 = jnp.bfloat16
NT = (((1,), (1,)), ((), ()))
NN = (((1,), (0,)), ((), ()))


def split2(value):
    high = value.astype(BF16)
    low = (value - high.astype(F32)).astype(BF16)
    return high, low


def split3(value):
    high = value.astype(BF16)
    rest = value - high.astype(F32)
    middle = rest.astype(BF16)
    low = (rest - middle.astype(F32)).astype(BF16)
    return high, middle, low


def stack3(value):
    return jnp.concatenate(split3(value), axis=0)


def dot(left, right, dims):
    return lax.dot_general(left, right, dims, preferred_element_type=F32)


def sum3(value):
    rows = value.shape[0] // 3
    return value[2 * rows :] + value[rows : 2 * rows] + value[:rows]


def rcopy(src, dst, send, recv, device):
    return pltpu.make_async_remote_copy(
        src_ref=src,
        dst_ref=dst,
        send_sem=send,
        recv_sem=recv,
        device_id=device,
        device_id_type=MESH,
    )


def group_start(src, buf, mine, send, recv, peers):
    for device, _ in peers:
        rcopy(src, buf.at[mine], send, recv, device).start()


def group_copy(buf, send, recv, peers):
    part = buf.at[pl.ds(0, len(peers))]
    return rcopy(part, part, send, recv, peers[0][0])


def group_wait(buf, send, recv, peers):
    group_copy(buf, send, recv, peers).wait_recv()


def group_sent(buf, send, recv, peers):
    group_copy(buf, send, recv, peers).wait_send()


def kernel(
    flex, cinv, cpl_in, weight_in, rhs_in, dof_in, map_in, partner, counts,
    x_out, r_out,
    stage, flex_hi, flex_lo, m32, m2, cpl, weight, rhs, dof, rowmap, dof_inv, cplp, info, infop,
    maps_yz, maps_xc, wo, wp, scatter, pick, tbuf, cbuf, xbuf, y1buf, z1buf, y2buf, z2buf,
    psend, precv, qsend, qrecv, gsend, frecv, usend, urecv,
    vblk, vsp, gsp, fsp, yv, tv, dv, sv, zv, rv, mask, ulink, clink, cface, sc,
    pxbuf, pcbuf, pybuf,
    flex_sem, load_sem, mloc_sem, info_s, info_r, cpl_s, cpl_r, mapa_s, mapa_r, mapb_s, mapb_r,
    m_s, m_r, t_s, t_r, c_s, c_r, x_s, x_r, y1_s, y1_r, z1_s, z1_r, y2_s, y2_r, z2_s, z2_r,
    p_s, p_r, q_s, q_r, f_s, f_r, u_s, u_r, px_s, px_r, pc_s, pc_r, py_s, py_r,
):
    slots, iface = flex.shape[:2]
    half = iface // 2
    links, width = dof.shape[1:]
    loads = rhs.shape[1]
    corners = cpl.shape[1]
    own_rows, coarse = cinv.shape
    nxc = NX * NK
    kset = coarse // nxc
    rset = own_rows * nxc
    khalf = kset // 2
    blocks = slots * links
    tiles = 2 * width

    row, col = lax.axis_index("row"), lax.axis_index("col")
    cz = lax.div(col, NY * NK)
    cy = lax.rem(lax.div(col, NK), NY)
    ck = lax.rem(col, NK)
    cols = NZ * NY * NK
    me_yz = cz * NY + cy
    me_xc = ck * NX + row
    prev = (row, lax.rem(col + cols - 1, cols))
    nxt = (row, lax.rem(col + 1, cols))

    def device(x, z, y, k):
        return (x, (z * NY + y) * NK + k)

    def turn(value, by, size):
        return lax.rem(value + by, size)

    xs = [(device(turn(row, i, NX), cz, cy, ck), turn(row, i, NX)) for i in (2, 1, 3)]
    ys = [(device(row, cz, turn(cy, i, NY), ck), turn(cy, i, NY)) for i in (2, 1, 3)]
    zs = [(device(row, turn(cz, i, NZ), cy, ck), turn(cz, i, NZ)) for i in (2, 1, 3)]
    cs = [(device(row, cz, cy, 1 - ck), 1 - ck)]
    order = sorted(
        [(i, j) for i in range(NZ) for j in range(NY) if (i, j) != (0, 0)],
        key=lambda ij: -(min(ij[0], NZ - ij[0]) + min(ij[1], NY - ij[1])),
    )
    yzs = [
        (device(row, turn(cz, i, NZ), turn(cy, j, NY), ck), turn(cz, i, NZ) * NY + turn(cy, j, NY))
        for i, j in order
    ]
    xcs = [
        (device(turn(row, i, NX), cz, cy, turn(ck, j, NK)), turn(ck, j, NK) * NX + turn(row, i, NX))
        for i in (2, 1, 3, 0)
        for j in range(NK)
        if (i, j) != (0, 0)
    ]

    barrier = pltpu.get_barrier_semaphore()
    everyone = [d for d, _ in yzs] + [d for d, _ in xcs] + [prev, nxt]
    for d in everyone:
        pl.semaphore_signal(barrier, inc=1, device_id=d, device_id_type=MESH)

    def flex_copy(s):
        return pltpu.make_async_copy(flex.at[s], stage.at[s % STAGES], flex_sem.at[s])

    def m_part(other):
        return cinv.at[:, pl.ds(pl.multiple_of(other * kset, 128), kset)]

    loaded = [
        pltpu.make_async_copy(src, dst, load_sem.at[i])
        for i, (src, dst) in enumerate(
            [(map_in, rowmap), (dof_in, dof), (rhs_in, rhs), (weight_in, weight), (cpl_in, cpl)]
        )
    ]
    for copy in loaded:
        copy.start()
    m_local = pltpu.make_async_copy(m_part(me_xc), m32.at[me_xc], mloc_sem)
    m_local.start()
    for s in range(STAGES):
        flex_copy(s).start()

    for s in range(slots):
        live = jnp.where(s < counts[0, 0], 1.0, 0.0).astype(F32)
        info[s] = jnp.broadcast_to(live, (1, width))
    loaded[0].wait()
    lane8 = lax.broadcasted_iota(jnp.int32, (8, width), 1)
    found = jnp.full((8, width), -1, jnp.int32)
    for s in range(slots):
        ids = jnp.broadcast_to(rowmap[s], (8, corners))
        ids = jnp.concatenate([ids, jnp.zeros((8, width - corners), jnp.int32)], axis=1)
        if s:
            ids = pltpu.roll(ids, s * corners, 1)
        inside = jnp.logical_and(lane8 >= s * corners, lane8 < (s + 1) * corners)
        found = jnp.where(inside, ids, found)
    info[slots] = found[0:1].astype(F32)

    pl.semaphore_wait(barrier, len(everyone))

    info_copy = rcopy(info, infop, info_s, info_r, nxt)
    info_copy.start()
    loaded[4].wait()
    cpl_copy = rcopy(cpl.at[:, :, half:], cplp, cpl_s, cpl_r, nxt)
    cpl_copy.start()
    for d, other in xcs:
        rcopy(m_part(other), m32.at[me_xc], m_s, m_r, d).start()
    map_groups = [(maps_yz, me_yz, mapa_s, mapa_r, yzs), (maps_xc, me_xc, mapb_s, mapb_r, xcs)]

    def send_maps(src, h):
        for buf, mine, send, recv, peers in map_groups:
            for d, _ in peers:
                rcopy(src, buf.at[mine, h], send, recv, d).start()
            buf[mine, h] = src[...]

    def wait_maps(group):
        buf, _, send, recv, peers = map_groups[group]
        group_wait(buf, send, recv, peers)
        group_sent(buf, send, recv, peers)

    send_maps(info.at[slots], 0)

    def build_coupling(source, out):
        for s in range(slots):
            value = source[s, :, 0:half]
            high = value.astype(BF16).astype(F32)
            out[s] = jnp.concatenate([high, value - high], axis=0).astype(BF16)

    build_coupling(cpl, wo)
    tv[...] = jnp.zeros_like(tv)
    dv[...] = jnp.zeros_like(dv)
    sv[...] = jnp.zeros_like(sv)
    x_out[...] = jnp.zeros_like(x_out)
    sc[0] = jnp.ones_like(sc[0])
    sc[1] = jnp.zeros_like(sc[1])
    sc[2] = jnp.zeros_like(sc[2])
    sc[3] = jnp.zeros_like(sc[3])

    loaded[1].wait()
    sub = lax.broadcasted_iota(jnp.int32, (width, width), 0)
    numbers = lane8.astype(F32).astype(BF16)
    for b in range(blocks):
        ids = dof[b // links, b % links : b % links + 1, :]
        hit = jnp.where(sub == ids, 1.0, 0.0).astype(BF16)
        dof_inv[b] = dot(numbers, hit, NT).astype(jnp.int32)

    inverse = {}
    for k in range(links):
        for p in range(slots):
            at = jnp.int32(0)
            for j in range(1, slots):
                at = jnp.where(partner[k, j] == p, j, at)
            inverse[k, p] = at

    loaded[2].wait()
    loaded[3].wait()
    info_copy.wait_recv()
    send_maps(infop.at[slots], 1)

    def weight_of(b):
        return weight[b // links, b % links : b % links + 1, :]

    for b in range(blocks):
        s, k = b // links, b % links
        live = info[s] * infop[partner[k, s]]
        live = jnp.broadcast_to(live, (loads, width))
        mask[b] = live
        resid = live * rhs[s, :, k, :]
        rv[b] = resid
        yv[b] = resid
        zv[b] = weight_of(b) * resid

    lane = lax.broadcasted_iota(jnp.int32, (loads, width), 1)
    load_id = lax.broadcasted_iota(jnp.int32, (loads, width), 0)

    def total(first, second):
        return jnp.sum(jnp.sum(first * second, axis=0), axis=1, keepdims=True)

    def scalar_terms(packed):
        z, y = zv[...], yv[...]
        found = [total(rv[...], z), total(z, y), total(z, sv[...]), total(dv[...], y)]
        tile = jnp.zeros((loads, width), F32)
        for i, value in enumerate(found):
            at = lane == (4 * load_id + i if packed else i)
            tile = jnp.where(at, value, tile)
        return tile

    def update(tile, packed, first):
        rz, zy, zs_, dy = [
            jnp.broadcast_to(
                jnp.sum(
                    jnp.where(lane == (4 * load_id + i if packed else i), tile, 0.0),
                    axis=1,
                    keepdims=True,
                ),
                tile.shape,
            )
            for i in range(4)
        ]
        beta = rz / sc[0]
        if first is not None:
            beta = jnp.where(first, 0.0, beta)
        curv = zy + beta * (zs_ + dy) + beta * beta * sc[1]
        alpha = rz / curv
        sc[0], sc[1], sc[2], sc[3] = rz, curv, alpha, beta
        direction = zv[...] + beta[None] * dv[...]
        image = yv[...] + beta[None] * sv[...]
        dv[...] = direction
        sv[...] = image
        x_out[...] = x_out[...] + alpha[None] * direction
        resid = rv[...] - alpha[None] * image
        rv[...] = resid
        return resid

    def put3(ref, s, k, value):
        for i, part in enumerate(split3(value)):
            ref[s, i * loads : (i + 1) * loads, k * width : (k + 1) * width] = part

    def take(value, index):
        return jnp.take_along_axis(value, index, axis=1, mode="promise_in_bounds")

    def convert(s):
        flex_copy(s).wait()
        here = s % STAGES

        def chunk(i, _):
            at = pl.ds(pl.multiple_of(i * 64, 64), 64)
            high, low = split2(stage[here, at, :])
            flex_hi[s, at, :] = high
            flex_lo[s, at, :] = low
            return 0

        lax.fori_loop(0, iface // 64, chunk, 0)
        if s + STAGES < slots:
            flex_copy(s + STAGES).start()

    def local_answers(it, first, last):
        def one(s, _):
            left = jnp.concatenate([vsp[s], fsp[s]], axis=1)
            for n in range(iface // 256):
                at = slice(n * 256, (n + 1) * 256)
                out = dot(left, flex_hi[s, :, at], NN) + dot(left, flex_lo[s, :, at], NN)
                out = sum3(out)
                for h in range(2):
                    piece = out[:, h * width : (h + 1) * width]
                    k = 2 * n + h
                    if k < links:
                        ulink[s * links + k] = piece
                    else:
                        usend[it, s * links + k - links] = piece
            return 0

        lax.fori_loop(first, last, one, 0)

    def within(s):
        return jnp.logical_and(lane >= s * corners, lane < (s + 1) * corners)

    def shift(value, by):
        by = by % width
        return pltpu.roll(value, by, 1) if by else value

    def sent(it):
        group_sent(tbuf.at[it], t_s.at[it], t_r.at[it, 0], yzs)
        group_sent(cbuf.at[it], c_s.at[it], c_r.at[it], cs)
        group_sent(xbuf.at[it], x_s.at[it], x_r.at[it], xs)
        group_sent(y1buf.at[it], y1_s.at[it], y1_r.at[it], ys)
        group_sent(z1buf.at[it], z1_s.at[it], z1_r.at[it], zs)
        group_sent(z2buf.at[it], z2_s.at[it], z2_r.at[it], zs)
        group_sent(y2buf.at[it], y2_s.at[it], y2_r.at[it], ys)
        rcopy(psend.at[it], precv.at[it], p_s.at[it], p_r.at[it], cs[0][0]).wait_send()
        group_sent(qrecv.at[it], q_s.at[it], q_r.at[it], xs)
        rcopy(gsend.at[it], frecv.at[it], f_s.at[it], f_r.at[it], prev).wait_send()
        rcopy(usend.at[it], urecv.at[it], u_s.at[it], u_r.at[it], nxt).wait_send()

    def body(it, _):
        for b in range(blocks):
            value = weight_of(b) * yv[b]
            vblk[b] = value
            put3(vsp, b // links, b % links, value)
        for b in range(blocks):
            p, k = b // links, b % links
            from_block = inverse[k, p] * links + k
            index = jnp.concatenate([dof_inv[from_block]] * (loads // 8), axis=0)
            value = -take(vblk[from_block], index)
            gsend[it, b] = value
            put3(gsp, p, k, value)

        def terms(blocks3, factors):
            found = jnp.zeros((loads, width), F32)
            for s in range(slots):
                part = sum3(dot(blocks3[s], factors[s], NT))
                rest = jnp.zeros((loads, width - 2 * corners), F32)
                part = jnp.concatenate([part, rest], axis=1)
                part = shift(part, s * corners) + shift(part, (s - 1) * corners)
                found = jnp.where(within(s), part, found)
            return found

        tbuf[it, me_yz, :, 0:width] = terms(vsp, wo)

        @pl.when(it == 0)
        def _():
            cpl_copy.wait_recv()
            build_coupling(cplp, wp)

        tbuf[it, me_yz, :, width:tiles] = terms(gsp, wp)
        for d, _ in yzs:
            rcopy(
                tbuf.at[it, me_yz], tbuf.at[it, me_yz], t_s.at[it], t_r.at[it, me_yz], d
            ).start()
        tile = scalar_terms(False)

        @pl.when(it > 0)
        def _():
            sent(it - 1)

        @pl.when(it == 0)
        def _():
            wait_maps(0)

            def rows(p, _):
                base = (lax.rem(p, NX) * cols + me_yz * NK + lax.div(p, NX)) * own_rows
                index = lax.broadcasted_iota(jnp.int32, (own_rows, width), 0) + base
                index = index.astype(F32)
                at = pl.ds(pl.multiple_of(p * own_rows, own_rows), own_rows)
                for q in range(NYZ):
                    for h in range(2):
                        hit = jnp.where(index == maps_yz[q, h], 1.0, 0.0)
                        scatter[q, at, h * width : (h + 1) * width] = hit.astype(BF16)
                return 0

            lax.fori_loop(0, nxc, rows, 0)
            for s in range(STAGES):
                convert(s)

        def spread(q):
            return dot(stack3(tbuf[it, q]), scatter[q], NT)

        found = spread(me_yz)
        for d, q in reversed(yzs):
            rcopy(tbuf.at[it, me_yz], tbuf.at[it, q], t_s.at[it], t_r.at[it, q], d).wait_recv()
            found = found + spread(q)
        cbuf[it, ck, :, 0:rset] = sum3(found)
        cbuf[it, ck, :, rset : rset + width] = tile
        group_start(cbuf.at[it, ck], cbuf.at[it], ck, c_s.at[it], c_r.at[it], cs)
        force_copy = rcopy(gsend.at[it], frecv.at[it], f_s.at[it], f_r.at[it], prev)
        force_copy.start()
        group_wait(cbuf.at[it], c_s.at[it], c_r.at[it], cs)
        xbuf[it, row] = cbuf[it, 0] + cbuf[it, 1]
        group_start(xbuf.at[it, row], xbuf.at[it], row, x_s.at[it], x_r.at[it], xs)

        @pl.when(it == 0)
        def _():
            for s in range(STAGES, slots):
                convert(s)
            m_local.wait()
            group_wait(m32, m_s, m_r, xcs)
            group_sent(m32, m_s, m_r, xcs)
            for b in range(nxc):
                high, low = split2(m32[b])
                m2[b * own_rows : (b + 1) * own_rows, :] = high
                m2[rset + b * own_rows : rset + (b + 1) * own_rows, :] = low

        group_wait(xbuf.at[it], x_s.at[it], x_r.at[it], xs)
        load = xbuf[it, 0] + xbuf[it, 1] + xbuf[it, 2] + xbuf[it, 3]
        left = stack3(load[:, :rset])
        answer = sum3(dot(jnp.concatenate([left, left], axis=1), m2[...], NN))
        y1buf[it, cy, :, 0:khalf] = answer[:, :khalf]
        y1buf[it, cy, :, khalf : khalf + width] = load[:, rset:]
        z1buf[it, cz] = answer[:, khalf:]
        group_start(y1buf.at[it, cy], y1buf.at[it], cy, y1_s.at[it], y1_r.at[it], ys)
        group_start(z1buf.at[it, cz], z1buf.at[it], cz, z1_s.at[it], z1_r.at[it], zs)

        force_copy.wait_recv()
        for b in range(blocks):
            put3(fsp, b // links, b % links, frecv[it, b])
        local_answers(it, 0, 3)

        group_wait(y1buf.at[it], y1_s.at[it], y1_r.at[it], ys)
        group_wait(z1buf.at[it], z1_s.at[it], z1_r.at[it], zs)
        z2buf[it, cz] = y1buf[it, 0] + y1buf[it, 1] + y1buf[it, 2] + y1buf[it, 3]
        y2buf[it, cy] = z1buf[it, 0] + z1buf[it, 1] + z1buf[it, 2] + z1buf[it, 3]
        group_start(z2buf.at[it, cz], z2buf.at[it], cz, z2_s.at[it], z2_r.at[it], zs)
        group_start(y2buf.at[it, cy], y2buf.at[it], cy, y2_s.at[it], y2_r.at[it], ys)
        local_answers(it, 3, slots)

        @pl.when(it == 0)
        def _():
            wait_maps(1)
            step = own_rows

            def rows(b, _):
                index = lax.broadcasted_iota(jnp.int32, (step, width), 0) + (me_xc * kset + b * step)
                index = index.astype(F32)
                at = pl.ds(pl.multiple_of(b * step, step), step)
                for q in range(nxc):
                    for h in range(2):
                        hit = jnp.where(index == maps_xc[q, h], 1.0, 0.0)
                        lo = (2 * (q % NX) + h) * width
                        pick[q // NX, at, lo : lo + width] = hit.astype(BF16)
                return 0

            lax.fori_loop(0, kset // step, rows, 0)

        group_wait(z2buf.at[it], z2_s.at[it], z2_r.at[it], zs)
        group_wait(y2buf.at[it], y2_s.at[it], y2_r.at[it], ys)
        answer_copy = rcopy(usend.at[it], urecv.at[it], u_s.at[it], u_r.at[it], nxt)
        answer_copy.start()
        first = z2buf[it, 0] + z2buf[it, 1] + z2buf[it, 2] + z2buf[it, 3]
        second = y2buf[it, 0] + y2buf[it, 1] + y2buf[it, 2] + y2buf[it, 3]
        scalars = first[:, khalf:]
        left = stack3(jnp.concatenate([first[:, :khalf], second], axis=1))
        found = sum3(dot(left, pick[1 - ck], NN))
        for q in range(NX):
            psend[it, q] = found[:, q * tiles : (q + 1) * tiles]
        core_copy = rcopy(psend.at[it], precv.at[it], p_s.at[it], p_r.at[it], cs[0][0])
        core_copy.start()
        found = sum3(dot(left, pick[ck], NN))
        core_copy.wait_recv()
        for q in range(NX):
            qsend[it, q] = found[:, q * tiles : (q + 1) * tiles] + precv[it, q]
        for d, other in xs:
            rcopy(qsend.at[it, other], qrecv.at[it, row], q_s.at[it], q_r.at[it], d).start()
        qrecv[it, row] = qsend[it, row]

        @pl.when(it > 0)
        def _():
            resid = update(scalars, False, it == 1)
            for b in range(blocks):
                zv[b] = weight_of(b) * resid[b]

        group_wait(qrecv.at[it], q_s.at[it], q_r.at[it], xs)
        picked = qrecv[it, 0] + qrecv[it, 1] + qrecv[it, 2] + qrecv[it, 3]

        def spread_back(part, s, factors):
            left = shift(part, -s * corners)
            left = jnp.where(lane < corners, left, shift(part, (1 - s) * corners))
            return sum3(dot(stack3(left[:, : 2 * corners]), factors[s], NN))

        for s in range(slots):
            found = spread_back(picked[:, :width], s, wo)
            other = spread_back(picked[:, width:], s, wp)
            for k in range(links):
                clink[s * links + k] = found[:, k * width : (k + 1) * width]
                cface[s * links + k] = other[:, k * width : (k + 1) * width]

        answer_copy.wait_recv()
        alpha, beta = sc[2], sc[3]
        for b in range(blocks):
            s, k = b // links, b % links
            facing = partner[k, s] * links + k
            index = jnp.broadcast_to(dof[s, k : k + 1, :], (loads, width))
            far = take(urecv[it, facing] + cface[facing], index)
            image = (ulink[b] + clink[b] - far) * mask[b]
            image = image + beta * tv[b]
            tv[b] = jnp.where(it == 0, 0.0, image)
            yv[b] = jnp.where(it == 0, image, yv[b] - alpha * image)
        return 0

    lax.fori_loop(0, ITERS, body, 0)

    pxbuf[row] = jnp.sum(scalar_terms(True), axis=0, keepdims=True)
    group_start(pxbuf.at[row], pxbuf, row, px_s, px_r, xs)
    sent(ITERS - 1)
    info_copy.wait_send()
    cpl_copy.wait_send()
    group_wait(pxbuf, px_s, px_r, xs)
    pcbuf[ck] = pxbuf[0] + pxbuf[1] + pxbuf[2] + pxbuf[3]
    group_start(pcbuf.at[ck], pcbuf, ck, pc_s, pc_r, cs)
    group_wait(pcbuf, pc_s, pc_r, cs)
    pybuf[me_yz] = pcbuf[0] + pcbuf[1]
    group_start(pybuf.at[me_yz], pybuf, me_yz, py_s, py_r, yzs)
    group_wait(pybuf, py_s, py_r, yzs)
    group_sent(pxbuf, px_s, px_r, xs)
    group_sent(pcbuf, pc_s, pc_r, cs)
    group_sent(pybuf, py_s, py_r, yzs)
    line = pybuf[0]
    for b in range(1, NYZ):
        line = line + pybuf[b]
    r_out[...] = update(jnp.broadcast_to(line, (loads, width)), True, None)


def local(
    flexibility,
    coupling,
    coarse_inverse,
    precon_weight,
    right_side,
    counts,
    partner,
    dof_index,
    corner_map,
):
    flex = flexibility[0, 0]
    cpl = coupling[0, 0]
    slots, iface = flex.shape[:2]
    half = iface // 2
    links, width = dof_index.shape[3:]
    loads = right_side.shape[3]
    own_rows, coarse = coarse_inverse.shape
    corners = corner_map.shape[-1]
    blocks = slots * links
    nxc = NX * NK
    kset, rset = coarse // nxc, own_rows * nxc
    rows3 = 3 * loads
    pair = 2 * width

    vec = (blocks, loads, width)
    per = (ITERS,)
    vm = pltpu.VMEM
    dma = pltpu.SemaphoreType.DMA
    scratch = [
        vm((STAGES, iface, iface), F32),
        vm((slots, iface, iface), BF16),
        vm((slots, iface, iface), BF16),
        vm((nxc, own_rows, kset), F32),
        vm((2 * rset, kset), BF16),
        vm(cpl.shape, F32),
        vm((slots, links, width), F32),
        vm((slots, loads, links, width), F32),
        vm((slots, links, width), jnp.int32),
        vm((slots, 1, corners), jnp.int32),
        vm((blocks, 8, width), jnp.int32),
        vm((slots, corners, half), F32),
        vm((slots + 1, 1, width), F32),
        vm((slots + 1, 1, width), F32),
        vm((NYZ, 2, 1, width), F32),
        vm((nxc, 2, 1, width), F32),
        vm((slots, 2 * corners, half), BF16),
        vm((slots, 2 * corners, half), BF16),
        vm((NYZ, rset, pair), BF16),
        vm((NK, kset, NX * pair), BF16),
        vm(per + (NYZ, loads, pair), F32),
        vm(per + (NK, loads, rset + width), F32),
        vm(per + (NX, loads, rset + width), F32),
        vm(per + (NY, loads, kset // 2 + width), F32),
        vm(per + (NZ, loads, kset // 2), F32),
        vm(per + (NY, loads, kset // 2), F32),
        vm(per + (NZ, loads, kset // 2 + width), F32),
        vm(per + (NX, loads, pair), F32),
        vm(per + (NX, loads, pair), F32),
        vm(per + (NX, loads, pair), F32),
        vm(per + (NX, loads, pair), F32),
        vm(per + vec, F32),
        vm(per + vec, F32),
        vm(per + vec, F32),
        vm(per + vec, F32),
        vm(vec, F32),
        vm((slots, rows3, half), BF16),
        vm((slots, rows3, half), BF16),
        vm((slots, rows3, half), BF16),
    ]
    scratch += [vm(vec, F32)] * 10
    scratch += [
        vm((4, loads, width), F32),
        vm((NX, 1, width), F32),
        vm((NK, 1, width), F32),
        vm((NYZ, 1, width), F32),
        dma((slots,)),
        dma((5,)),
        dma,
        dma,
        dma,
        dma,
        dma,
        dma,
        dma,
        dma,
        dma,
        dma,
        dma,
        dma(per),
        dma(per + (NYZ,)),
    ]
    scratch += [dma(per)] * 20 + [dma] * 6
    in_vmem = pl.BlockSpec(memory_space=pltpu.VMEM)
    in_smem = pl.BlockSpec(memory_space=pltpu.SMEM)
    in_place = pl.BlockSpec(memory_space=pl.ANY)
    solved, resid = pl.pallas_call(
        kernel,
        name="feti",
        out_shape=[jax.ShapeDtypeStruct(vec, F32)] * 2,
        in_specs=[in_place] * 7 + [in_smem] * 2,
        out_specs=[in_vmem] * 2,
        scratch_shapes=scratch,
        compiler_params=pltpu.CompilerParams(
            collective_id=0, has_side_effects=True, vmem_limit_bytes=67043328
        ),
    )(
        flex,
        coarse_inverse,
        cpl,
        precon_weight[0, 0],
        right_side[0, 0],
        dof_index[0, 0],
        corner_map.reshape(slots, 1, corners),
        partner[0, 0],
        counts,
    )

    def outer(value):
        value = value.reshape(slots, links, loads, width).transpose(0, 2, 1, 3)
        return value[None, None]

    return outer(solved), outer(resid)


def solution(mesh):
    in_specs = (
        P("row", "col", None, None, None),
        P("row", "col", None, None, None),
        P(("row", "col"), None),
        P("row", "col", None, None, None),
        P("row", "col", None, None, None, None),
        P("row", "col"),
        P("row", "col", None, None),
        P("row", "col", None, None, None),
        P("row", "col", None, None),
    )
    out_specs = (P("row", "col", None, None, None, None), P("row", "col", None, None, None, None))
    return jax.shard_map(local, mesh=mesh, in_specs=in_specs, out_specs=out_specs, check_vma=False)
```

```python
import functools

import jax
import jax.numpy as jnp
from jax import lax
from jax.experimental import pallas as pl
from jax.experimental.pallas import tpu as pltpu
from jax.sharding import PartitionSpec as P

ITERS = 3
NX, NZ, NY, NK = 4, 4, 4, 2
NYZ = NZ * NY
STAGES = 3

MESH = pl.DeviceIdType.MESH
F32 = jnp.float32
BF16 = jnp.bfloat16
NT = (((1,), (1,)), ((), ()))
NN = (((1,), (0,)), ((), ()))


def split2(value):
    high = value.astype(BF16)
    low = (value - high.astype(F32)).astype(BF16)
    return high, low


def split3(value):
    high = value.astype(BF16)
    rest = value - high.astype(F32)
    middle = rest.astype(BF16)
    low = (rest - middle.astype(F32)).astype(BF16)
    return high, middle, low


def stack3(value):
    return jnp.concatenate(split3(value), axis=0)


def dot(left, right, dims):
    return lax.dot_general(left, right, dims, preferred_element_type=F32)


def sum3(value):
    rows = value.shape[0] // 3
    return value[2 * rows :] + value[rows : 2 * rows] + value[:rows]


def rcopy(src, dst, send, recv, device):
    return pltpu.make_async_remote_copy(
        src_ref=src,
        dst_ref=dst,
        send_sem=send,
        recv_sem=recv,
        device_id=device,
        device_id_type=MESH,
    )


def group_start(src, buf, mine, send, recv, peers):
    for device, _ in peers:
        rcopy(src, buf.at[mine], send, recv, device).start()


def group_copy(buf, send, recv, peers):
    part = buf.at[pl.ds(0, len(peers))]
    return rcopy(part, part, send, recv, peers[0][0])


def group_wait(buf, send, recv, peers):
    group_copy(buf, send, recv, peers).wait_recv()


def group_sent(buf, send, recv, peers):
    group_copy(buf, send, recv, peers).wait_send()


def kernel(
    flex, cinv, cpl_in, weight_in, rhs_in, dof_in, map_in, partner, counts,
    x_out, r_out,
    stage, flex_hi, flex_lo, m32, m2, cpl, weight, rhs, dof, rowmap, dof_inv, cplp, info, infop,
    maps_yz, maps_xc, wo, wp, scatter, pick, tbuf, cbuf, xbuf, y1buf, z1buf, y2buf, z2buf,
    psend, precv, qsend, qrecv, gsend, frecv, usend, urecv,
    vblk, vsp, gsp, fsp, yv, tv, dv, sv, zv, rv, mask, ulink, clink, cface, sc,
    pybuf,
    flex_sem, load_sem, mloc_sem, info_s, info_r, cpl_s, cpl_r, mapa_s, mapa_r, mapb_s, mapb_r,
    m_s, m_r, t_s, t_r, c_s, c_r, x_s, x_r, y1_s, y1_r, z1_s, z1_r, y2_s, y2_r, z2_s, z2_r,
    p_s, p_r, q_s, q_r, f_s, f_r, u_s, u_r, py_s, py_r,
):
    slots, iface = flex.shape[:2]
    half = iface // 2
    links, width = dof.shape[1:]
    loads = rhs.shape[1]
    corners = cpl.shape[1]
    own_rows, coarse = cinv.shape
    nxc = NX * NK
    kset = coarse // nxc
    rset = own_rows * nxc
    khalf = kset // 2
    blocks = slots * links
    tiles = 2 * width

    row, col = lax.axis_index("row"), lax.axis_index("col")
    cz = lax.div(col, NY * NK)
    cy = lax.rem(lax.div(col, NK), NY)
    ck = lax.rem(col, NK)
    cols = NZ * NY * NK
    me_yz = cz * NY + cy
    me_xc = ck * NX + row
    prev = (row, lax.rem(col + cols - 1, cols))
    nxt = (row, lax.rem(col + 1, cols))

    def device(x, z, y, k):
        return (x, (z * NY + y) * NK + k)

    def turn(value, by, size):
        return lax.rem(value + by, size)

    xs = [(device(turn(row, i, NX), cz, cy, ck), turn(row, i, NX)) for i in (2, 1, 3)]
    ys = [(device(row, cz, turn(cy, i, NY), ck), turn(cy, i, NY)) for i in (2, 1, 3)]
    zs = [(device(row, turn(cz, i, NZ), cy, ck), turn(cz, i, NZ)) for i in (2, 1, 3)]
    cs = [(device(row, cz, cy, 1 - ck), 1 - ck)]
    order = sorted(
        [(i, j) for i in range(NZ) for j in range(NY) if (i, j) != (0, 0)],
        key=lambda ij: -(min(ij[0], NZ - ij[0]) + min(ij[1], NY - ij[1])),
    )
    yzs = [
        (device(row, turn(cz, i, NZ), turn(cy, j, NY), ck), turn(cz, i, NZ) * NY + turn(cy, j, NY))
        for i, j in order
    ]
    xcs = [
        (device(turn(row, i, NX), cz, cy, turn(ck, j, NK)), turn(ck, j, NK) * NX + turn(row, i, NX))
        for i in (2, 1, 3, 0)
        for j in range(NK)
        if (i, j) != (0, 0)
    ]

    barrier = pltpu.get_barrier_semaphore()
    everyone = [d for d, _ in yzs] + [d for d, _ in xcs] + [prev, nxt]
    for d in everyone:
        pl.semaphore_signal(barrier, inc=1, device_id=d, device_id_type=MESH)

    def flex_copy(s):
        return pltpu.make_async_copy(flex.at[s], stage.at[s % STAGES], flex_sem.at[s])

    def m_part(other):
        return cinv.at[:, pl.ds(pl.multiple_of(other * kset, 128), kset)]

    loaded = [
        pltpu.make_async_copy(src, dst, load_sem.at[i])
        for i, (src, dst) in enumerate(
            [(map_in, rowmap), (dof_in, dof), (rhs_in, rhs), (weight_in, weight), (cpl_in, cpl)]
        )
    ]
    for copy in loaded:
        copy.start()
    m_local = pltpu.make_async_copy(m_part(me_xc), m32.at[me_xc], mloc_sem)
    m_local.start()
    for s in range(STAGES):
        flex_copy(s).start()

    for s in range(slots):
        live = jnp.where(s < counts[0, 0], 1.0, 0.0).astype(F32)
        info[s] = jnp.broadcast_to(live, (1, width))
    loaded[0].wait()
    lane8 = lax.broadcasted_iota(jnp.int32, (8, width), 1)
    found = jnp.full((8, width), -1, jnp.int32)
    for s in range(slots):
        ids = jnp.broadcast_to(rowmap[s], (8, corners))
        ids = jnp.concatenate([ids, jnp.zeros((8, width - corners), jnp.int32)], axis=1)
        if s:
            ids = pltpu.roll(ids, s * corners, 1)
        inside = jnp.logical_and(lane8 >= s * corners, lane8 < (s + 1) * corners)
        found = jnp.where(inside, ids, found)
    info[slots] = found[0:1].astype(F32)

    pl.semaphore_wait(barrier, len(everyone))

    info_copy = rcopy(info, infop, info_s, info_r, nxt)
    info_copy.start()
    loaded[4].wait()
    cpl_copy = rcopy(cpl.at[:, :, half:], cplp, cpl_s, cpl_r, nxt)
    cpl_copy.start()
    for d, other in xcs:
        rcopy(m_part(other), m32.at[me_xc], m_s, m_r, d).start()
    map_groups = [(maps_yz, me_yz, mapa_s, mapa_r, yzs), (maps_xc, me_xc, mapb_s, mapb_r, xcs)]

    def send_maps(src, h):
        for buf, mine, send, recv, peers in map_groups:
            for d, _ in peers:
                rcopy(src, buf.at[mine, h], send, recv, d).start()
            buf[mine, h] = src[...]

    def wait_maps(group):
        buf, _, send, recv, peers = map_groups[group]
        group_wait(buf, send, recv, peers)
        group_sent(buf, send, recv, peers)

    send_maps(info.at[slots], 0)

    def build_coupling(source, out):
        for s in range(slots):
            value = source[s, :, 0:half]
            high = value.astype(BF16).astype(F32)
            out[s] = jnp.concatenate([high, value - high], axis=0).astype(BF16)

    build_coupling(cpl, wo)
    tv[...] = jnp.zeros_like(tv)
    dv[...] = jnp.zeros_like(dv)
    sv[...] = jnp.zeros_like(sv)
    x_out[...] = jnp.zeros_like(x_out)
    sc[0] = jnp.ones_like(sc[0])
    sc[1] = jnp.zeros_like(sc[1])
    sc[2] = jnp.zeros_like(sc[2])
    sc[3] = jnp.zeros_like(sc[3])

    loaded[1].wait()
    sub = lax.broadcasted_iota(jnp.int32, (width, width), 0)
    numbers = lane8.astype(F32).astype(BF16)
    for b in range(blocks):
        ids = dof[b // links, b % links : b % links + 1, :]
        hit = jnp.where(sub == ids, 1.0, 0.0).astype(BF16)
        dof_inv[b] = dot(numbers, hit, NT).astype(jnp.int32)

    inverse = {}
    for k in range(links):
        for p in range(slots):
            at = jnp.int32(0)
            for j in range(1, slots):
                at = jnp.where(partner[k, j] == p, j, at)
            inverse[k, p] = at

    loaded[2].wait()
    loaded[3].wait()
    info_copy.wait_recv()
    send_maps(infop.at[slots], 1)

    def weight_of(b):
        return weight[b // links, b % links : b % links + 1, :]

    for b in range(blocks):
        s, k = b // links, b % links
        live = info[s] * infop[partner[k, s]]
        live = jnp.broadcast_to(live, (loads, width))
        mask[b] = live
        resid = live * rhs[s, :, k, :]
        rv[b] = resid
        yv[b] = resid
        zv[b] = weight_of(b) * resid

    lane = lax.broadcasted_iota(jnp.int32, (loads, width), 1)
    load_id = lax.broadcasted_iota(jnp.int32, (loads, width), 0)

    def total(first, second):
        return jnp.sum(jnp.sum(first * second, axis=0), axis=1, keepdims=True)

    def scalar_terms(packed):
        z, y = zv[...], yv[...]
        found = [total(rv[...], z), total(z, y), total(z, sv[...]), total(dv[...], y)]
        tile = jnp.zeros((loads, width), F32)
        for i, value in enumerate(found):
            at = lane == (4 * load_id + i if packed else i)
            tile = jnp.where(at, value, tile)
        return tile

    def update(tile, packed, first):
        rz, zy, zs_, dy = [
            jnp.broadcast_to(
                jnp.sum(
                    jnp.where(lane == (4 * load_id + i if packed else i), tile, 0.0),
                    axis=1,
                    keepdims=True,
                ),
                tile.shape,
            )
            for i in range(4)
        ]
        beta = rz / sc[0]
        if first is not None:
            beta = jnp.where(first, 0.0, beta)
        curv = zy + beta * (zs_ + dy) + beta * beta * sc[1]
        alpha = rz / curv
        sc[0], sc[1], sc[2], sc[3] = rz, curv, alpha, beta
        direction = zv[...] + beta[None] * dv[...]
        image = yv[...] + beta[None] * sv[...]
        dv[...] = direction
        sv[...] = image
        x_out[...] = x_out[...] + alpha[None] * direction
        resid = rv[...] - alpha[None] * image
        rv[...] = resid
        return resid

    def put3(ref, s, k, value):
        for i, part in enumerate(split3(value)):
            ref[s, i * loads : (i + 1) * loads, k * width : (k + 1) * width] = part

    def take(value, index):
        return jnp.take_along_axis(value, index, axis=1, mode="promise_in_bounds")

    def convert(s):
        flex_copy(s).wait()
        here = s % STAGES

        def chunk(i, _):
            at = pl.ds(pl.multiple_of(i * 64, 64), 64)
            high, low = split2(stage[here, at, :])
            flex_hi[s, at, :] = high
            flex_lo[s, at, :] = low
            return 0

        lax.fori_loop(0, iface // 64, chunk, 0)
        if s + STAGES < slots:
            flex_copy(s + STAGES).start()

    def local_answers(it, first, last):
        def one(s, _):
            left = jnp.concatenate([vsp[s], fsp[s]], axis=1)
            for n in range(iface // 256):
                at = slice(n * 256, (n + 1) * 256)
                out = dot(left, flex_hi[s, :, at], NN) + dot(left, flex_lo[s, :, at], NN)
                out = sum3(out)
                for h in range(2):
                    piece = out[:, h * width : (h + 1) * width]
                    k = 2 * n + h
                    if k < links:
                        ulink[s * links + k] = piece
                    else:
                        usend[it, s * links + k - links] = piece
            return 0

        lax.fori_loop(first, last, one, 0)

    def within(s):
        return jnp.logical_and(lane >= s * corners, lane < (s + 1) * corners)

    def shift(value, by):
        by = by % width
        return pltpu.roll(value, by, 1) if by else value

    def sent(it):
        group_sent(tbuf.at[it], t_s.at[it], t_r.at[it, 0], yzs)
        group_sent(cbuf.at[it], c_s.at[it], c_r.at[it], cs)
        group_sent(xbuf.at[it], x_s.at[it], x_r.at[it], xs)
        group_sent(y1buf.at[it], y1_s.at[it], y1_r.at[it], ys)
        group_sent(z1buf.at[it], z1_s.at[it], z1_r.at[it], zs)
        group_sent(z2buf.at[it], z2_s.at[it], z2_r.at[it], zs)
        group_sent(y2buf.at[it], y2_s.at[it], y2_r.at[it], ys)
        rcopy(psend.at[it], precv.at[it], p_s.at[it], p_r.at[it], cs[0][0]).wait_send()
        group_sent(qrecv.at[it], q_s.at[it], q_r.at[it], xs)
        rcopy(gsend.at[it], frecv.at[it], f_s.at[it], f_r.at[it], prev).wait_send()
        rcopy(usend.at[it], urecv.at[it], u_s.at[it], u_r.at[it], nxt).wait_send()

    def body(it, _):
        for b in range(blocks):
            value = weight_of(b) * yv[b]
            vblk[b] = value
            put3(vsp, b // links, b % links, value)
        for b in range(blocks):
            p, k = b // links, b % links
            from_block = inverse[k, p] * links + k
            index = jnp.concatenate([dof_inv[from_block]] * (loads // 8), axis=0)
            value = -take(vblk[from_block], index)
            gsend[it, b] = value
            put3(gsp, p, k, value)

        def terms(blocks3, factors):
            found = jnp.zeros((loads, width), F32)
            for s in range(slots):
                part = sum3(dot(blocks3[s], factors[s], NT))
                rest = jnp.zeros((loads, width - 2 * corners), F32)
                part = jnp.concatenate([part, rest], axis=1)
                part = shift(part, s * corners) + shift(part, (s - 1) * corners)
                found = jnp.where(within(s), part, found)
            return found

        tbuf[it, me_yz, :, 0:width] = terms(vsp, wo)

        @pl.when(it == 0)
        def _():
            cpl_copy.wait_recv()
            build_coupling(cplp, wp)

        tbuf[it, me_yz, :, width:tiles] = terms(gsp, wp)
        for d, _ in yzs:
            rcopy(
                tbuf.at[it, me_yz], tbuf.at[it, me_yz], t_s.at[it], t_r.at[it, me_yz], d
            ).start()
        tile = scalar_terms(False)

        @pl.when(it > 0)
        def _():
            sent(it - 1)

        @pl.when(it == 0)
        def _():
            wait_maps(0)

            def rows(p, _):
                base = (lax.rem(p, NX) * cols + me_yz * NK + lax.div(p, NX)) * own_rows
                index = lax.broadcasted_iota(jnp.int32, (own_rows, width), 0) + base
                index = index.astype(F32)
                at = pl.ds(pl.multiple_of(p * own_rows, own_rows), own_rows)
                for q in range(NYZ):
                    for h in range(2):
                        hit = jnp.where(index == maps_yz[q, h], 1.0, 0.0)
                        scatter[q, at, h * width : (h + 1) * width] = hit.astype(BF16)
                return 0

            lax.fori_loop(0, nxc, rows, 0)
            for s in range(STAGES):
                convert(s)

        def spread(q):
            return dot(stack3(tbuf[it, q]), scatter[q], NT)

        found = spread(me_yz)
        for d, q in reversed(yzs):
            rcopy(tbuf.at[it, me_yz], tbuf.at[it, q], t_s.at[it], t_r.at[it, q], d).wait_recv()
            found = found + spread(q)
        cbuf[it, ck, :, 0:rset] = sum3(found)
        cbuf[it, ck, :, rset : rset + width] = tile
        group_start(cbuf.at[it, ck], cbuf.at[it], ck, c_s.at[it], c_r.at[it], cs)
        force_copy = rcopy(gsend.at[it], frecv.at[it], f_s.at[it], f_r.at[it], prev)
        force_copy.start()
        group_wait(cbuf.at[it], c_s.at[it], c_r.at[it], cs)
        xbuf[it, row] = cbuf[it, 0] + cbuf[it, 1]
        group_start(xbuf.at[it, row], xbuf.at[it], row, x_s.at[it], x_r.at[it], xs)

        @pl.when(it == 0)
        def _():
            for s in range(STAGES, slots):
                convert(s)
            m_local.wait()
            group_wait(m32, m_s, m_r, xcs)
            group_sent(m32, m_s, m_r, xcs)
            for b in range(nxc):
                high, low = split2(m32[b])
                m2[b * own_rows : (b + 1) * own_rows, :] = high
                m2[rset + b * own_rows : rset + (b + 1) * own_rows, :] = low

        group_wait(xbuf.at[it], x_s.at[it], x_r.at[it], xs)
        load = xbuf[it, 0] + xbuf[it, 1] + xbuf[it, 2] + xbuf[it, 3]
        left = stack3(load[:, :rset])
        answer = sum3(dot(jnp.concatenate([left, left], axis=1), m2[...], NN))
        y1buf[it, cy, :, 0:khalf] = answer[:, :khalf]
        y1buf[it, cy, :, khalf : khalf + width] = load[:, rset:]
        z1buf[it, cz] = answer[:, khalf:]
        group_start(y1buf.at[it, cy], y1buf.at[it], cy, y1_s.at[it], y1_r.at[it], ys)
        group_start(z1buf.at[it, cz], z1buf.at[it], cz, z1_s.at[it], z1_r.at[it], zs)

        force_copy.wait_recv()
        for b in range(blocks):
            put3(fsp, b // links, b % links, frecv[it, b])
        local_answers(it, 0, 3)

        group_wait(y1buf.at[it], y1_s.at[it], y1_r.at[it], ys)
        group_wait(z1buf.at[it], z1_s.at[it], z1_r.at[it], zs)
        z2buf[it, cz] = y1buf[it, 0] + y1buf[it, 1] + y1buf[it, 2] + y1buf[it, 3]
        y2buf[it, cy] = z1buf[it, 0] + z1buf[it, 1] + z1buf[it, 2] + z1buf[it, 3]
        group_start(z2buf.at[it, cz], z2buf.at[it], cz, z2_s.at[it], z2_r.at[it], zs)
        group_start(y2buf.at[it, cy], y2buf.at[it], cy, y2_s.at[it], y2_r.at[it], ys)
        local_answers(it, 3, slots)

        @pl.when(it == 0)
        def _():
            wait_maps(1)
            step = own_rows

            def rows(b, _):
                index = lax.broadcasted_iota(jnp.int32, (step, width), 0) + (me_xc * kset + b * step)
                index = index.astype(F32)
                at = pl.ds(pl.multiple_of(b * step, step), step)
                for q in range(nxc):
                    for h in range(2):
                        hit = jnp.where(index == maps_xc[q, h], 1.0, 0.0)
                        lo = (2 * (q % NX) + h) * width
                        pick[q // NX, at, lo : lo + width] = hit.astype(BF16)
                return 0

            lax.fori_loop(0, kset // step, rows, 0)

        group_wait(z2buf.at[it], z2_s.at[it], z2_r.at[it], zs)
        group_wait(y2buf.at[it], y2_s.at[it], y2_r.at[it], ys)
        answer_copy = rcopy(usend.at[it], urecv.at[it], u_s.at[it], u_r.at[it], nxt)
        answer_copy.start()
        first = z2buf[it, 0] + z2buf[it, 1] + z2buf[it, 2] + z2buf[it, 3]
        second = y2buf[it, 0] + y2buf[it, 1] + y2buf[it, 2] + y2buf[it, 3]
        scalars = first[:, khalf:]
        left = stack3(jnp.concatenate([first[:, :khalf], second], axis=1))
        found = sum3(dot(left, pick[1 - ck], NN))
        for q in range(NX):
            psend[it, q] = found[:, q * tiles : (q + 1) * tiles]
        core_copy = rcopy(psend.at[it], precv.at[it], p_s.at[it], p_r.at[it], cs[0][0])
        core_copy.start()
        found = sum3(dot(left, pick[ck], NN))
        core_copy.wait_recv()
        for q in range(NX):
            qsend[it, q] = found[:, q * tiles : (q + 1) * tiles] + precv[it, q]
        for d, other in xs:
            rcopy(qsend.at[it, other], qrecv.at[it, row], q_s.at[it], q_r.at[it], d).start()
        qrecv[it, row] = qsend[it, row]

        @pl.when(it > 0)
        def _():
            resid = update(scalars, False, it == 1)
            for b in range(blocks):
                zv[b] = weight_of(b) * resid[b]

        group_wait(qrecv.at[it], q_s.at[it], q_r.at[it], xs)
        picked = qrecv[it, 0] + qrecv[it, 1] + qrecv[it, 2] + qrecv[it, 3]

        def spread_back(part, s, factors):
            left = shift(part, -s * corners)
            left = jnp.where(lane < corners, left, shift(part, (1 - s) * corners))
            return sum3(dot(stack3(left[:, : 2 * corners]), factors[s], NN))

        for s in range(slots):
            found = spread_back(picked[:, :width], s, wo)
            other = spread_back(picked[:, width:], s, wp)
            for k in range(links):
                clink[s * links + k] = found[:, k * width : (k + 1) * width]
                cface[s * links + k] = other[:, k * width : (k + 1) * width]

        answer_copy.wait_recv()
        alpha, beta = sc[2], sc[3]
        for b in range(blocks):
            s, k = b // links, b % links
            facing = partner[k, s] * links + k
            index = jnp.broadcast_to(dof[s, k : k + 1, :], (loads, width))
            far = take(urecv[it, facing] + cface[facing], index)
            image = (ulink[b] + clink[b] - far) * mask[b]
            image = image + beta * tv[b]
            tv[b] = jnp.where(it == 0, 0.0, image)
            yv[b] = jnp.where(it == 0, image, yv[b] - alpha * image)
        return 0

    lax.fori_loop(0, ITERS, body, 0)

    me_all = row * cols + col
    pybuf[me_all] = jnp.sum(scalar_terms(True), axis=0, keepdims=True)

    def tell(i, _):
        d = (turn(row, lax.div(i, cols), NX), turn(col, lax.rem(i, cols), cols))
        rcopy(pybuf.at[me_all], pybuf.at[me_all], py_s, py_r, d).start()
        return 0

    lax.fori_loop(1, NX * cols, tell, 0)
    sent(ITERS - 1)
    info_copy.wait_send()
    cpl_copy.wait_send()
    everything = pybuf.at[pl.ds(0, NX * cols - 1)]
    final = rcopy(everything, everything, py_s, py_r, nxt)
    final.wait_recv()
    line = jnp.sum(pybuf[...], axis=0)
    final.wait_send()
    r_out[...] = update(jnp.broadcast_to(line, (loads, width)), True, None)


def local(
    flexibility,
    coupling,
    coarse_inverse,
    precon_weight,
    right_side,
    counts,
    partner,
    dof_index,
    corner_map,
):
    flex = flexibility[0, 0]
    cpl = coupling[0, 0]
    slots, iface = flex.shape[:2]
    half = iface // 2
    links, width = dof_index.shape[3:]
    loads = right_side.shape[3]
    own_rows, coarse = coarse_inverse.shape
    corners = corner_map.shape[-1]
    blocks = slots * links
    nxc = NX * NK
    kset, rset = coarse // nxc, own_rows * nxc
    rows3 = 3 * loads
    pair = 2 * width

    vec = (blocks, loads, width)
    per = (ITERS,)
    vm = pltpu.VMEM
    dma = pltpu.SemaphoreType.DMA
    scratch = [
        vm((STAGES, iface, iface), F32),
        vm((slots, iface, iface), BF16),
        vm((slots, iface, iface), BF16),
        vm((nxc, own_rows, kset), F32),
        vm((2 * rset, kset), BF16),
        vm(cpl.shape, F32),
        vm((slots, links, width), F32),
        vm((slots, loads, links, width), F32),
        vm((slots, links, width), jnp.int32),
        vm((slots, 1, corners), jnp.int32),
        vm((blocks, 8, width), jnp.int32),
        vm((slots, corners, half), F32),
        vm((slots + 1, 1, width), F32),
        vm((slots + 1, 1, width), F32),
        vm((NYZ, 2, 1, width), F32),
        vm((nxc, 2, 1, width), F32),
        vm((slots, 2 * corners, half), BF16),
        vm((slots, 2 * corners, half), BF16),
        vm((NYZ, rset, pair), BF16),
        vm((NK, kset, NX * pair), BF16),
        vm(per + (NYZ, loads, pair), F32),
        vm(per + (NK, loads, rset + width), F32),
        vm(per + (NX, loads, rset + width), F32),
        vm(per + (NY, loads, kset // 2 + width), F32),
        vm(per + (NZ, loads, kset // 2), F32),
        vm(per + (NY, loads, kset // 2), F32),
        vm(per + (NZ, loads, kset // 2 + width), F32),
        vm(per + (NX, loads, pair), F32),
        vm(per + (NX, loads, pair), F32),
        vm(per + (NX, loads, pair), F32),
        vm(per + (NX, loads, pair), F32),
        vm(per + vec, F32),
        vm(per + vec, F32),
        vm(per + vec, F32),
        vm(per + vec, F32),
        vm(vec, F32),
        vm((slots, rows3, half), BF16),
        vm((slots, rows3, half), BF16),
        vm((slots, rows3, half), BF16),
    ]
    scratch += [vm(vec, F32)] * 10
    scratch += [
        vm((4, loads, width), F32),
        vm((NYZ * nxc, 1, width), F32),
        dma((slots,)),
        dma((5,)),
        dma,
        dma,
        dma,
        dma,
        dma,
        dma,
        dma,
        dma,
        dma,
        dma,
        dma,
        dma(per),
        dma(per + (NYZ,)),
    ]
    scratch += [dma(per)] * 20 + [dma] * 2
    in_vmem = pl.BlockSpec(memory_space=pltpu.VMEM)
    in_smem = pl.BlockSpec(memory_space=pltpu.SMEM)
    in_place = pl.BlockSpec(memory_space=pl.ANY)
    solved, resid = pl.pallas_call(
        kernel,
        name="feti",
        out_shape=[jax.ShapeDtypeStruct(vec, F32)] * 2,
        in_specs=[in_place] * 7 + [in_smem] * 2,
        out_specs=[in_vmem] * 2,
        scratch_shapes=scratch,
        compiler_params=pltpu.CompilerParams(
            collective_id=0, has_side_effects=True, vmem_limit_bytes=67043328
        ),
    )(
        flex,
        coarse_inverse,
        cpl,
        precon_weight[0, 0],
        right_side[0, 0],
        dof_index[0, 0],
        corner_map.reshape(slots, 1, corners),
        partner[0, 0],
        counts,
    )

    def outer(value):
        value = value.reshape(slots, links, loads, width).transpose(0, 2, 1, 3)
        return value[None, None]

    return outer(solved), outer(resid)


def solution(mesh):
    in_specs = (
        P("row", "col", None, None, None),
        P("row", "col", None, None, None),
        P(("row", "col"), None),
        P("row", "col", None, None, None),
        P("row", "col", None, None, None, None),
        P("row", "col"),
        P("row", "col", None, None),
        P("row", "col", None, None, None),
        P("row", "col", None, None),
    )
    out_specs = (P("row", "col", None, None, None, None), P("row", "col", None, None, None, None))
    return jax.shard_map(local, mesh=mesh, in_specs=in_specs, out_specs=out_specs, check_vma=False)
```

```python
import functools

import jax
import jax.numpy as jnp
from jax import lax
from jax.experimental import pallas as pl
from jax.experimental.pallas import tpu as pltpu
from jax.sharding import PartitionSpec as P

ITERS = 3
NX, NZ, NY, NK = 4, 4, 4, 2
NYZ = NZ * NY
STAGES = 3

MESH = pl.DeviceIdType.MESH
F32 = jnp.float32
BF16 = jnp.bfloat16
NT = (((1,), (1,)), ((), ()))
NN = (((1,), (0,)), ((), ()))


def split2(value):
    high = value.astype(BF16)
    low = (value - high.astype(F32)).astype(BF16)
    return high, low


def split3(value):
    high = value.astype(BF16)
    return high, (value - high.astype(F32)).astype(BF16)


def stack3(value):
    return jnp.concatenate(split3(value), axis=0)


def dot(left, right, dims):
    return lax.dot_general(left, right, dims, preferred_element_type=F32)


def sum3(value):
    rows = value.shape[0] // 2
    return value[rows:] + value[:rows]


def rcopy(src, dst, send, recv, device):
    return pltpu.make_async_remote_copy(
        src_ref=src,
        dst_ref=dst,
        send_sem=send,
        recv_sem=recv,
        device_id=device,
        device_id_type=MESH,
    )


def group_start(src, buf, mine, send, recv, peers):
    for device, _ in peers:
        rcopy(src, buf.at[mine], send, recv, device).start()


def group_copy(buf, send, recv, peers):
    part = buf.at[pl.ds(0, len(peers))]
    return rcopy(part, part, send, recv, peers[0][0])


def group_wait(buf, send, recv, peers):
    group_copy(buf, send, recv, peers).wait_recv()


def group_sent(buf, send, recv, peers):
    group_copy(buf, send, recv, peers).wait_send()


def kernel(
    flex, cinv, cpl_in, weight_in, rhs_in, dof_in, map_in, partner, counts,
    x_out, r_out,
    stage, flex_hi, flex_lo, m32, m2, cpl, weight, rhs, dof, rowmap, dof_inv, cplp, info, infop,
    maps_yz, maps_xc, wo, wp, scatter, pick, tbuf, cbuf, xbuf, y1buf, z1buf, y2buf, z2buf,
    psend, precv, qsend, qrecv, gsend, frecv, usend, urecv,
    vblk, vsp, gsp, fsp, yv, tv, dv, sv, zv, rv, mask, ulink, clink, cface, sc,
    pybuf,
    flex_sem, load_sem, mloc_sem, info_s, info_r, cpl_s, cpl_r, mapa_s, mapa_r, mapb_s, mapb_r,
    m_s, m_r, t_s, t_r, c_s, c_r, x_s, x_r, y1_s, y1_r, z1_s, z1_r, y2_s, y2_r, z2_s, z2_r,
    p_s, p_r, q_s, q_r, f_s, f_r, u_s, u_r, py_s, py_r,
):
    slots, iface = flex.shape[:2]
    half = iface // 2
    links, width = dof.shape[1:]
    loads = rhs.shape[1]
    corners = cpl.shape[1]
    own_rows, coarse = cinv.shape
    nxc = NX * NK
    kset = coarse // nxc
    rset = own_rows * nxc
    khalf = kset // 2
    blocks = slots * links
    tiles = 2 * width
    spare = slots * corners

    row, col = lax.axis_index("row"), lax.axis_index("col")
    cz = lax.div(col, NY * NK)
    cy = lax.rem(lax.div(col, NK), NY)
    ck = lax.rem(col, NK)
    cols = NZ * NY * NK
    me_yz = cz * NY + cy
    me_xc = ck * NX + row
    prev = (row, lax.rem(col + cols - 1, cols))
    nxt = (row, lax.rem(col + 1, cols))

    def device(x, z, y, k):
        return (x, (z * NY + y) * NK + k)

    def turn(value, by, size):
        return lax.rem(value + by, size)

    xs = [(device(turn(row, i, NX), cz, cy, ck), turn(row, i, NX)) for i in (2, 1, 3)]
    ys = [(device(row, cz, turn(cy, i, NY), ck), turn(cy, i, NY)) for i in (2, 1, 3)]
    zs = [(device(row, turn(cz, i, NZ), cy, ck), turn(cz, i, NZ)) for i in (2, 1, 3)]
    cs = [(device(row, cz, cy, 1 - ck), 1 - ck)]
    order = sorted(
        [(i, j) for i in range(NZ) for j in range(NY) if (i, j) != (0, 0)],
        key=lambda ij: -(min(ij[0], NZ - ij[0]) + min(ij[1], NY - ij[1])),
    )
    yzs = [
        (device(row, turn(cz, i, NZ), turn(cy, j, NY), ck), turn(cz, i, NZ) * NY + turn(cy, j, NY))
        for i, j in order
    ]
    xcs = [
        (device(turn(row, i, NX), cz, cy, turn(ck, j, NK)), turn(ck, j, NK) * NX + turn(row, i, NX))
        for i in (2, 1, 3, 0)
        for j in range(NK)
        if (i, j) != (0, 0)
    ]

    barrier = pltpu.get_barrier_semaphore()
    everyone = [d for d, _ in yzs] + [d for d, _ in xcs] + [prev, nxt]
    for d in everyone:
        pl.semaphore_signal(barrier, inc=1, device_id=d, device_id_type=MESH)

    def flex_copy(s):
        return pltpu.make_async_copy(flex.at[s], stage.at[s % STAGES], flex_sem.at[s])

    def m_part(other):
        return cinv.at[:, pl.ds(pl.multiple_of(other * kset, 128), kset)]

    loaded = [
        pltpu.make_async_copy(src, dst, load_sem.at[i])
        for i, (src, dst) in enumerate(
            [(map_in, rowmap), (dof_in, dof), (rhs_in, rhs), (weight_in, weight), (cpl_in, cpl)]
        )
    ]
    for copy in loaded:
        copy.start()
    m_local = pltpu.make_async_copy(m_part(me_xc), m32.at[me_xc], mloc_sem)
    m_local.start()
    for s in range(STAGES):
        flex_copy(s).start()

    for s in range(slots):
        live = jnp.where(s < counts[0, 0], 1.0, 0.0).astype(F32)
        info[s] = jnp.broadcast_to(live, (1, width))
    loaded[0].wait()
    lane8 = lax.broadcasted_iota(jnp.int32, (8, width), 1)
    found = jnp.full((8, width), -1, jnp.int32)
    for s in range(slots):
        ids = jnp.broadcast_to(rowmap[s], (8, corners))
        ids = jnp.concatenate([ids, jnp.zeros((8, width - corners), jnp.int32)], axis=1)
        if s:
            ids = pltpu.roll(ids, s * corners, 1)
        inside = jnp.logical_and(lane8 >= s * corners, lane8 < (s + 1) * corners)
        found = jnp.where(inside, ids, found)
    info[slots] = found[0:1].astype(F32)

    pl.semaphore_wait(barrier, len(everyone))

    info_copy = rcopy(info, infop, info_s, info_r, nxt)
    info_copy.start()
    loaded[4].wait()
    cpl_copy = rcopy(cpl.at[:, :, half:], cplp, cpl_s, cpl_r, nxt)
    cpl_copy.start()
    for d, other in xcs:
        rcopy(m_part(other), m32.at[me_xc], m_s, m_r, d).start()
    map_groups = [(maps_yz, me_yz, mapa_s, mapa_r, yzs), (maps_xc, me_xc, mapb_s, mapb_r, xcs)]

    def send_maps(src, h):
        for buf, mine, send, recv, peers in map_groups:
            for d, _ in peers:
                rcopy(src, buf.at[mine, h], send, recv, d).start()
            buf[mine, h] = src[...]

    def wait_maps(group):
        buf, _, send, recv, peers = map_groups[group]
        group_wait(buf, send, recv, peers)
        group_sent(buf, send, recv, peers)

    send_maps(info.at[slots], 0)

    def build_coupling(source, out):
        for s in range(slots):
            value = source[s, :, 0:half]
            high = value.astype(BF16).astype(F32)
            out[s] = jnp.concatenate([high, value - high], axis=0).astype(BF16)

    build_coupling(cpl, wo)
    tv[...] = jnp.zeros_like(tv)
    dv[...] = jnp.zeros_like(dv)
    sv[...] = jnp.zeros_like(sv)
    x_out[...] = jnp.zeros_like(x_out)
    sc[0] = jnp.ones_like(sc[0])
    sc[1] = jnp.zeros_like(sc[1])
    sc[2] = jnp.zeros_like(sc[2])
    sc[3] = jnp.zeros_like(sc[3])

    loaded[1].wait()
    sub = lax.broadcasted_iota(jnp.int32, (width, width), 0)
    numbers = lane8.astype(F32).astype(BF16)
    for b in range(blocks):
        ids = dof[b // links, b % links : b % links + 1, :]
        hit = jnp.where(sub == ids, 1.0, 0.0).astype(BF16)
        dof_inv[b] = dot(numbers, hit, NT).astype(jnp.int32)

    inverse = {}
    for k in range(links):
        for p in range(slots):
            at = jnp.int32(0)
            for j in range(1, slots):
                at = jnp.where(partner[k, j] == p, j, at)
            inverse[k, p] = at

    loaded[2].wait()
    loaded[3].wait()
    info_copy.wait_recv()
    send_maps(infop.at[slots], 1)

    def put3(ref, s, k, value):
        for i, part in enumerate(split3(value)):
            ref[s, i * loads : (i + 1) * loads, k * width : (k + 1) * width] = part

    def multipliers(b, value):
        vblk[b] = value
        put3(vsp, b // links, b % links, value)

    def weight_of(b):
        return weight[b // links, b % links : b % links + 1, :]

    for b in range(blocks):
        s, k = b // links, b % links
        live = info[s] * infop[partner[k, s]]
        live = jnp.broadcast_to(live, (loads, width))
        mask[b] = live
        resid = live * rhs[s, :, k, :]
        rv[b] = resid
        yv[b] = resid
        value = weight_of(b) * resid
        zv[b] = value
        multipliers(b, value)

    lane = lax.broadcasted_iota(jnp.int32, (loads, width), 1)
    load_id = lax.broadcasted_iota(jnp.int32, (loads, width), 0)

    def total(first, second):
        return jnp.sum(jnp.sum(first * second, axis=0), axis=1, keepdims=True)

    def scalar_terms(packed):
        z, y = zv[...], yv[...]
        found = [total(rv[...], z), total(z, y), total(z, sv[...]), total(dv[...], y)]
        tile = jnp.zeros((loads, width), F32)
        for i, value in enumerate(found):
            at = lane == (4 * load_id + i if packed else spare + i)
            tile = jnp.where(at, value, tile)
        return tile

    def update(tile, packed, first):
        rz, zy, zs_, dy = [
            jnp.broadcast_to(
                jnp.sum(
                    jnp.where(lane == (4 * load_id + i if packed else spare + i), tile, 0.0),
                    axis=1,
                    keepdims=True,
                ),
                tile.shape,
            )
            for i in range(4)
        ]
        beta = rz / sc[0]
        if first is not None:
            beta = jnp.where(first, 0.0, beta)
        curv = zy + beta * (zs_ + dy) + beta * beta * sc[1]
        alpha = rz / curv
        sc[0], sc[1], sc[2], sc[3] = rz, curv, alpha, beta
        direction = zv[...] + beta[None] * dv[...]
        image = yv[...] + beta[None] * sv[...]
        dv[...] = direction
        sv[...] = image
        x_out[...] = x_out[...] + alpha[None] * direction
        resid = rv[...] - alpha[None] * image
        rv[...] = resid
        return resid

    def take(value, index):
        return jnp.take_along_axis(value, index, axis=1, mode="promise_in_bounds")

    def convert(s):
        flex_copy(s).wait()
        here = s % STAGES

        def chunk(i, _):
            at = pl.ds(pl.multiple_of(i * 64, 64), 64)
            high, low = split2(stage[here, at, :])
            flex_hi[s, at, :] = high
            flex_lo[s, at, :] = low
            return 0

        lax.fori_loop(0, iface // 64, chunk, 0)
        if s + STAGES < slots:
            flex_copy(s + STAGES).start()

    def local_answers(it, first, last):
        def one(s, _):
            left = jnp.concatenate([vsp[s], fsp[s]], axis=1)
            for n in range(iface // 256):
                at = slice(n * 256, (n + 1) * 256)
                out = dot(left, flex_hi[s, :, at], NN) + dot(left, flex_lo[s, :, at], NN)
                out = sum3(out)
                for h in range(2):
                    piece = out[:, h * width : (h + 1) * width]
                    k = 2 * n + h
                    if k < links:
                        ulink[s * links + k] = piece
                    else:
                        usend[it, s * links + k - links] = piece
            return 0

        lax.fori_loop(first, last, one, 0)

    def within(s):
        return jnp.logical_and(lane >= s * corners, lane < (s + 1) * corners)

    def shift(value, by):
        by = by % width
        return pltpu.roll(value, by, 1) if by else value

    def sent(it):
        group_sent(tbuf.at[it], t_s.at[it], t_r.at[it, 0], yzs)
        group_sent(cbuf.at[it], c_s.at[it], c_r.at[it], cs)
        group_sent(xbuf.at[it], x_s.at[it], x_r.at[it], xs)
        group_sent(y1buf.at[it], y1_s.at[it], y1_r.at[it], ys)
        group_sent(z1buf.at[it], z1_s.at[it], z1_r.at[it], zs)
        group_sent(z2buf.at[it], z2_s.at[it], z2_r.at[it], zs)
        group_sent(y2buf.at[it], y2_s.at[it], y2_r.at[it], ys)
        rcopy(psend.at[it], precv.at[it], p_s.at[it], p_r.at[it], cs[0][0]).wait_send()
        group_sent(qrecv.at[it], q_s.at[it], q_r.at[it], xs)
        rcopy(gsend.at[it], frecv.at[it], f_s.at[it], f_r.at[it], prev).wait_send()
        rcopy(usend.at[it], urecv.at[it], u_s.at[it], u_r.at[it], nxt).wait_send()

    def body(it, _):
        for b in range(blocks):
            p, k = b // links, b % links
            from_block = inverse[k, p] * links + k
            index = jnp.concatenate([dof_inv[from_block]] * (loads // 8), axis=0)
            value = -take(vblk[from_block], index)
            gsend[it, b] = value
            put3(gsp, p, k, value)

        def terms(blocks3, factors):
            found = jnp.zeros((loads, width), F32)
            for s in range(slots):
                part = sum3(dot(blocks3[s], factors[s], NT))
                rest = jnp.zeros((loads, width - 2 * corners), F32)
                part = jnp.concatenate([part, rest], axis=1)
                part = shift(part, s * corners) + shift(part, (s - 1) * corners)
                found = jnp.where(within(s), part, found)
            return found

        tbuf[it, me_yz, :, 0:width] = jnp.where(
            lane < spare, terms(vsp, wo), scalar_terms(False)
        )

        @pl.when(it == 0)
        def _():
            cpl_copy.wait_recv()
            build_coupling(cplp, wp)

        tbuf[it, me_yz, :, width:tiles] = terms(gsp, wp)
        for d, _ in yzs:
            rcopy(
                tbuf.at[it, me_yz], tbuf.at[it, me_yz], t_s.at[it], t_r.at[it, me_yz], d
            ).start()
        @pl.when(it > 0)
        def _():
            sent(it - 1)

        @pl.when(it == 0)
        def _():
            wait_maps(0)

            def rows(p, _):
                base = (lax.rem(p, NX) * cols + me_yz * NK + lax.div(p, NX)) * own_rows
                index = lax.broadcasted_iota(jnp.int32, (own_rows, width), 0) + base
                index = index.astype(F32)
                at = pl.ds(pl.multiple_of(p * own_rows, own_rows), own_rows)
                for q in range(NYZ):
                    for h in range(2):
                        hit = jnp.where(index == maps_yz[q, h], 1.0, 0.0)
                        scatter[q, at, h * width : (h + 1) * width] = hit.astype(BF16)
                return 0

            lax.fori_loop(0, nxc, rows, 0)
            for s in range(STAGES):
                convert(s)

        def spread(q):
            return dot(stack3(tbuf[it, q]), scatter[q], NT)

        found, carried = spread(me_yz), tbuf[it, me_yz, :, 0:width]
        for d, q in reversed(yzs):
            rcopy(tbuf.at[it, me_yz], tbuf.at[it, q], t_s.at[it], t_r.at[it, q], d).wait_recv()
            found, carried = found + spread(q), carried + tbuf[it, q, :, 0:width]
        cbuf[it, ck, :, 0:rset] = sum3(found)
        cbuf[it, ck, :, rset : rset + width] = carried
        group_start(cbuf.at[it, ck], cbuf.at[it], ck, c_s.at[it], c_r.at[it], cs)
        force_copy = rcopy(gsend.at[it], frecv.at[it], f_s.at[it], f_r.at[it], prev)
        force_copy.start()
        group_wait(cbuf.at[it], c_s.at[it], c_r.at[it], cs)
        xbuf[it, row] = cbuf[it, 0] + cbuf[it, 1]
        group_start(xbuf.at[it, row], xbuf.at[it], row, x_s.at[it], x_r.at[it], xs)

        @pl.when(it == 0)
        def _():
            for s in range(STAGES, slots):
                convert(s)
            m_local.wait()
            group_wait(m32, m_s, m_r, xcs)
            group_sent(m32, m_s, m_r, xcs)
            for b in range(nxc):
                high, low = split2(m32[b])
                m2[b * own_rows : (b + 1) * own_rows, :] = high
                m2[rset + b * own_rows : rset + (b + 1) * own_rows, :] = low

        group_wait(xbuf.at[it], x_s.at[it], x_r.at[it], xs)
        load = xbuf[it, 0] + xbuf[it, 1] + xbuf[it, 2] + xbuf[it, 3]
        left = stack3(load[:, :rset])
        answer = sum3(dot(jnp.concatenate([left, left], axis=1), m2[...], NN))
        y1buf[it, cy] = answer[:, :khalf]
        z1buf[it, cz] = answer[:, khalf:]
        group_start(y1buf.at[it, cy], y1buf.at[it], cy, y1_s.at[it], y1_r.at[it], ys)
        group_start(z1buf.at[it, cz], z1buf.at[it], cz, z1_s.at[it], z1_r.at[it], zs)

        force_copy.wait_recv()
        for b in range(blocks):
            put3(fsp, b // links, b % links, frecv[it, b])
        local_answers(it, 0, 3)

        group_wait(y1buf.at[it], y1_s.at[it], y1_r.at[it], ys)
        group_wait(z1buf.at[it], z1_s.at[it], z1_r.at[it], zs)
        z2buf[it, cz] = y1buf[it, 0] + y1buf[it, 1] + y1buf[it, 2] + y1buf[it, 3]
        y2buf[it, cy] = z1buf[it, 0] + z1buf[it, 1] + z1buf[it, 2] + z1buf[it, 3]
        group_start(z2buf.at[it, cz], z2buf.at[it], cz, z2_s.at[it], z2_r.at[it], zs)
        group_start(y2buf.at[it, cy], y2buf.at[it], cy, y2_s.at[it], y2_r.at[it], ys)
        local_answers(it, 3, slots)

        @pl.when(it == 0)
        def _():
            wait_maps(1)
            step = own_rows

            def rows(b, _):
                index = lax.broadcasted_iota(jnp.int32, (step, width), 0) + (me_xc * kset + b * step)
                index = index.astype(F32)
                at = pl.ds(pl.multiple_of(b * step, step), step)
                for q in range(nxc):
                    for h in range(2):
                        hit = jnp.where(index == maps_xc[q, h], 1.0, 0.0)
                        lo = (2 * (q % NX) + h) * width
                        pick[q // NX, at, lo : lo + width] = hit.astype(BF16)
                return 0

            lax.fori_loop(0, kset // step, rows, 0)

        group_wait(z2buf.at[it], z2_s.at[it], z2_r.at[it], zs)
        group_wait(y2buf.at[it], y2_s.at[it], y2_r.at[it], ys)
        answer_copy = rcopy(usend.at[it], urecv.at[it], u_s.at[it], u_r.at[it], nxt)
        answer_copy.start()
        first = z2buf[it, 0] + z2buf[it, 1] + z2buf[it, 2] + z2buf[it, 3]
        second = y2buf[it, 0] + y2buf[it, 1] + y2buf[it, 2] + y2buf[it, 3]
        left = stack3(jnp.concatenate([first, second], axis=1))
        found = sum3(dot(left, pick[1 - ck], NN))
        for q in range(NX):
            psend[it, q] = found[:, q * tiles : (q + 1) * tiles]
        core_copy = rcopy(psend.at[it], precv.at[it], p_s.at[it], p_r.at[it], cs[0][0])
        core_copy.start()
        found = sum3(dot(left, pick[ck], NN))
        core_copy.wait_recv()
        for q in range(NX):
            qsend[it, q] = found[:, q * tiles : (q + 1) * tiles] + precv[it, q]
        for d, other in xs:
            rcopy(qsend.at[it, other], qrecv.at[it, row], q_s.at[it], q_r.at[it], d).start()
        qrecv[it, row] = qsend[it, row]

        @pl.when(it > 0)
        def _():
            resid = update(load[:, rset:], False, it == 1)
            for b in range(blocks):
                zv[b] = weight_of(b) * resid[b]

        group_wait(qrecv.at[it], q_s.at[it], q_r.at[it], xs)
        picked = qrecv[it, 0] + qrecv[it, 1] + qrecv[it, 2] + qrecv[it, 3]

        def spread_back(part, s, factors):
            left = shift(part, -s * corners)
            left = jnp.where(lane < corners, left, shift(part, (1 - s) * corners))
            return sum3(dot(stack3(left[:, : 2 * corners]), factors[s], NN))

        for s in range(slots):
            found = spread_back(picked[:, :width], s, wo)
            other = spread_back(picked[:, width:], s, wp)
            for k in range(links):
                clink[s * links + k] = found[:, k * width : (k + 1) * width]
                cface[s * links + k] = other[:, k * width : (k + 1) * width]

        answer_copy.wait_recv()
        alpha, beta = sc[2], sc[3]
        for b in range(blocks):
            s, k = b // links, b % links
            facing = partner[k, s] * links + k
            index = jnp.broadcast_to(dof[s, k : k + 1, :], (loads, width))
            far = take(urecv[it, facing] + cface[facing], index)
            image = (ulink[b] + clink[b] - far) * mask[b]
            image = image + beta * tv[b]
            tv[b] = jnp.where(it == 0, 0.0, image)
            image = jnp.where(it == 0, image, yv[b] - alpha * image)
            yv[b] = image
            multipliers(b, weight_of(b) * image)
        return 0

    lax.fori_loop(0, ITERS, body, 0)

    me_all = row * cols + col
    pybuf[me_all] = jnp.sum(scalar_terms(True), axis=0, keepdims=True)

    def tell(i, _):
        d = (turn(row, lax.div(i, cols), NX), turn(col, lax.rem(i, cols), cols))
        rcopy(pybuf.at[me_all], pybuf.at[me_all], py_s, py_r, d).start()
        return 0

    lax.fori_loop(1, NX * cols, tell, 0)
    sent(ITERS - 1)
    info_copy.wait_send()
    cpl_copy.wait_send()
    everything = pybuf.at[pl.ds(0, NX * cols - 1)]
    final = rcopy(everything, everything, py_s, py_r, nxt)
    final.wait_recv()
    line = jnp.sum(pybuf[...], axis=0)
    final.wait_send()
    r_out[...] = update(jnp.broadcast_to(line, (loads, width)), True, None)


def local(
    flexibility,
    coupling,
    coarse_inverse,
    precon_weight,
    right_side,
    counts,
    partner,
    dof_index,
    corner_map,
):
    flex = flexibility[0, 0]
    cpl = coupling[0, 0]
    slots, iface = flex.shape[:2]
    half = iface // 2
    links, width = dof_index.shape[3:]
    loads = right_side.shape[3]
    own_rows, coarse = coarse_inverse.shape
    corners = corner_map.shape[-1]
    blocks = slots * links
    nxc = NX * NK
    kset, rset = coarse // nxc, own_rows * nxc
    rows3 = 2 * loads
    pair = 2 * width

    vec = (blocks, loads, width)
    per = (ITERS,)
    vm = pltpu.VMEM
    dma = pltpu.SemaphoreType.DMA
    scratch = [
        vm((STAGES, iface, iface), F32),
        vm((slots, iface, iface), BF16),
        vm((slots, iface, iface), BF16),
        vm((nxc, own_rows, kset), F32),
        vm((2 * rset, kset), BF16),
        vm(cpl.shape, F32),
        vm((slots, links, width), F32),
        vm((slots, loads, links, width), F32),
        vm((slots, links, width), jnp.int32),
        vm((slots, 1, corners), jnp.int32),
        vm((blocks, 8, width), jnp.int32),
        vm((slots, corners, half), F32),
        vm((slots + 1, 1, width), F32),
        vm((slots + 1, 1, width), F32),
        vm((NYZ, 2, 1, width), F32),
        vm((nxc, 2, 1, width), F32),
        vm((slots, 2 * corners, half), BF16),
        vm((slots, 2 * corners, half), BF16),
        vm((NYZ, rset, pair), BF16),
        vm((NK, kset, NX * pair), BF16),
        vm(per + (NYZ, loads, pair), F32),
        vm(per + (NK, loads, rset + width), F32),
        vm(per + (NX, loads, rset + width), F32),
        vm(per + (NY, loads, kset // 2), F32),
        vm(per + (NZ, loads, kset // 2), F32),
        vm(per + (NY, loads, kset // 2), F32),
        vm(per + (NZ, loads, kset // 2), F32),
        vm(per + (NX, loads, pair), F32),
        vm(per + (NX, loads, pair), F32),
        vm(per + (NX, loads, pair), F32),
        vm(per + (NX, loads, pair), F32),
        vm(per + vec, F32),
        vm(per + vec, F32),
        vm(per + vec, F32),
        vm(per + vec, F32),
        vm(vec, F32),
        vm((slots, rows3, half), BF16),
        vm((slots, rows3, half), BF16),
        vm((slots, rows3, half), BF16),
    ]
    scratch += [vm(vec, F32)] * 10
    scratch += [
        vm((4, loads, width), F32),
        vm((NYZ * nxc, 1, width), F32),
        dma((slots,)),
        dma((5,)),
        dma,
        dma,
        dma,
        dma,
        dma,
        dma,
        dma,
        dma,
        dma,
        dma,
        dma,
        dma(per),
        dma(per + (NYZ,)),
    ]
    scratch += [dma(per)] * 20 + [dma] * 2
    in_vmem = pl.BlockSpec(memory_space=pltpu.VMEM)
    in_smem = pl.BlockSpec(memory_space=pltpu.SMEM)
    in_place = pl.BlockSpec(memory_space=pl.ANY)
    solved, resid = pl.pallas_call(
        kernel,
        name="feti",
        out_shape=[jax.ShapeDtypeStruct(vec, F32)] * 2,
        in_specs=[in_place] * 7 + [in_smem] * 2,
        out_specs=[in_vmem] * 2,
        scratch_shapes=scratch,
        compiler_params=pltpu.CompilerParams(
            collective_id=0, has_side_effects=True, vmem_limit_bytes=67043328
        ),
    )(
        flex,
        coarse_inverse,
        cpl,
        precon_weight[0, 0],
        right_side[0, 0],
        dof_index[0, 0],
        corner_map.reshape(slots, 1, corners),
        partner[0, 0],
        counts,
    )

    def outer(value):
        value = value.reshape(slots, links, loads, width).transpose(0, 2, 1, 3)
        return value[None, None]

    return outer(solved), outer(resid)


def solution(mesh):
    in_specs = (
        P("row", "col", None, None, None),
        P("row", "col", None, None, None),
        P(("row", "col"), None),
        P("row", "col", None, None, None),
        P("row", "col", None, None, None, None),
        P("row", "col"),
        P("row", "col", None, None),
        P("row", "col", None, None, None),
        P("row", "col", None, None),
    )
    out_specs = (P("row", "col", None, None, None, None), P("row", "col", None, None, None, None))
    return jax.shard_map(local, mesh=mesh, in_specs=in_specs, out_specs=out_specs, check_vma=False)
```

```python
import functools

import jax
import jax.numpy as jnp
from jax import lax
from jax.experimental import pallas as pl
from jax.experimental.pallas import tpu as pltpu
from jax.sharding import PartitionSpec as P

ITERS = 3
NX, NZ, NY, NK = 4, 4, 4, 2
NYZ = NZ * NY
STAGES = 3

MESH = pl.DeviceIdType.MESH
F32 = jnp.float32
BF16 = jnp.bfloat16
NT = (((1,), (1,)), ((), ()))
NN = (((1,), (0,)), ((), ()))


def split2(value):
    high = value.astype(BF16)
    low = (value - high.astype(F32)).astype(BF16)
    return high, low


def split3(value):
    high = value.astype(BF16)
    return high, (value - high.astype(F32)).astype(BF16)


def stack3(value):
    return jnp.concatenate(split3(value), axis=0)


def dot(left, right, dims):
    return lax.dot_general(left, right, dims, preferred_element_type=F32)


def sum3(value):
    rows = value.shape[0] // 2
    return value[rows:] + value[:rows]


def rcopy(src, dst, send, recv, device):
    return pltpu.make_async_remote_copy(
        src_ref=src,
        dst_ref=dst,
        send_sem=send,
        recv_sem=recv,
        device_id=device,
        device_id_type=MESH,
    )


def group_start(src, buf, mine, send, recv, peers):
    for device, _ in peers:
        rcopy(src, buf.at[mine], send, recv, device).start()


def group_copy(buf, send, recv, peers):
    part = buf.at[pl.ds(0, len(peers))]
    return rcopy(part, part, send, recv, peers[0][0])


def group_wait(buf, send, recv, peers):
    group_copy(buf, send, recv, peers).wait_recv()


def group_sent(buf, send, recv, peers):
    group_copy(buf, send, recv, peers).wait_send()


def kernel(
    flex, cinv, cpl_in, weight_in, rhs_in, dof_in, map_in, partner, counts,
    x_out, r_out,
    stage, flex_hi, flex_lo, m32, m2, cpl, weight, rhs, dof, rowmap, dof_inv, cplp, info, infop,
    maps_yz, maps_xc, wo, wp, scatter, pick, tbuf, cbuf, xbuf, y1buf, z1buf, y2buf, z2buf,
    psend, precv, qsend, qrecv, gsend, frecv, usend, urecv,
    vblk, vsp, gsp, fsp, yv, tv, dv, sv, zv, rv, mask, ulink, clink, cface, sc,
    pybuf,
    flex_sem, load_sem, mloc_sem, info_s, info_r, cpl_s, cpl_r, mapn_s, mapn_r, mapa_s, mapa_r,
    mapb_s, mapb_r,
    m_s, m_r, t_s, t_r, c_s, c_r, x_s, x_r, y1_s, y1_r, z1_s, z1_r, y2_s, y2_r, z2_s, z2_r,
    p_s, p_r, q_s, q_r, f_s, f_r, u_s, u_r, py_s, py_r,
):
    slots, iface = flex.shape[:2]
    half = iface // 2
    links, width = dof.shape[1:]
    loads = rhs.shape[1]
    corners = cpl.shape[1]
    own_rows, coarse = cinv.shape
    nxc = NX * NK
    kset = coarse // nxc
    rset = own_rows * nxc
    khalf = kset // 2
    blocks = slots * links
    tiles = 2 * width
    spare = slots * corners

    row, col = lax.axis_index("row"), lax.axis_index("col")
    cz = lax.div(col, NY * NK)
    cy = lax.rem(lax.div(col, NK), NY)
    ck = lax.rem(col, NK)
    cols = NZ * NY * NK
    me_yz = cz * NY + cy
    me_xc = ck * NX + row
    prev = (row, lax.rem(col + cols - 1, cols))
    nxt = (row, lax.rem(col + 1, cols))

    def device(x, z, y, k):
        return (x, (z * NY + y) * NK + k)

    def turn(value, by, size):
        return lax.rem(value + by, size)

    xs = [(device(turn(row, i, NX), cz, cy, ck), turn(row, i, NX)) for i in (2, 1, 3)]
    ys = [(device(row, cz, turn(cy, i, NY), ck), turn(cy, i, NY)) for i in (2, 1, 3)]
    zs = [(device(row, turn(cz, i, NZ), cy, ck), turn(cz, i, NZ)) for i in (2, 1, 3)]
    cs = [(device(row, cz, cy, 1 - ck), 1 - ck)]
    order = sorted(
        [(i, j) for i in range(NZ) for j in range(NY) if (i, j) != (0, 0)],
        key=lambda ij: -(min(ij[0], NZ - ij[0]) + min(ij[1], NY - ij[1])),
    )
    yzs = [
        (device(row, turn(cz, i, NZ), turn(cy, j, NY), ck), turn(cz, i, NZ) * NY + turn(cy, j, NY))
        for i, j in order
    ]
    xcs = [
        (device(turn(row, i, NX), cz, cy, turn(ck, j, NK)), turn(ck, j, NK) * NX + turn(row, i, NX))
        for i in (2, 1, 3, 0)
        for j in range(NK)
        if (i, j) != (0, 0)
    ]

    near = [p for p, (i, j) in zip(yzs, order) if i == 0 or j == 0]
    far = [p for p, (i, j) in zip(yzs, order) if i != 0 and j != 0]
    barrier = pltpu.get_barrier_semaphore()
    everyone = [d for d, _ in near] + [d for d, _ in xcs] + [prev, nxt]
    for d in everyone:
        pl.semaphore_signal(barrier, inc=1, device_id=d, device_id_type=MESH)

    def flex_copy(s):
        return pltpu.make_async_copy(flex.at[s], stage.at[s % STAGES], flex_sem.at[s])

    def m_part(other):
        return cinv.at[:, pl.ds(pl.multiple_of(other * kset, 128), kset)]

    loaded = [
        pltpu.make_async_copy(src, dst, load_sem.at[i])
        for i, (src, dst) in enumerate(
            [(map_in, rowmap), (dof_in, dof), (rhs_in, rhs), (weight_in, weight), (cpl_in, cpl)]
        )
    ]
    for copy in loaded:
        copy.start()
    m_local = pltpu.make_async_copy(m_part(me_xc), m32.at[me_xc], mloc_sem)
    m_local.start()
    for s in range(STAGES):
        flex_copy(s).start()

    for s in range(slots):
        live = jnp.where(s < counts[0, 0], 1.0, 0.0).astype(F32)
        info[s] = jnp.broadcast_to(live, (1, width))
    loaded[0].wait()
    lane8 = lax.broadcasted_iota(jnp.int32, (8, width), 1)
    found = jnp.full((8, width), -1, jnp.int32)
    for s in range(slots):
        ids = jnp.broadcast_to(rowmap[s], (8, corners))
        ids = jnp.concatenate([ids, jnp.zeros((8, width - corners), jnp.int32)], axis=1)
        if s:
            ids = pltpu.roll(ids, s * corners, 1)
        inside = jnp.logical_and(lane8 >= s * corners, lane8 < (s + 1) * corners)
        found = jnp.where(inside, ids, found)
    info[slots] = found[0:1].astype(F32)

    pl.semaphore_wait(barrier, len(everyone))

    info_copy = rcopy(info, infop, info_s, info_r, nxt)
    info_copy.start()
    loaded[4].wait()
    cpl_copy = rcopy(cpl.at[:, :, half:], cplp, cpl_s, cpl_r, nxt)
    cpl_copy.start()
    for d, other in xcs:
        rcopy(m_part(other), m32.at[me_xc], m_s, m_r, d).start()
    def send_maps(src, h, buf, mine, send, recv, peers):
        for d, _ in peers:
            rcopy(src, buf.at[mine, h], send, recv, d).start()

    own_map, prev_map = info.at[slots], infop.at[slots]
    send_maps(own_map, 0, maps_yz, me_yz, mapn_s, mapn_r, near)
    send_maps(own_map, 0, maps_xc, me_xc, mapb_s, mapb_r, xcs)
    maps_yz[me_yz, 0] = info[slots]
    maps_xc[me_xc, 0] = info[slots]

    def build_coupling(source, out):
        for s in range(slots):
            value = source[s, :, 0:half]
            high = value.astype(BF16).astype(F32)
            out[s] = jnp.concatenate([high, value - high], axis=0).astype(BF16)

    build_coupling(cpl, wo)
    tv[...] = jnp.zeros_like(tv)
    dv[...] = jnp.zeros_like(dv)
    sv[...] = jnp.zeros_like(sv)
    x_out[...] = jnp.zeros_like(x_out)
    sc[0] = jnp.ones_like(sc[0])
    sc[1] = jnp.zeros_like(sc[1])
    sc[2] = jnp.zeros_like(sc[2])
    sc[3] = jnp.zeros_like(sc[3])

    loaded[1].wait()
    sub = lax.broadcasted_iota(jnp.int32, (width, width), 0)
    numbers = lane8.astype(F32).astype(BF16)
    for b in range(blocks):
        ids = dof[b // links, b % links : b % links + 1, :]
        hit = jnp.where(sub == ids, 1.0, 0.0).astype(BF16)
        dof_inv[b] = dot(numbers, hit, NT).astype(jnp.int32)

    inverse = {}
    for k in range(links):
        for p in range(slots):
            at = jnp.int32(0)
            for j in range(1, slots):
                at = jnp.where(partner[k, j] == p, j, at)
            inverse[k, p] = at

    loaded[2].wait()
    loaded[3].wait()
    info_copy.wait_recv()
    near_maps = maps_yz.at[pl.ds(0, len(near)), 0]
    near_copy = rcopy(near_maps, near_maps, mapn_s, mapn_r, near[0][0])
    near_copy.wait_recv()
    send_maps(prev_map, 1, maps_yz, me_yz, mapa_s, mapa_r, yzs)
    send_maps(own_map, 0, maps_yz, me_yz, mapa_s, mapa_r, far)
    send_maps(prev_map, 1, maps_xc, me_xc, mapb_s, mapb_r, xcs)
    maps_yz[me_yz, 1] = infop[slots]
    maps_xc[me_xc, 1] = infop[slots]

    def put3(ref, s, k, value):
        for i, part in enumerate(split3(value)):
            ref[s, i * loads : (i + 1) * loads, k * width : (k + 1) * width] = part

    def multipliers(b, value):
        vblk[b] = value
        put3(vsp, b // links, b % links, value)

    def weight_of(b):
        return weight[b // links, b % links : b % links + 1, :]

    for b in range(blocks):
        s, k = b // links, b % links
        live = info[s] * infop[partner[k, s]]
        live = jnp.broadcast_to(live, (loads, width))
        mask[b] = live
        resid = live * rhs[s, :, k, :]
        rv[b] = resid
        yv[b] = resid
        value = weight_of(b) * resid
        zv[b] = value
        multipliers(b, value)

    lane = lax.broadcasted_iota(jnp.int32, (loads, width), 1)
    load_id = lax.broadcasted_iota(jnp.int32, (loads, width), 0)

    def total(first, second):
        return jnp.sum(jnp.sum(first * second, axis=0), axis=1, keepdims=True)

    def scalar_terms(packed):
        z, y = zv[...], yv[...]
        found = [total(rv[...], z), total(z, y), total(z, sv[...]), total(dv[...], y)]
        tile = jnp.zeros((loads, width), F32)
        for i, value in enumerate(found):
            at = lane == (4 * load_id + i if packed else spare + i)
            tile = jnp.where(at, value, tile)
        return tile

    def update(tile, packed, first):
        rz, zy, zs_, dy = [
            jnp.broadcast_to(
                jnp.sum(
                    jnp.where(lane == (4 * load_id + i if packed else spare + i), tile, 0.0),
                    axis=1,
                    keepdims=True,
                ),
                tile.shape,
            )
            for i in range(4)
        ]
        beta = rz / sc[0]
        if first is not None:
            beta = jnp.where(first, 0.0, beta)
        curv = zy + beta * (zs_ + dy) + beta * beta * sc[1]
        alpha = rz / curv
        sc[0], sc[1], sc[2], sc[3] = rz, curv, alpha, beta
        direction = zv[...] + beta[None] * dv[...]
        image = yv[...] + beta[None] * sv[...]
        dv[...] = direction
        sv[...] = image
        x_out[...] = x_out[...] + alpha[None] * direction
        resid = rv[...] - alpha[None] * image
        rv[...] = resid
        return resid

    def take(value, index):
        return jnp.take_along_axis(value, index, axis=1, mode="promise_in_bounds")

    def convert(s):
        flex_copy(s).wait()
        here = s % STAGES

        def chunk(i, _):
            at = pl.ds(pl.multiple_of(i * 64, 64), 64)
            high, low = split2(stage[here, at, :])
            flex_hi[s, at, :] = high
            flex_lo[s, at, :] = low
            return 0

        lax.fori_loop(0, iface // 64, chunk, 0)
        if s + STAGES < slots:
            flex_copy(s + STAGES).start()

    def local_answers(it, first, last):
        def one(s, _):
            left = jnp.concatenate([vsp[s], fsp[s]], axis=1)
            for n in range(iface // 256):
                at = slice(n * 256, (n + 1) * 256)
                out = dot(left, flex_hi[s, :, at], NN) + dot(left, flex_lo[s, :, at], NN)
                out = sum3(out)
                for h in range(2):
                    piece = out[:, h * width : (h + 1) * width]
                    k = 2 * n + h
                    if k < links:
                        ulink[s * links + k] = piece
                    else:
                        usend[it, s * links + k - links] = piece
            return 0

        lax.fori_loop(first, last, one, 0)

    def within(s):
        return jnp.logical_and(lane >= s * corners, lane < (s + 1) * corners)

    def shift(value, by):
        by = by % width
        return pltpu.roll(value, by, 1) if by else value

    def sent(it):
        group_sent(tbuf.at[it], t_s.at[it], t_r.at[it, 0], yzs)
        group_sent(cbuf.at[it], c_s.at[it], c_r.at[it], cs)
        group_sent(xbuf.at[it], x_s.at[it], x_r.at[it], xs)
        group_sent(y1buf.at[it], y1_s.at[it], y1_r.at[it], ys)
        group_sent(z1buf.at[it], z1_s.at[it], z1_r.at[it], zs)
        group_sent(z2buf.at[it], z2_s.at[it], z2_r.at[it], zs)
        group_sent(y2buf.at[it], y2_s.at[it], y2_r.at[it], ys)
        rcopy(psend.at[it], precv.at[it], p_s.at[it], p_r.at[it], cs[0][0]).wait_send()
        group_sent(qrecv.at[it], q_s.at[it], q_r.at[it], xs)
        rcopy(gsend.at[it], frecv.at[it], f_s.at[it], f_r.at[it], prev).wait_send()
        rcopy(usend.at[it], urecv.at[it], u_s.at[it], u_r.at[it], nxt).wait_send()

    def body(it, _):
        for b in range(blocks):
            p, k = b // links, b % links
            from_block = inverse[k, p] * links + k
            index = jnp.concatenate([dof_inv[from_block]] * (loads // 8), axis=0)
            value = -take(vblk[from_block], index)
            gsend[it, b] = value
            put3(gsp, p, k, value)

        def terms(blocks3, factors):
            found = jnp.zeros((loads, width), F32)
            for s in range(slots):
                part = sum3(dot(blocks3[s], factors[s], NT))
                rest = jnp.zeros((loads, width - 2 * corners), F32)
                part = jnp.concatenate([part, rest], axis=1)
                part = shift(part, s * corners) + shift(part, (s - 1) * corners)
                found = jnp.where(within(s), part, found)
            return found

        tbuf[it, me_yz, :, 0:width] = jnp.where(
            lane < spare, terms(vsp, wo), scalar_terms(False)
        )

        @pl.when(it == 0)
        def _():
            cpl_copy.wait_recv()
            build_coupling(cplp, wp)

        tbuf[it, me_yz, :, width:tiles] = terms(gsp, wp)
        for d, _ in yzs:
            rcopy(
                tbuf.at[it, me_yz], tbuf.at[it, me_yz], t_s.at[it], t_r.at[it, me_yz], d
            ).start()
        @pl.when(it > 0)
        def _():
            sent(it - 1)

        @pl.when(it == 0)
        def _():
            late = maps_yz.at[pl.ds(0, (len(yzs) + len(far)) // 2)]
            late_copy = rcopy(late, late, mapa_s, mapa_r, near[0][0])
            late_copy.wait_recv()
            late_copy.wait_send()
            near_copy.wait_send()

            def rows(p, _):
                base = (lax.rem(p, NX) * cols + me_yz * NK + lax.div(p, NX)) * own_rows
                index = lax.broadcasted_iota(jnp.int32, (own_rows, width), 0) + base
                index = index.astype(F32)
                at = pl.ds(pl.multiple_of(p * own_rows, own_rows), own_rows)
                for q in range(NYZ):
                    for h in range(2):
                        hit = jnp.where(index == maps_yz[q, h], 1.0, 0.0)
                        scatter[q, at, h * width : (h + 1) * width] = hit.astype(BF16)
                return 0

            lax.fori_loop(0, nxc, rows, 0)
            for s in range(STAGES):
                convert(s)

        def spread(q):
            return dot(stack3(tbuf[it, q]), scatter[q], NT)

        found, carried = spread(me_yz), tbuf[it, me_yz, :, 0:width]
        for d, q in reversed(yzs):
            rcopy(tbuf.at[it, me_yz], tbuf.at[it, q], t_s.at[it], t_r.at[it, q], d).wait_recv()
            found, carried = found + spread(q), carried + tbuf[it, q, :, 0:width]
        cbuf[it, ck, :, 0:rset] = sum3(found)
        cbuf[it, ck, :, rset : rset + width] = carried
        group_start(cbuf.at[it, ck], cbuf.at[it], ck, c_s.at[it], c_r.at[it], cs)
        force_copy = rcopy(gsend.at[it], frecv.at[it], f_s.at[it], f_r.at[it], prev)
        force_copy.start()
        group_wait(cbuf.at[it], c_s.at[it], c_r.at[it], cs)
        xbuf[it, row] = cbuf[it, 0] + cbuf[it, 1]
        group_start(xbuf.at[it, row], xbuf.at[it], row, x_s.at[it], x_r.at[it], xs)

        @pl.when(it == 0)
        def _():
            for s in range(STAGES, slots):
                convert(s)
            m_local.wait()
            group_wait(m32, m_s, m_r, xcs)
            group_sent(m32, m_s, m_r, xcs)
            for b in range(nxc):
                high, low = split2(m32[b])
                m2[b * own_rows : (b + 1) * own_rows, :] = high
                m2[rset + b * own_rows : rset + (b + 1) * own_rows, :] = low

        group_wait(xbuf.at[it], x_s.at[it], x_r.at[it], xs)
        load = xbuf[it, 0] + xbuf[it, 1] + xbuf[it, 2] + xbuf[it, 3]
        left = stack3(load[:, :rset])
        answer = sum3(dot(jnp.concatenate([left, left], axis=1), m2[...], NN))
        y1buf[it, cy] = answer[:, :khalf]
        z1buf[it, cz] = answer[:, khalf:]
        group_start(y1buf.at[it, cy], y1buf.at[it], cy, y1_s.at[it], y1_r.at[it], ys)
        group_start(z1buf.at[it, cz], z1buf.at[it], cz, z1_s.at[it], z1_r.at[it], zs)

        force_copy.wait_recv()
        for b in range(blocks):
            put3(fsp, b // links, b % links, frecv[it, b])
        local_answers(it, 0, 3)

        group_wait(y1buf.at[it], y1_s.at[it], y1_r.at[it], ys)
        group_wait(z1buf.at[it], z1_s.at[it], z1_r.at[it], zs)
        z2buf[it, cz] = y1buf[it, 0] + y1buf[it, 1] + y1buf[it, 2] + y1buf[it, 3]
        y2buf[it, cy] = z1buf[it, 0] + z1buf[it, 1] + z1buf[it, 2] + z1buf[it, 3]
        group_start(z2buf.at[it, cz], z2buf.at[it], cz, z2_s.at[it], z2_r.at[it], zs)
        group_start(y2buf.at[it, cy], y2buf.at[it], cy, y2_s.at[it], y2_r.at[it], ys)
        local_answers(it, 3, slots)

        @pl.when(it == 0)
        def _():
            group_wait(maps_xc, mapb_s, mapb_r, xcs)
            group_sent(maps_xc, mapb_s, mapb_r, xcs)
            step = own_rows

            def rows(b, _):
                index = lax.broadcasted_iota(jnp.int32, (step, width), 0) + (me_xc * kset + b * step)
                index = index.astype(F32)
                at = pl.ds(pl.multiple_of(b * step, step), step)
                for q in range(nxc):
                    for h in range(2):
                        hit = jnp.where(index == maps_xc[q, h], 1.0, 0.0)
                        lo = (2 * (q % NX) + h) * width
                        pick[q // NX, at, lo : lo + width] = hit.astype(BF16)
                return 0

            lax.fori_loop(0, kset // step, rows, 0)

        group_wait(z2buf.at[it], z2_s.at[it], z2_r.at[it], zs)
        group_wait(y2buf.at[it], y2_s.at[it], y2_r.at[it], ys)
        answer_copy = rcopy(usend.at[it], urecv.at[it], u_s.at[it], u_r.at[it], nxt)
        answer_copy.start()
        first = z2buf[it, 0] + z2buf[it, 1] + z2buf[it, 2] + z2buf[it, 3]
        second = y2buf[it, 0] + y2buf[it, 1] + y2buf[it, 2] + y2buf[it, 3]
        left = stack3(jnp.concatenate([first, second], axis=1))
        found = sum3(dot(left, pick[1 - ck], NN))
        for q in range(NX):
            psend[it, q] = found[:, q * tiles : (q + 1) * tiles]
        core_copy = rcopy(psend.at[it], precv.at[it], p_s.at[it], p_r.at[it], cs[0][0])
        core_copy.start()
        found = sum3(dot(left, pick[ck], NN))
        core_copy.wait_recv()
        for q in range(NX):
            qsend[it, q] = found[:, q * tiles : (q + 1) * tiles] + precv[it, q]
        for d, other in xs:
            rcopy(qsend.at[it, other], qrecv.at[it, row], q_s.at[it], q_r.at[it], d).start()
        qrecv[it, row] = qsend[it, row]

        @pl.when(it > 0)
        def _():
            resid = update(load[:, rset:], False, it == 1)
            for b in range(blocks):
                zv[b] = weight_of(b) * resid[b]

        group_wait(qrecv.at[it], q_s.at[it], q_r.at[it], xs)
        picked = qrecv[it, 0] + qrecv[it, 1] + qrecv[it, 2] + qrecv[it, 3]

        def spread_back(part, s, factors):
            left = shift(part, -s * corners)
            left = jnp.where(lane < corners, left, shift(part, (1 - s) * corners))
            return sum3(dot(stack3(left[:, : 2 * corners]), factors[s], NN))

        for s in range(slots):
            found = spread_back(picked[:, :width], s, wo)
            other = spread_back(picked[:, width:], s, wp)
            for k in range(links):
                clink[s * links + k] = found[:, k * width : (k + 1) * width]
                cface[s * links + k] = other[:, k * width : (k + 1) * width]

        answer_copy.wait_recv()
        alpha, beta = sc[2], sc[3]
        for b in range(blocks):
            s, k = b // links, b % links
            facing = partner[k, s] * links + k
            index = jnp.broadcast_to(dof[s, k : k + 1, :], (loads, width))
            faced = take(urecv[it, facing] + cface[facing], index)
            image = (ulink[b] + clink[b] - faced) * mask[b]
            image = image + beta * tv[b]
            tv[b] = jnp.where(it == 0, 0.0, image)
            image = jnp.where(it == 0, image, yv[b] - alpha * image)
            yv[b] = image
            multipliers(b, weight_of(b) * image)
        return 0

    lax.fori_loop(0, ITERS, body, 0)

    me_all = row * cols + col
    pybuf[me_all] = jnp.sum(scalar_terms(True), axis=0, keepdims=True)

    def tell(i, _):
        d = (turn(row, lax.div(i, cols), NX), turn(col, lax.rem(i, cols), cols))
        rcopy(pybuf.at[me_all], pybuf.at[me_all], py_s, py_r, d).start()
        return 0

    lax.fori_loop(1, NX * cols, tell, 0)
    sent(ITERS - 1)
    info_copy.wait_send()
    cpl_copy.wait_send()
    everything = pybuf.at[pl.ds(0, NX * cols - 1)]
    final = rcopy(everything, everything, py_s, py_r, nxt)
    final.wait_recv()
    line = jnp.sum(pybuf[...], axis=0)
    final.wait_send()
    r_out[...] = update(jnp.broadcast_to(line, (loads, width)), True, None)


def local(
    flexibility,
    coupling,
    coarse_inverse,
    precon_weight,
    right_side,
    counts,
    partner,
    dof_index,
    corner_map,
):
    flex = flexibility[0, 0]
    cpl = coupling[0, 0]
    slots, iface = flex.shape[:2]
    half = iface // 2
    links, width = dof_index.shape[3:]
    loads = right_side.shape[3]
    own_rows, coarse = coarse_inverse.shape
    corners = corner_map.shape[-1]
    blocks = slots * links
    nxc = NX * NK
    kset, rset = coarse // nxc, own_rows * nxc
    rows3 = 2 * loads
    pair = 2 * width

    vec = (blocks, loads, width)
    per = (ITERS,)
    vm = pltpu.VMEM
    dma = pltpu.SemaphoreType.DMA
    scratch = [
        vm((STAGES, iface, iface), F32),
        vm((slots, iface, iface), BF16),
        vm((slots, iface, iface), BF16),
        vm((nxc, own_rows, kset), F32),
        vm((2 * rset, kset), BF16),
        vm(cpl.shape, F32),
        vm((slots, links, width), F32),
        vm((slots, loads, links, width), F32),
        vm((slots, links, width), jnp.int32),
        vm((slots, 1, corners), jnp.int32),
        vm((blocks, 8, width), jnp.int32),
        vm((slots, corners, half), F32),
        vm((slots + 1, 1, width), F32),
        vm((slots + 1, 1, width), F32),
        vm((NYZ, 2, 1, width), F32),
        vm((nxc, 2, 1, width), F32),
        vm((slots, 2 * corners, half), BF16),
        vm((slots, 2 * corners, half), BF16),
        vm((NYZ, rset, pair), BF16),
        vm((NK, kset, NX * pair), BF16),
        vm(per + (NYZ, loads, pair), F32),
        vm(per + (NK, loads, rset + width), F32),
        vm(per + (NX, loads, rset + width), F32),
        vm(per + (NY, loads, kset // 2), F32),
        vm(per + (NZ, loads, kset // 2), F32),
        vm(per + (NY, loads, kset // 2), F32),
        vm(per + (NZ, loads, kset // 2), F32),
        vm(per + (NX, loads, pair), F32),
        vm(per + (NX, loads, pair), F32),
        vm(per + (NX, loads, pair), F32),
        vm(per + (NX, loads, pair), F32),
        vm(per + vec, F32),
        vm(per + vec, F32),
        vm(per + vec, F32),
        vm(per + vec, F32),
        vm(vec, F32),
        vm((slots, rows3, half), BF16),
        vm((slots, rows3, half), BF16),
        vm((slots, rows3, half), BF16),
    ]
    scratch += [vm(vec, F32)] * 10
    scratch += [
        vm((4, loads, width), F32),
        vm((NYZ * nxc, 1, width), F32),
        dma((slots,)),
        dma((5,)),
        dma,
        dma,
        dma,
        dma,
        dma,
        dma,
        dma,
        dma,
        dma,
        dma,
        dma,
        dma,
        dma,
        dma(per),
        dma(per + (NYZ,)),
    ]
    scratch += [dma(per)] * 20 + [dma] * 2
    in_vmem = pl.BlockSpec(memory_space=pltpu.VMEM)
    in_smem = pl.BlockSpec(memory_space=pltpu.SMEM)
    in_place = pl.BlockSpec(memory_space=pl.ANY)
    solved, resid = pl.pallas_call(
        kernel,
        name="feti",
        out_shape=[jax.ShapeDtypeStruct(vec, F32)] * 2,
        in_specs=[in_place] * 7 + [in_smem] * 2,
        out_specs=[in_vmem] * 2,
        scratch_shapes=scratch,
        compiler_params=pltpu.CompilerParams(
            collective_id=0, has_side_effects=True, vmem_limit_bytes=67043328
        ),
    )(
        flex,
        coarse_inverse,
        cpl,
        precon_weight[0, 0],
        right_side[0, 0],
        dof_index[0, 0],
        corner_map.reshape(slots, 1, corners),
        partner[0, 0],
        counts,
    )

    def outer(value):
        value = value.reshape(slots, links, loads, width).transpose(0, 2, 1, 3)
        return value[None, None]

    return outer(solved), outer(resid)


def solution(mesh):
    in_specs = (
        P("row", "col", None, None, None),
        P("row", "col", None, None, None),
        P(("row", "col"), None),
        P("row", "col", None, None, None),
        P("row", "col", None, None, None, None),
        P("row", "col"),
        P("row", "col", None, None),
        P("row", "col", None, None, None),
        P("row", "col", None, None),
    )
    out_specs = (P("row", "col", None, None, None, None), P("row", "col", None, None, None, None))
    return jax.shard_map(local, mesh=mesh, in_specs=in_specs, out_specs=out_specs, check_vma=False)
```

```python
import functools

import jax
import jax.numpy as jnp
from jax import lax
from jax.experimental import pallas as pl
from jax.experimental.pallas import tpu as pltpu
from jax.sharding import PartitionSpec as P

ITERS = 3
NX, NZ, NY, NK = 4, 4, 4, 2
NYZ = NZ * NY
STAGES = 3

MESH = pl.DeviceIdType.MESH
F32 = jnp.float32
BF16 = jnp.bfloat16
NT = (((1,), (1,)), ((), ()))
NN = (((1,), (0,)), ((), ()))


def split2(value):
    high = value.astype(BF16)
    low = (value - high.astype(F32)).astype(BF16)
    return high, low


def split3(value):
    high = value.astype(BF16)
    return high, (value - high.astype(F32)).astype(BF16)


def stack3(value):
    return jnp.concatenate(split3(value), axis=0)


def dot(left, right, dims):
    return lax.dot_general(left, right, dims, preferred_element_type=F32)


def sum3(value):
    rows = value.shape[0] // 2
    return value[rows:] + value[:rows]


def rcopy(src, dst, send, recv, device):
    return pltpu.make_async_remote_copy(
        src_ref=src,
        dst_ref=dst,
        send_sem=send,
        recv_sem=recv,
        device_id=device,
        device_id_type=MESH,
    )


def group_start(src, buf, mine, send, recv, peers):
    for device, _ in peers:
        rcopy(src, buf.at[mine], send, recv, device).start()


def group_copy(buf, send, recv, peers):
    part = buf.at[pl.ds(0, len(peers))]
    return rcopy(part, part, send, recv, peers[0][0])


def group_wait(buf, send, recv, peers):
    group_copy(buf, send, recv, peers).wait_recv()


def group_sent(buf, send, recv, peers):
    group_copy(buf, send, recv, peers).wait_send()


def kernel(
    flex, cinv, cpl_in, weight_in, rhs_in, dof_in, map_in, partner, counts,
    x_out, r_out,
    stage, flex_hi, flex_lo, m32, m2, cpl, weight, rhs, dof, rowmap, dof_inv, cplp, info, infop,
    maps_yz, maps_xc, wo, wp, scatter, pick, tbuf, cbuf, xbuf, y1buf, z1buf, y2buf, z2buf,
    psend, precv, qsend, qrecv, gsend, frecv, usend, urecv,
    vblk, vsp, gsp, fsp, yv, tv, dv, sv, zv, rv, mask, ulink, clink, cface, sc,
    pybuf,
    flex_sem, load_sem, mloc_sem, info_s, info_r, cpl_s, cpl_r, mapa_s, mapa_r, mapb_s, mapb_r,
    m_s, m_r, t_s, t_r, c_s, c_r, x_s, x_r, y1_s, y1_r, z1_s, z1_r, y2_s, y2_r, z2_s, z2_r,
    p_s, p_r, q_s, q_r, f_s, f_r, u_s, u_r, py_s, py_r,
):
    slots, iface = flex.shape[:2]
    half = iface // 2
    links, width = dof.shape[1:]
    loads = rhs.shape[1]
    corners = cpl.shape[1]
    own_rows, coarse = cinv.shape
    nxc = NX * NK
    kset = coarse // nxc
    rset = own_rows * nxc
    khalf = kset // 2
    blocks = slots * links
    tiles = 2 * width
    spare = slots * corners

    row, col = lax.axis_index("row"), lax.axis_index("col")
    cz = lax.div(col, NY * NK)
    cy = lax.rem(lax.div(col, NK), NY)
    ck = lax.rem(col, NK)
    cols = NZ * NY * NK
    me_yz = cz * NY + cy
    me_xc = ck * NX + row
    prev = (row, lax.rem(col + cols - 1, cols))
    nxt = (row, lax.rem(col + 1, cols))

    def device(x, z, y, k):
        return (x, (z * NY + y) * NK + k)

    def turn(value, by, size):
        return lax.rem(value + by, size)

    xs = [(device(turn(row, i, NX), cz, cy, ck), turn(row, i, NX)) for i in (2, 1, 3)]
    ys = [(device(row, cz, turn(cy, i, NY), ck), turn(cy, i, NY)) for i in (2, 1, 3)]
    zs = [(device(row, turn(cz, i, NZ), cy, ck), turn(cz, i, NZ)) for i in (2, 1, 3)]
    cs = [(device(row, cz, cy, 1 - ck), 1 - ck)]
    order = sorted(
        [(i, j) for i in range(NZ) for j in range(NY) if (i, j) != (0, 0)],
        key=lambda ij: -(min(ij[0], NZ - ij[0]) + min(ij[1], NY - ij[1])),
    )
    yzs = [
        (device(row, turn(cz, i, NZ), turn(cy, j, NY), ck), turn(cz, i, NZ) * NY + turn(cy, j, NY))
        for i, j in order
    ]
    xcs = [
        (device(turn(row, i, NX), cz, cy, turn(ck, j, NK)), turn(ck, j, NK) * NX + turn(row, i, NX))
        for i in (2, 1, 3, 0)
        for j in range(NK)
        if (i, j) != (0, 0)
    ]

    barrier = pltpu.get_barrier_semaphore()
    everyone = [d for d, _ in yzs] + [d for d, _ in xcs] + [prev, nxt]
    for d in everyone:
        pl.semaphore_signal(barrier, inc=1, device_id=d, device_id_type=MESH)

    def flex_copy(s):
        return pltpu.make_async_copy(flex.at[s], stage.at[s % STAGES], flex_sem.at[s])

    def m_part(other):
        return cinv.at[:, pl.ds(pl.multiple_of(other * kset, 128), kset)]

    loaded = [
        pltpu.make_async_copy(src, dst, load_sem.at[i])
        for i, (src, dst) in enumerate(
            [(map_in, rowmap), (dof_in, dof), (rhs_in, rhs), (weight_in, weight), (cpl_in, cpl)]
        )
    ]
    for copy in loaded:
        copy.start()
    m_local = pltpu.make_async_copy(m_part(me_xc), m32.at[me_xc], mloc_sem)
    m_local.start()
    for s in range(STAGES):
        flex_copy(s).start()

    for s in range(slots):
        live = jnp.where(s < counts[0, 0], 1.0, 0.0).astype(F32)
        info[s] = jnp.broadcast_to(live, (1, width))
    loaded[0].wait()
    lane8 = lax.broadcasted_iota(jnp.int32, (8, width), 1)
    found = jnp.full((8, width), -1, jnp.int32)
    for s in range(slots):
        ids = jnp.broadcast_to(rowmap[s], (8, corners))
        ids = jnp.concatenate([ids, jnp.zeros((8, width - corners), jnp.int32)], axis=1)
        if s:
            ids = pltpu.roll(ids, s * corners, 1)
        inside = jnp.logical_and(lane8 >= s * corners, lane8 < (s + 1) * corners)
        found = jnp.where(inside, ids, found)
    info[slots] = found[0:1].astype(F32)

    pl.semaphore_wait(barrier, len(everyone))

    info_copy = rcopy(info, infop, info_s, info_r, nxt)
    info_copy.start()
    loaded[4].wait()
    cpl_copy = rcopy(cpl.at[:, :, half:], cplp, cpl_s, cpl_r, nxt)
    cpl_copy.start()
    for d, other in xcs:
        rcopy(m_part(other), m32.at[me_xc], m_s, m_r, d).start()
    map_groups = [(maps_yz, me_yz, mapa_s, mapa_r, yzs), (maps_xc, me_xc, mapb_s, mapb_r, xcs)]

    def send_maps(src, h):
        for buf, mine, send, recv, peers in map_groups:
            for d, _ in peers:
                rcopy(src, buf.at[mine, h], send, recv, d).start()
            buf[mine, h] = src[...]

    def wait_maps(group):
        buf, _, send, recv, peers = map_groups[group]
        group_wait(buf, send, recv, peers)
        group_sent(buf, send, recv, peers)

    send_maps(info.at[slots], 0)

    def build_coupling(source, out):
        for s in range(slots):
            value = source[s, :, 0:half]
            high = value.astype(BF16).astype(F32)
            out[s] = jnp.concatenate([high, value - high], axis=0).astype(BF16)

    build_coupling(cpl, wo)
    tv[...] = jnp.zeros_like(tv)
    dv[...] = jnp.zeros_like(dv)
    sv[...] = jnp.zeros_like(sv)
    x_out[...] = jnp.zeros_like(x_out)
    sc[0] = jnp.ones_like(sc[0])
    sc[1] = jnp.zeros_like(sc[1])
    sc[2] = jnp.zeros_like(sc[2])
    sc[3] = jnp.zeros_like(sc[3])

    loaded[1].wait()
    sub = lax.broadcasted_iota(jnp.int32, (width, width), 0)
    numbers = lane8.astype(F32).astype(BF16)
    for b in range(blocks):
        ids = dof[b // links, b % links : b % links + 1, :]
        hit = jnp.where(sub == ids, 1.0, 0.0).astype(BF16)
        dof_inv[b] = dot(numbers, hit, NT).astype(jnp.int32)

    inverse = {}
    for k in range(links):
        for p in range(slots):
            at = jnp.int32(0)
            for j in range(1, slots):
                at = jnp.where(partner[k, j] == p, j, at)
            inverse[k, p] = at

    loaded[2].wait()
    loaded[3].wait()
    info_copy.wait_recv()
    send_maps(infop.at[slots], 1)

    def put3(ref, s, k, value):
        for i, part in enumerate(split3(value)):
            ref[s, i * loads : (i + 1) * loads, k * width : (k + 1) * width] = part

    def multipliers(b, value):
        vblk[b] = value
        put3(vsp, b // links, b % links, value)

    def weight_of(b):
        return weight[b // links, b % links : b % links + 1, :]

    for b in range(blocks):
        s, k = b // links, b % links
        live = info[s] * infop[partner[k, s]]
        live = jnp.broadcast_to(live, (loads, width))
        mask[b] = live
        resid = live * rhs[s, :, k, :]
        rv[b] = resid
        yv[b] = resid
        value = weight_of(b) * resid
        zv[b] = value
        multipliers(b, value)

    lane = lax.broadcasted_iota(jnp.int32, (loads, width), 1)
    load_id = lax.broadcasted_iota(jnp.int32, (loads, width), 0)

    def total(first, second):
        return jnp.sum(jnp.sum(first * second, axis=0), axis=1, keepdims=True)

    def scalar_terms(packed):
        z, y = zv[...], yv[...]
        found = [total(rv[...], z), total(z, y), total(z, sv[...]), total(dv[...], y)]
        tile = jnp.zeros((loads, width), F32)
        for i, value in enumerate(found):
            at = lane == (4 * load_id + i if packed else spare + i)
            tile = jnp.where(at, value, tile)
        return tile

    def update(tile, packed, first):
        rz, zy, zs_, dy = [
            jnp.broadcast_to(
                jnp.sum(
                    jnp.where(lane == (4 * load_id + i if packed else spare + i), tile, 0.0),
                    axis=1,
                    keepdims=True,
                ),
                tile.shape,
            )
            for i in range(4)
        ]
        beta = rz / sc[0]
        if first is not None:
            beta = jnp.where(first, 0.0, beta)
        curv = zy + beta * (zs_ + dy) + beta * beta * sc[1]
        alpha = rz / curv
        sc[0], sc[1], sc[2], sc[3] = rz, curv, alpha, beta
        direction = zv[...] + beta[None] * dv[...]
        image = yv[...] + beta[None] * sv[...]
        dv[...] = direction
        sv[...] = image
        x_out[...] = x_out[...] + alpha[None] * direction
        resid = rv[...] - alpha[None] * image
        rv[...] = resid
        return resid

    def take(value, index):
        return jnp.take_along_axis(value, index, axis=1, mode="promise_in_bounds")

    def convert(s):
        flex_copy(s).wait()
        here = s % STAGES

        def chunk(i, _):
            at = pl.ds(pl.multiple_of(i * 64, 64), 64)
            high, low = split2(stage[here, at, :])
            flex_hi[s, at, :] = high
            flex_lo[s, at, :] = low
            return 0

        lax.fori_loop(0, iface // 64, chunk, 0)
        if s + STAGES < slots:
            flex_copy(s + STAGES).start()

    def local_answers(it, first, last):
        def one(s, _):
            left = jnp.concatenate([vsp[s], fsp[s]], axis=1)
            for n in range(iface // 256):
                at = slice(n * 256, (n + 1) * 256)
                out = dot(left, flex_hi[s, :, at], NN) + dot(left, flex_lo[s, :, at], NN)
                out = sum3(out)
                for h in range(2):
                    piece = out[:, h * width : (h + 1) * width]
                    k = 2 * n + h
                    if k < links:
                        ulink[s * links + k] = piece
                    else:
                        usend[it, s * links + k - links] = piece
            return 0

        lax.fori_loop(first, last, one, 0)

    def within(s):
        return jnp.logical_and(lane >= s * corners, lane < (s + 1) * corners)

    def shift(value, by):
        by = by % width
        return pltpu.roll(value, by, 1) if by else value

    def sent(it):
        group_sent(tbuf.at[it], t_s.at[it], t_r.at[it, 0], yzs)
        group_sent(cbuf.at[it], c_s.at[it], c_r.at[it], cs)
        group_sent(xbuf.at[it], x_s.at[it], x_r.at[it], xs)
        group_sent(y1buf.at[it], y1_s.at[it], y1_r.at[it], ys)
        group_sent(z1buf.at[it], z1_s.at[it], z1_r.at[it], zs)
        group_sent(z2buf.at[it], z2_s.at[it], z2_r.at[it], zs)
        group_sent(y2buf.at[it], y2_s.at[it], y2_r.at[it], ys)
        rcopy(psend.at[it], precv.at[it], p_s.at[it], p_r.at[it], cs[0][0]).wait_send()
        group_sent(qrecv.at[it], q_s.at[it], q_r.at[it], xs)
        rcopy(gsend.at[it], frecv.at[it], f_s.at[it], f_r.at[it], prev).wait_send()
        rcopy(usend.at[it], urecv.at[it], u_s.at[it], u_r.at[it], nxt).wait_send()

    def body(it, _):
        for b in range(blocks):
            p, k = b // links, b % links
            from_block = inverse[k, p] * links + k
            index = jnp.concatenate([dof_inv[from_block]] * (loads // 8), axis=0)
            value = -take(vblk[from_block], index)
            gsend[it, b] = value
            put3(gsp, p, k, value)

        def terms(blocks3, factors):
            found = jnp.zeros((loads, width), F32)
            for s in range(slots):
                part = sum3(dot(blocks3[s], factors[s], NT))
                rest = jnp.zeros((loads, width - 2 * corners), F32)
                part = jnp.concatenate([part, rest], axis=1)
                part = shift(part, s * corners) + shift(part, (s - 1) * corners)
                found = jnp.where(within(s), part, found)
            return found

        tbuf[it, me_yz, :, 0:width] = jnp.where(
            lane < spare, terms(vsp, wo), scalar_terms(False)
        )

        @pl.when(it == 0)
        def _():
            cpl_copy.wait_recv()
            build_coupling(cplp, wp)

        tbuf[it, me_yz, :, width:tiles] = terms(gsp, wp)
        for d, _ in yzs:
            rcopy(
                tbuf.at[it, me_yz], tbuf.at[it, me_yz], t_s.at[it], t_r.at[it, me_yz], d
            ).start()
        @pl.when(it > 0)
        def _():
            sent(it - 1)

        @pl.when(it == 0)
        def _():
            wait_maps(0)

            def rows(p, _):
                base = (lax.rem(p, NX) * cols + me_yz * NK + lax.div(p, NX)) * own_rows
                index = lax.broadcasted_iota(jnp.int32, (own_rows, width), 0) + base
                index = index.astype(F32)
                at = pl.ds(pl.multiple_of(p * own_rows, own_rows), own_rows)
                for q in range(NYZ):
                    for h in range(2):
                        hit = jnp.where(index == maps_yz[q, h], 1.0, 0.0)
                        scatter[q, at, h * width : (h + 1) * width] = hit.astype(BF16)
                return 0

            lax.fori_loop(0, nxc, rows, 0)
            for s in range(STAGES):
                convert(s)

        def spread(q):
            return dot(stack3(tbuf[it, q]), scatter[q], NT)

        found, carried = spread(me_yz), tbuf[it, me_yz, :, 0:width]
        for d, q in reversed(yzs):
            rcopy(tbuf.at[it, me_yz], tbuf.at[it, q], t_s.at[it], t_r.at[it, q], d).wait_recv()
            found, carried = found + spread(q), carried + tbuf[it, q, :, 0:width]
        cbuf[it, ck, :, 0:rset] = sum3(found)
        cbuf[it, ck, :, rset : rset + width] = carried
        group_start(cbuf.at[it, ck], cbuf.at[it], ck, c_s.at[it], c_r.at[it], cs)
        force_copy = rcopy(gsend.at[it], frecv.at[it], f_s.at[it], f_r.at[it], prev)
        force_copy.start()
        group_wait(cbuf.at[it], c_s.at[it], c_r.at[it], cs)
        xbuf[it, row] = cbuf[it, 0] + cbuf[it, 1]
        group_start(xbuf.at[it, row], xbuf.at[it], row, x_s.at[it], x_r.at[it], xs)

        @pl.when(it == 0)
        def _():
            for s in range(STAGES, slots):
                convert(s)
            m_local.wait()
            group_wait(m32, m_s, m_r, xcs)
            group_sent(m32, m_s, m_r, xcs)
            for b in range(nxc):
                high, low = split2(m32[b])
                m2[b * own_rows : (b + 1) * own_rows, :] = high
                m2[rset + b * own_rows : rset + (b + 1) * own_rows, :] = low

        group_wait(xbuf.at[it], x_s.at[it], x_r.at[it], xs)
        load = xbuf[it, 0] + xbuf[it, 1] + xbuf[it, 2] + xbuf[it, 3]
        left = stack3(load[:, :rset])
        answer = sum3(dot(jnp.concatenate([left, left], axis=1), m2[...], NN))
        y1buf[it, cy] = answer[:, :khalf]
        z1buf[it, cz] = answer[:, khalf:]
        group_start(y1buf.at[it, cy], y1buf.at[it], cy, y1_s.at[it], y1_r.at[it], ys)
        group_start(z1buf.at[it, cz], z1buf.at[it], cz, z1_s.at[it], z1_r.at[it], zs)

        force_copy.wait_recv()
        for b in range(blocks):
            put3(fsp, b // links, b % links, frecv[it, b])
        local_answers(it, 0, 3)

        group_wait(y1buf.at[it], y1_s.at[it], y1_r.at[it], ys)
        group_wait(z1buf.at[it], z1_s.at[it], z1_r.at[it], zs)
        z2buf[it, cz] = y1buf[it, 0] + y1buf[it, 1] + y1buf[it, 2] + y1buf[it, 3]
        y2buf[it, cy] = z1buf[it, 0] + z1buf[it, 1] + z1buf[it, 2] + z1buf[it, 3]
        group_start(z2buf.at[it, cz], z2buf.at[it], cz, z2_s.at[it], z2_r.at[it], zs)
        group_start(y2buf.at[it, cy], y2buf.at[it], cy, y2_s.at[it], y2_r.at[it], ys)
        local_answers(it, 3, slots)

        @pl.when(it == 0)
        def _():
            wait_maps(1)
            step = own_rows

            def rows(b, _):
                index = lax.broadcasted_iota(jnp.int32, (step, width), 0) + (me_xc * kset + b * step)
                index = index.astype(F32)
                at = pl.ds(pl.multiple_of(b * step, step), step)
                for q in range(nxc):
                    for h in range(2):
                        hit = jnp.where(index == maps_xc[q, h], 1.0, 0.0)
                        lo = (2 * (q % NX) + h) * width
                        pick[q // NX, at, lo : lo + width] = hit.astype(BF16)
                return 0

            lax.fori_loop(0, kset // step, rows, 0)

        group_wait(z2buf.at[it], z2_s.at[it], z2_r.at[it], zs)
        group_wait(y2buf.at[it], y2_s.at[it], y2_r.at[it], ys)
        answer_copy = rcopy(usend.at[it], urecv.at[it], u_s.at[it], u_r.at[it], nxt)
        answer_copy.start()
        first = z2buf[it, 0] + z2buf[it, 1] + z2buf[it, 2] + z2buf[it, 3]
        second = y2buf[it, 0] + y2buf[it, 1] + y2buf[it, 2] + y2buf[it, 3]
        left = stack3(jnp.concatenate([first, second], axis=1))
        found = sum3(dot(left, pick[1 - ck], NN))
        for q in range(NX):
            psend[it, q] = found[:, q * tiles : (q + 1) * tiles]
        core_copy = rcopy(psend.at[it], precv.at[it], p_s.at[it], p_r.at[it], cs[0][0])
        core_copy.start()
        found = sum3(dot(left, pick[ck], NN))
        core_copy.wait_recv()
        for q in range(NX):
            qsend[it, q] = found[:, q * tiles : (q + 1) * tiles] + precv[it, q]
        for d, other in xs:
            rcopy(qsend.at[it, other], qrecv.at[it, row], q_s.at[it], q_r.at[it], d).start()
        qrecv[it, row] = qsend[it, row]

        @pl.when(it > 0)
        def _():
            resid = update(load[:, rset:], False, it == 1)
            for b in range(blocks):
                zv[b] = weight_of(b) * resid[b]

        group_wait(qrecv.at[it], q_s.at[it], q_r.at[it], xs)
        picked = qrecv[it, 0] + qrecv[it, 1] + qrecv[it, 2] + qrecv[it, 3]

        def spread_back(part, s, factors):
            left = shift(part, -s * corners)
            left = jnp.where(lane < corners, left, shift(part, (1 - s) * corners))
            return sum3(dot(stack3(left[:, : 2 * corners]), factors[s], NN))

        for s in range(slots):
            found = spread_back(picked[:, :width], s, wo)
            other = spread_back(picked[:, width:], s, wp)
            for k in range(links):
                clink[s * links + k] = found[:, k * width : (k + 1) * width]
                cface[s * links + k] = other[:, k * width : (k + 1) * width]

        answer_copy.wait_recv()
        alpha, beta = sc[2], sc[3]
        for b in range(blocks):
            s, k = b // links, b % links
            facing = partner[k, s] * links + k
            index = jnp.broadcast_to(dof[s, k : k + 1, :], (loads, width))
            far = take(urecv[it, facing] + cface[facing], index)
            image = (ulink[b] + clink[b] - far) * mask[b]
            image = image + beta * tv[b]
            tv[b] = jnp.where(it == 0, 0.0, image)
            image = jnp.where(it == 0, image, yv[b] - alpha * image)
            yv[b] = image
            multipliers(b, weight_of(b) * image)
        return 0

    lax.fori_loop(0, ITERS, body, 0)

    me_all = row * cols + col
    pybuf[me_all] = jnp.sum(scalar_terms(True), axis=0, keepdims=True)

    group = 8

    def tell(x, first):
        def some(n, _):
            for j in range(group):
                d = (x, lax.rem(col + n * group + j, cols))
                rcopy(pybuf.at[me_all], pybuf.at[me_all], py_s, py_r, d).start()
            return 0

        for j in range(first, group if first else 0):
            d = (x, lax.rem(col + j, cols))
            rcopy(pybuf.at[me_all], pybuf.at[me_all], py_s, py_r, d).start()
        lax.fori_loop(1 if first else 0, cols // group, some, 0)

    for i in (2, 1, 3):
        tell(turn(row, i, NX), 0)
    tell(row, 1)
    sent(ITERS - 1)
    info_copy.wait_send()
    cpl_copy.wait_send()
    everything = pybuf.at[pl.ds(0, NX * cols - 1)]
    final = rcopy(everything, everything, py_s, py_r, nxt)
    final.wait_recv()
    line = jnp.sum(pybuf[...], axis=0)
    final.wait_send()
    r_out[...] = update(jnp.broadcast_to(line, (loads, width)), True, None)


def local(
    flexibility,
    coupling,
    coarse_inverse,
    precon_weight,
    right_side,
    counts,
    partner,
    dof_index,
    corner_map,
):
    flex = flexibility[0, 0]
    cpl = coupling[0, 0]
    slots, iface = flex.shape[:2]
    half = iface // 2
    links, width = dof_index.shape[3:]
    loads = right_side.shape[3]
    own_rows, coarse = coarse_inverse.shape
    corners = corner_map.shape[-1]
    blocks = slots * links
    nxc = NX * NK
    kset, rset = coarse // nxc, own_rows * nxc
    rows3 = 2 * loads
    pair = 2 * width

    vec = (blocks, loads, width)
    per = (ITERS,)
    vm = pltpu.VMEM
    dma = pltpu.SemaphoreType.DMA
    scratch = [
        vm((STAGES, iface, iface), F32),
        vm((slots, iface, iface), BF16),
        vm((slots, iface, iface), BF16),
        vm((nxc, own_rows, kset), F32),
        vm((2 * rset, kset), BF16),
        vm(cpl.shape, F32),
        vm((slots, links, width), F32),
        vm((slots, loads, links, width), F32),
        vm((slots, links, width), jnp.int32),
        vm((slots, 1, corners), jnp.int32),
        vm((blocks, 8, width), jnp.int32),
        vm((slots, corners, half), F32),
        vm((slots + 1, 1, width), F32),
        vm((slots + 1, 1, width), F32),
        vm((NYZ, 2, 1, width), F32),
        vm((nxc, 2, 1, width), F32),
        vm((slots, 2 * corners, half), BF16),
        vm((slots, 2 * corners, half), BF16),
        vm((NYZ, rset, pair), BF16),
        vm((NK, kset, NX * pair), BF16),
        vm(per + (NYZ, loads, pair), F32),
        vm(per + (NK, loads, rset + width), F32),
        vm(per + (NX, loads, rset + width), F32),
        vm(per + (NY, loads, kset // 2), F32),
        vm(per + (NZ, loads, kset // 2), F32),
        vm(per + (NY, loads, kset // 2), F32),
        vm(per + (NZ, loads, kset // 2), F32),
        vm(per + (NX, loads, pair), F32),
        vm(per + (NX, loads, pair), F32),
        vm(per + (NX, loads, pair), F32),
        vm(per + (NX, loads, pair), F32),
        vm(per + vec, F32),
        vm(per + vec, F32),
        vm(per + vec, F32),
        vm(per + vec, F32),
        vm(vec, F32),
        vm((slots, rows3, half), BF16),
        vm((slots, rows3, half), BF16),
        vm((slots, rows3, half), BF16),
    ]
    scratch += [vm(vec, F32)] * 10
    scratch += [
        vm((4, loads, width), F32),
        vm((NYZ * nxc, 1, width), F32),
        dma((slots,)),
        dma((5,)),
        dma,
        dma,
        dma,
        dma,
        dma,
        dma,
        dma,
        dma,
        dma,
        dma,
        dma,
        dma(per),
        dma(per + (NYZ,)),
    ]
    scratch += [dma(per)] * 20 + [dma] * 2
    in_vmem = pl.BlockSpec(memory_space=pltpu.VMEM)
    in_smem = pl.BlockSpec(memory_space=pltpu.SMEM)
    in_place = pl.BlockSpec(memory_space=pl.ANY)
    solved, resid = pl.pallas_call(
        kernel,
        name="feti",
        out_shape=[jax.ShapeDtypeStruct(vec, F32)] * 2,
        in_specs=[in_place] * 7 + [in_smem] * 2,
        out_specs=[in_vmem] * 2,
        scratch_shapes=scratch,
        compiler_params=pltpu.CompilerParams(
            collective_id=0, has_side_effects=True, vmem_limit_bytes=67043328
        ),
    )(
        flex,
        coarse_inverse,
        cpl,
        precon_weight[0, 0],
        right_side[0, 0],
        dof_index[0, 0],
        corner_map.reshape(slots, 1, corners),
        partner[0, 0],
        counts,
    )

    def outer(value):
        value = value.reshape(slots, links, loads, width).transpose(0, 2, 1, 3)
        return value[None, None]

    return outer(solved), outer(resid)


def solution(mesh):
    in_specs = (
        P("row", "col", None, None, None),
        P("row", "col", None, None, None),
        P(("row", "col"), None),
        P("row", "col", None, None, None),
        P("row", "col", None, None, None, None),
        P("row", "col"),
        P("row", "col", None, None),
        P("row", "col", None, None, None),
        P("row", "col", None, None),
    )
    out_specs = (P("row", "col", None, None, None, None), P("row", "col", None, None, None, None))
    return jax.shard_map(local, mesh=mesh, in_specs=in_specs, out_specs=out_specs, check_vma=False)
```
